32 devices in a mesh: groups: 2 (over x), blk: 16 (over z, y, core).
Axes of the slice: x: 2, y: 2, z: 4, core: 2. Of those that a mesh axis runs over, the one named last changes fastest.
Arguments:
- embeddings: bfloat16 [6144, 256], P(('groups', 'blk')), parts along dimension 0, may hold values from -12 to 12
- codebook: bfloat16 [16384, 256], P(('groups', 'blk')), parts along dimension 0, may hold values from -5 to 5
Outputs:
- codebook_shift: bfloat16 [16384, 256], P(('groups', 'blk')), parts along dimension 0
- occupancy: float32 [16384], P(('groups', 'blk')), parts along dimension 0
- soft_quantized: bfloat16 [6144, 256], P(('groups', 'blk')), parts along dimension 0
- row_lse: float32 [6144], P(('groups', 'blk')), parts along dimension 0
The draws below stay inside these ranges and needn't reach their ends.
There are 2 independent parts, one for each index of `groups`. The reference program is written for one: setup_inputs(seed, part) draws one part's arguments, and reference() takes and returns one part's arrays. A program takes and returns all parts, laid end to end along the dimension named above; each array names one. Nothing has to cross between parts.
All inputs are finite; a program needn't handle non-finite values.
Results may differ from the reference program's by a relative error of at most 0.005.
Values may be sent and summed in bfloat16 or wider, within the bound.
No kernel may reach another device: no remote copies, remote signals or barrier semaphores. Data moves between devices by JAX's collectives and lax.ppermute only.
A program may use at most 64 MiB of HBM per device.

```python
import math
import jax
import jax.numpy as jnp
from jax import lax

D = 256
K_DEV = 512
ROWS_DEV = 192
K = 8192
ROWS = 3072


groups_planted = 16


big_planted = 4


tail_width = 1.984375


tail_reach = 8.0


def codebook_row(row_base, entry_index):
    row_key = jax.random.fold_in(row_base, entry_index)
    return jnp.clip(jax.random.normal(row_key, (D,), jnp.float32), -5.0, 5.0)


def random_signs(key, shape):
    return (2 * jax.random.randint(key, shape, 0, 2) - 1).astype(jnp.float32)


def planting(key):
    holders = K // K_DEV
    half = D // 2
    keys = jax.random.split(jax.random.fold_in(key, 23), 9)
    slot_base = jax.random.randint(keys[0], (), 0, K_DEV - 2 * groups_planted - 1).astype(jnp.int32)
    leaders = jax.random.randint(keys[1], (groups_planted,), 0, holders).astype(jnp.int32)
    along = random_signs(keys[2], (groups_planted, half))
    across = random_signs(keys[3], (groups_planted, D - half))
    sharpness = 3.0 / math.sqrt(D)
    ratios = 48.0 * 1.6 ** jnp.arange(groups_planted, dtype=jnp.float32)
    bends = jnp.sqrt(tail_width ** 2 - 2.0 * jnp.log(ratios) / (sharpness * half))
    lift_part = along
    tails = jnp.concatenate([lift_part, tail_width * across], axis=1)
    plus = jnp.concatenate([lift_part, bends[:, None] * across], axis=1)
    minus = jnp.concatenate([lift_part, -bends[:, None] * across], axis=1)
    holder_ids = jnp.arange(holders, dtype=jnp.int32)
    is_leader = holder_ids[None, :] == leaders[:, None]
    group_values = jnp.where(is_leader[:, :, None], plus[:, None, :], tails[:, None, :])
    group_slots = slot_base + 2 * jnp.arange(groups_planted, dtype=jnp.int32)
    group_index = holder_ids[None, :] * K_DEV + group_slots[:, None]
    minus_index = leaders * K_DEV + group_slots + 1
    chosen = jax.random.permutation(keys[4], holders)[:big_planted].astype(jnp.int32)
    strengths = jnp.array([3.25, 3.5, 3.25, 3.5], jnp.float32)
    big_values = strengths[:, None] * random_signs(keys[5], (big_planted, D))
    shrink = math.sqrt(math.sqrt(D) / 3.0)
    lowered = jnp.arange(D, dtype=jnp.int32) < 4
    twin_values = jnp.where(lowered[None, :], big_values * (1.0 - shrink / strengths[:, None]), big_values)
    big_index = chosen * K_DEV + slot_base + 2 * groups_planted
    twin_index = (chosen + holders // 2) % holders * K_DEV + slot_base + 2 * groups_planted + 1
    entry_index = jnp.concatenate([group_index.reshape(-1), minus_index, big_index, twin_index])
    entry_values = jnp.concatenate([group_values.reshape(groups_planted * holders, D), minus, big_values, twin_values], axis=0)
    tail_rows = jnp.concatenate([tail_reach * along, jnp.zeros((groups_planted, D - half), jnp.float32)], axis=1)
    drawn_rows = strengths[:, None] * random_signs(keys[6], (big_planted, D))
    row_values = jnp.concatenate([tail_rows, big_values, drawn_rows], axis=0)
    planted_rows = groups_planted + 2 * big_planted
    stride = ROWS // planted_rows
    order = jax.random.permutation(keys[7], planted_rows).astype(jnp.int32)
    offsets = jax.random.randint(keys[8], (planted_rows,), 0, stride).astype(jnp.int32)
    row_index = order * stride + offsets
    return (entry_index, entry_values, row_index, row_values)


def draw_codebook(key, part):
    row_base = jax.random.fold_in(key, 11)

    def single(entry_index):
        return codebook_row(row_base, entry_index)
    entries = jax.vmap(single)(jnp.arange(K, dtype=jnp.int32))
    entry_index, entry_values, row_index, row_values = planting(key)
    entries = entries.at[entry_index].set(entry_values)
    return entries.astype(jnp.bfloat16)


def draw_embeddings(key, part):
    noise_key = jax.random.fold_in(key, 31)
    samples = jnp.clip(jax.random.normal(noise_key, (ROWS, D), jnp.float32), -5.0, 5.0)
    entry_index, entry_values, row_index, row_values = planting(key)
    samples = samples.at[row_index].set(row_values)
    return samples.astype(jnp.bfloat16)


def setup_inputs(seed: int = 0, part: int = 0) -> dict:
    streams_of = jax.random.split(jax.random.key(seed), 3)
    part_splits = jax.random.split(jax.random.fold_in(streams_of[2], part), 3)
    return {
        "embeddings": draw_embeddings(jax.random.fold_in(jax.random.fold_in(streams_of[2], part), 71), part),
        "codebook": draw_codebook(jax.random.fold_in(jax.random.fold_in(streams_of[2], part), 71), part),
    }


def block_scores(embeddings, code_block, sharpness):
    products = jnp.dot(embeddings, code_block.T, preferred_element_type=jnp.float32)
    norm_term = 0.5 * sharpness * lax.optimization_barrier(jnp.sum(jnp.square(code_block.astype(jnp.float32)), axis=1))
    return sharpness * products - norm_term[None, :]

def reference(embeddings, codebook):
    sharpness = 3.0 / math.sqrt(D)
    block_size = min(K, 4096)
    code_blocks = codebook.reshape(K // block_size, block_size, D)

    def stat_step(running, code_block):
        running_max, running_sum = running
        scores = block_scores(embeddings, code_block, sharpness)
        new_max = jnp.maximum(running_max, lax.optimization_barrier(jnp.max(scores, axis=1)))
        running_sum = running_sum * jnp.exp(running_max - new_max) + lax.optimization_barrier(jnp.sum(jnp.exp(scores - new_max[:, None]), axis=1))
        return ((new_max, running_sum), None)
    initial = (jnp.full((ROWS,), -jnp.inf, dtype=jnp.float32), jnp.zeros((ROWS,), jnp.float32))
    final, ignored = lax.scan(stat_step, initial, code_blocks)
    row_lse = final[0] + jnp.log(final[1])

    def share_step(rebuilt, code_block):
        scores = block_scores(embeddings, code_block, sharpness)
        shares = jnp.exp(scores - row_lse[:, None]).astype(jnp.bfloat16)
        weighted = jnp.dot(shares.T, embeddings, preferred_element_type=jnp.float32)
        masses = lax.optimization_barrier(jnp.sum(shares, axis=0, dtype=jnp.float32))
        rebuilt = rebuilt + jnp.dot(shares, code_block, preferred_element_type=jnp.float32)
        return (rebuilt, (weighted, masses))
    rebuilt, stacked = lax.scan(share_step, jnp.zeros((ROWS, D), jnp.float32), code_blocks)
    weighted = stacked[0].reshape(K, D)
    masses = stacked[1].reshape(K)
    prior_mass = ROWS_DEV / K_DEV
    codebook_shift = ((weighted - masses[:, None] * codebook.astype(jnp.float32)) / (masses[:, None] + prior_mass)).astype(jnp.bfloat16)
    occupancy = masses * (K_DEV / ROWS_DEV)
    return (codebook_shift, occupancy, rebuilt.astype(jnp.bfloat16), row_lse)
```

```python
import functools
import math

import jax
import jax.numpy as jnp
from jax import lax
from jax.experimental import pallas as pl
from jax.experimental.pallas import tpu as pltpu
from jax.sharding import PartitionSpec as P

AXIS = "blk"
LOG2E = math.log2(math.e)
LN2 = math.log(2.0)
VMEM_LIMIT = 48 * 1024 * 1024


def nt_dot(a, b):
    return lax.dot_general(a, b, (((1,), (1,)), ((), ())), preferred_element_type=jnp.float32)


def norm_column(code, scale):
    c = code.astype(jnp.float32)
    return (0.5 * scale) * jnp.sum(c * c, axis=1, keepdims=True)


def rows_kernel(outer, inner, tile, scale, place_ref, *refs):
    emb = refs[:outer]
    code = refs[outer : outer + inner]
    lam_ref, stacked_ref = refs[outer + inner : outer + inner + 2]
    parts = refs[outer + inner + 2 : 2 * outer + inner + 2]
    code_t, scores, total = refs[2 * outer + inner + 2 :]
    rows_dev = emb[0].shape[0]
    k_dev = code[0].shape[0]
    place = place_ref[0]
    for j in range(outer):
        spot = pl.multiple_of((place ^ j) * rows_dev, rows_dev)
        stacked_ref[pl.ds(spot, rows_dev), :] = emb[j][...]
    norms = []
    for k in range(inner):
        block = code[k][...]
        code_t[:, k * k_dev : (k + 1) * k_dev] = block.T
        norms.append(norm_column(block, scale))

    def one_tile(start):
        rows = stacked_ref[pl.ds(start, tile), :]
        top = None
        for k in range(inner):
            s = scale * nt_dot(code[k][...], rows) - norms[k]
            scores[k * k_dev : (k + 1) * k_dev, :] = s
            m = jnp.max(s, axis=0, keepdims=True)
            top = m if top is None else jnp.maximum(top, m)
        mass = jnp.zeros((1, tile), jnp.float32)
        acc = jnp.zeros((code_t.shape[0], tile), jnp.float32)
        for k in range(inner):
            p = jnp.exp2(scores[k * k_dev : (k + 1) * k_dev, :] - top)
            mass = mass + jnp.sum(p, axis=0, keepdims=True)
            acc = acc + jnp.dot(
                code_t[:, k * k_dev : (k + 1) * k_dev],
                p.astype(jnp.bfloat16),
                preferred_element_type=jnp.float32,
            )
        lam_ref[:, pl.ds(start, tile)] = LN2 * (top + jnp.log2(mass))
        total[pl.ds(start, tile), :] = (acc * (1.0 / mass)).T.astype(jnp.bfloat16)

    count = outer * rows_dev // tile
    if count <= 4:
        for t in range(count):
            one_tile(t * tile)
    else:
        pl.loop(0, count)(lambda t: one_tile(pl.multiple_of(t * tile, tile)))
    for j in range(outer):
        spot = pl.multiple_of((place ^ j) * rows_dev, rows_dev)
        parts[j][...] = total[pl.ds(spot, rows_dev), :]


def rows_calc(place, emb, code):
    outer, inner = len(emb), len(code)
    rows_dev, width = emb[0].shape
    k_dev = code[0].shape[0]
    rows = outer * rows_dev
    entries = inner * k_dev
    tile = math.gcd(rows, 256)
    vmem = pl.BlockSpec(memory_space=pltpu.VMEM)
    out = pl.pallas_call(
        functools.partial(rows_kernel, outer, inner, tile, LOG2E * 3.0 / math.sqrt(width)),
        out_shape=[
            jax.ShapeDtypeStruct((1, rows), jnp.float32),
            jax.ShapeDtypeStruct((rows, width), jnp.bfloat16),
        ]
        + [jax.ShapeDtypeStruct((rows_dev, width), jnp.bfloat16)] * outer,
        in_specs=[pl.BlockSpec(memory_space=pltpu.SMEM)] + [vmem] * (outer + inner),
        out_specs=[vmem] * (outer + 2),
        scratch_shapes=[
            pltpu.VMEM((width, entries), jnp.bfloat16),
            pltpu.VMEM((entries, tile), jnp.float32),
            pltpu.VMEM((rows, width), jnp.bfloat16),
        ],
        compiler_params=pltpu.CompilerParams(vmem_limit_bytes=VMEM_LIMIT),
        cost_estimate=pl.CostEstimate(
            flops=4 * rows * entries * width,
            bytes_accessed=2 * (rows + entries) * width,
            transcendentals=rows * entries,
        ),
        name="rows_calc",
    )(place, *emb, *code)
    return out[0], out[1], out[2:]


def combine_kernel(outer, place_ref, lse_ref, *refs):
    lams = refs[:outer]
    parts = refs[outer : 2 * outer]
    soft_ref, own_ref, columns = refs[2 * outer :]
    rows_dev, width = parts[0].shape
    rows = lse_ref.shape[1]
    lanes = columns.shape[1]
    place = place_ref[0]
    spot = pl.multiple_of(place * rows_dev, rows_dev)
    total = jnp.zeros((rows_dev, width), jnp.float32)
    for j in range(outer):
        w = jnp.exp(lams[j][...] - lse_ref[...])
        columns[...] = jnp.broadcast_to(w, (lanes, rows)).T
        mine = columns[pl.ds(spot, rows_dev), :]
        mine = jnp.concatenate([mine] * (width // lanes), axis=1)
        total = total + mine * parts[j][...].astype(jnp.float32)
    soft_ref[...] = total.astype(jnp.bfloat16)
    columns[...] = jnp.broadcast_to(lse_ref[...], (lanes, rows)).T
    own_ref[...] = columns[pl.ds(spot, rows_dev), :].T[:1, :]


def combine(place, lse, lams, parts):
    outer = len(parts)
    rows_dev, width = parts[0].shape
    lanes = math.gcd(width, 128)
    vmem = pl.BlockSpec(memory_space=pltpu.VMEM)
    return pl.pallas_call(
        functools.partial(combine_kernel, outer),
        out_shape=[
            jax.ShapeDtypeStruct((rows_dev, width), jnp.bfloat16),
            jax.ShapeDtypeStruct((1, rows_dev), jnp.float32),
        ],
        in_specs=[pl.BlockSpec(memory_space=pltpu.SMEM)] + [vmem] * (2 * outer + 1),
        out_specs=[vmem] * 2,
        scratch_shapes=[pltpu.VMEM((outer * rows_dev, lanes), jnp.float32)],
        compiler_params=pltpu.CompilerParams(vmem_limit_bytes=VMEM_LIMIT),
        cost_estimate=pl.CostEstimate(
            flops=2 * outer * rows_dev * width,
            bytes_accessed=2 * outer * rows_dev * width,
            transcendentals=0,
        ),
        name="combine",
    )(place, lse, *lams, *parts)


def columns_kernel(inner, tile, scale, rows_dev, *refs):
    code_ref = refs[0]
    emb = refs[1 : 1 + inner]
    lse = refs[1 + inner : 1 + 2 * inner]
    shift_ref, occ_ref, weighted, folded = refs[1 + 2 * inner :]
    k_dev, width = code_ref.shape
    code = code_ref[...]
    norm = norm_column(code, scale)
    lanes = folded.shape[1]
    weighted[...] = jnp.zeros_like(weighted)
    folded[...] = jnp.zeros_like(folded)

    def one_tile(g, start):
        rows = emb[g][pl.ds(start, tile), :]
        level = LOG2E * lse[g][:, pl.ds(start, tile)]
        s = scale * nt_dot(code, rows) - norm
        shares = jnp.exp2(s - level).astype(jnp.bfloat16)
        wide = shares.astype(jnp.float32)
        part = folded[...]
        for i in range(tile // lanes):
            part = part + wide[:, i * lanes : (i + 1) * lanes]
        folded[...] = part
        weighted[...] += jnp.dot(shares, rows, preferred_element_type=jnp.float32)

    count = emb[0].shape[0] // tile
    for g in range(inner):
        if count <= 4:
            for t in range(count):
                one_tile(g, t * tile)
        else:
            pl.loop(0, count)(lambda t: one_tile(g, pl.multiple_of(t * tile, tile)))
    masses = jnp.sum(folded[...], axis=1, keepdims=True)
    prior = rows_dev / k_dev
    shift_ref[...] = (
        (weighted[...] - masses * code.astype(jnp.float32)) / (masses + prior)
    ).astype(jnp.bfloat16)
    spread = jnp.broadcast_to(masses * (k_dev / rows_dev), (k_dev, lanes)).T
    occ_ref[...] = spread[:1, :]


def columns_calc(code, emb, lse, rows_dev):
    inner = len(emb)
    k_dev, width = code.shape
    rows = emb[0].shape[0]
    tile = math.gcd(rows, 256)
    lanes = math.gcd(tile, 128)
    vmem = pl.BlockSpec(memory_space=pltpu.VMEM)
    return pl.pallas_call(
        functools.partial(
            columns_kernel, inner, tile, LOG2E * 3.0 / math.sqrt(width), rows_dev
        ),
        out_shape=[
            jax.ShapeDtypeStruct((k_dev, width), jnp.bfloat16),
            jax.ShapeDtypeStruct((1, k_dev), jnp.float32),
        ],
        in_specs=[vmem] * (2 * inner + 1),
        out_specs=[vmem] * 2,
        scratch_shapes=[
            pltpu.VMEM((k_dev, width), jnp.float32),
            pltpu.VMEM((k_dev, lanes), jnp.float32),
        ],
        compiler_params=pltpu.CompilerParams(vmem_limit_bytes=VMEM_LIMIT),
        cost_estimate=pl.CostEstimate(
            flops=4 * inner * rows * k_dev * width,
            bytes_accessed=2 * (inner * rows + 2 * k_dev) * width,
            transcendentals=inner * rows * k_dev,
        ),
        name="columns_calc",
    )(code, *emb, *lse)


def on_device(size, embeddings, codebook):
    inner = 4
    outer = size // inner
    rows_dev = embeddings.shape[0]
    place = (lax.axis_index(AXIS) // inner).astype(jnp.int32).reshape(1)

    def swap(x, step):
        return lax.ppermute(x, AXIS, [(i, i ^ step) for i in range(size)])

    code_y = swap(codebook, 2)
    emb = [embeddings] + [swap(embeddings, inner * j) for j in range(1, outer)]
    code = [codebook, swap(codebook, 1), code_y, swap(code_y, 1)]
    lam, stacked, parts = rows_calc(place, emb, code)

    lams = [lam] + [swap(lam, inner * j) for j in range(1, outer)]
    parts = [parts[0]] + [swap(parts[j], inner * j) for j in range(1, outer)]
    top = functools.reduce(jnp.maximum, lams)
    lse = top + jnp.log(sum(jnp.exp(x - top) for x in lams))

    stacked_y = swap(stacked, 2)
    lse_y = swap(lse, 2)
    every_emb = [stacked, swap(stacked, 1), stacked_y, swap(stacked_y, 1)]
    every_lse = [lse, swap(lse, 1), lse_y, swap(lse_y, 1)]
    soft, own_lse = combine(place, lse, lams, parts)
    shift, occupancy = columns_calc(codebook, every_emb, every_lse, rows_dev)
    return shift, occupancy.reshape(-1), soft, own_lse.reshape(-1)


def solution(mesh):
    specs = P(("groups", AXIS), None)
    flat = P(("groups", AXIS))
    return jax.shard_map(
        functools.partial(on_device, mesh.shape[AXIS]),
        mesh=mesh,
        in_specs=(specs, specs),
        out_specs=(specs, flat, specs, flat),
        check_vma=False,
    )
```

```python
import functools
import math

import jax
import jax.numpy as jnp
from jax import lax
from jax.experimental import pallas as pl
from jax.experimental.pallas import tpu as pltpu
from jax.sharding import PartitionSpec as P

AXIS = "blk"
LOG2E = math.log2(math.e)
LN2 = math.log(2.0)
VMEM_LIMIT = 48 * 1024 * 1024


def nt_dot(a, b):
    return lax.dot_general(a, b, (((1,), (1,)), ((), ())), preferred_element_type=jnp.float32)


def norm_column(code, scale):
    c = code.astype(jnp.float32)
    return (0.5 * scale) * jnp.sum(c * c, axis=1, keepdims=True)


def stack_kernel(inner, place_ref, *refs):
    blocks, out_ref = refs[:-1], refs[-1]
    rows_dev = blocks[0].shape[0]
    place = place_ref[0] // inner
    for j, block in enumerate(blocks):
        spot = pl.multiple_of((place ^ j) * rows_dev, rows_dev)
        out_ref[pl.ds(spot, rows_dev), :] = block[...]


def stack(place, blocks, inner):
    rows_dev, width = blocks[0].shape
    vmem = pl.BlockSpec(memory_space=pltpu.VMEM)
    return pl.pallas_call(
        functools.partial(stack_kernel, inner),
        out_shape=jax.ShapeDtypeStruct((len(blocks) * rows_dev, width), blocks[0].dtype),
        in_specs=[pl.BlockSpec(memory_space=pltpu.SMEM)] + [vmem] * len(blocks),
        out_specs=vmem,
        compiler_params=pltpu.CompilerParams(vmem_limit_bytes=VMEM_LIMIT),
        cost_estimate=pl.CostEstimate(
            flops=0, bytes_accessed=4 * len(blocks) * rows_dev * width, transcendentals=0
        ),
        name="stack",
    )(place, *blocks)


def rows_kernel(outer, inner, tile, scale, place_ref, stacked_ref, *refs):
    code = refs[:inner]
    lam_ref = refs[inner]
    parts = refs[inner + 1 : inner + 1 + outer]
    code_t, scores, total = refs[inner + 1 + outer :]
    rows = stacked_ref.shape[0]
    rows_dev = rows // outer
    k_dev = code[0].shape[0]
    place = place_ref[0] // inner
    norms = []
    for k in range(inner):
        block = code[k][...]
        code_t[:, k * k_dev : (k + 1) * k_dev] = block.T
        norms.append(norm_column(block, scale))

    def one_tile(start):
        rows_here = stacked_ref[pl.ds(start, tile), :]
        top = None
        for k in range(inner):
            s = scale * nt_dot(code[k][...], rows_here) - norms[k]
            scores[k * k_dev : (k + 1) * k_dev, :] = s
            m = jnp.max(s, axis=0, keepdims=True)
            top = m if top is None else jnp.maximum(top, m)
        mass = jnp.zeros((1, tile), jnp.float32)
        acc = jnp.zeros((code_t.shape[0], tile), jnp.float32)
        for k in range(inner):
            p = jnp.exp2(scores[k * k_dev : (k + 1) * k_dev, :] - top)
            mass = mass + jnp.sum(p, axis=0, keepdims=True)
            acc = acc + jnp.dot(
                code_t[:, k * k_dev : (k + 1) * k_dev],
                p.astype(jnp.bfloat16),
                preferred_element_type=jnp.float32,
            )
        lam = LN2 * (top + jnp.log2(mass))
        lam_ref[:, :, pl.ds(start, tile)] = jnp.broadcast_to(
            lam.reshape(1, 1, tile), (lam_ref.shape[0], 1, tile)
        )
        total[pl.ds(start, tile), :] = (acc * (1.0 / mass)).T.astype(jnp.bfloat16)

    count = rows // tile
    if count <= 4:
        for t in range(count):
            one_tile(t * tile)
    else:
        pl.loop(0, count)(lambda t: one_tile(pl.multiple_of(t * tile, tile)))
    for j in range(outer):
        spot = pl.multiple_of((place ^ j) * rows_dev, rows_dev)
        parts[j][...] = total[pl.ds(spot, rows_dev), :]


def rows_calc(place, stacked, code, outer):
    inner = len(code)
    rows, width = stacked.shape
    rows_dev = rows // outer
    k_dev = code[0].shape[0]
    entries = inner * k_dev
    tile = math.gcd(rows, 256)
    vmem = pl.BlockSpec(memory_space=pltpu.VMEM)
    out = pl.pallas_call(
        functools.partial(rows_kernel, outer, inner, tile, LOG2E * 3.0 / math.sqrt(width)),
        out_shape=[jax.ShapeDtypeStruct((outer * inner, 1, rows), jnp.float32)]
        + [jax.ShapeDtypeStruct((rows_dev, width), jnp.bfloat16)] * outer,
        in_specs=[pl.BlockSpec(memory_space=pltpu.SMEM)] + [vmem] * (1 + inner),
        out_specs=[vmem] * (outer + 1),
        scratch_shapes=[
            pltpu.VMEM((width, entries), jnp.bfloat16),
            pltpu.VMEM((entries, tile), jnp.float32),
            pltpu.VMEM((rows, width), jnp.bfloat16),
        ],
        compiler_params=pltpu.CompilerParams(vmem_limit_bytes=VMEM_LIMIT),
        cost_estimate=pl.CostEstimate(
            flops=4 * rows * entries * width,
            bytes_accessed=2 * (rows + entries) * width,
            transcendentals=rows * entries,
        ),
        name="rows_calc",
    )(place, stacked, *code)
    return out[0], out[1:]


def final_kernel(outer, inner, tile, scale, place_ref, lam_ref, code_ref, *refs):
    emb = refs[:inner]
    parts = refs[inner : inner + outer]
    shift_ref, occ_ref, soft_ref, own_ref = refs[inner + outer : inner + outer + 4]
    lse, columns, weighted, folded = refs[inner + outer + 4 :]
    k_dev, width = code_ref.shape
    rows_dev = parts[0].shape[0]
    rows = emb[0].shape[0]
    lanes = folded.shape[1]
    place, spoke = place_ref[0] // inner, place_ref[0] % inner

    def lam(z, q):
        return lam_ref[z * inner + q]

    for g in range(inner):
        each = [lam(z, spoke ^ g) for z in range(outer)]
        top = functools.reduce(jnp.maximum, each)
        lse[g : g + 1, :] = top + jnp.log(sum(jnp.exp(x - top) for x in each))

    code = code_ref[...]
    norm = norm_column(code, scale)
    weighted[...] = jnp.zeros_like(weighted)
    folded[...] = jnp.zeros_like(folded)

    def one_tile(g, start):
        rows_here = emb[g][pl.ds(start, tile), :]
        level = LOG2E * lse[g : g + 1, pl.ds(start, tile)]
        s = scale * nt_dot(code, rows_here) - norm
        shares = jnp.exp2(s - level).astype(jnp.bfloat16)
        wide = shares.astype(jnp.float32)
        part = folded[...]
        for i in range(tile // lanes):
            part = part + wide[:, i * lanes : (i + 1) * lanes]
        folded[...] = part
        weighted[...] += jnp.dot(shares, rows_here, preferred_element_type=jnp.float32)

    count = rows // tile
    for g in range(inner):
        if count <= 4:
            for t in range(count):
                one_tile(g, t * tile)
        else:
            pl.loop(0, count)(lambda t: one_tile(g, pl.multiple_of(t * tile, tile)))
    masses = jnp.sum(folded[...], axis=1, keepdims=True)
    prior = rows_dev / k_dev
    shift_ref[...] = (
        (weighted[...] - masses * code.astype(jnp.float32)) / (masses + prior)
    ).astype(jnp.bfloat16)
    spread = jnp.broadcast_to(masses * (k_dev / rows_dev), (k_dev, lanes)).T
    occ_ref[...] = spread[:1, :]

    spot = pl.multiple_of(place * rows_dev, rows_dev)

    def own_rows(line):
        columns[...] = jnp.broadcast_to(line, (lanes, rows)).T
        return columns[pl.ds(spot, rows_dev), :]

    mine = lse[0:1, :]
    total = jnp.zeros((rows_dev, width), jnp.float32)
    for j in range(outer):
        w = own_rows(jnp.exp(lam(place ^ j, spoke) - mine))
        w = jnp.concatenate([w] * (width // lanes), axis=1)
        total = total + w * parts[j][...].astype(jnp.float32)
    soft_ref[...] = total.astype(jnp.bfloat16)
    own_ref[...] = own_rows(mine).T[:1, :]


def final_calc(place, lam, code, emb, parts):
    inner, outer = len(emb), len(parts)
    k_dev, width = code.shape
    rows = emb[0].shape[0]
    rows_dev = rows // outer
    tile = math.gcd(rows, 256)
    lanes = math.gcd(tile, 128)
    vmem = pl.BlockSpec(memory_space=pltpu.VMEM)
    return pl.pallas_call(
        functools.partial(
            final_kernel, outer, inner, tile, LOG2E * 3.0 / math.sqrt(width)
        ),
        out_shape=[
            jax.ShapeDtypeStruct((k_dev, width), jnp.bfloat16),
            jax.ShapeDtypeStruct((1, k_dev), jnp.float32),
            jax.ShapeDtypeStruct((rows_dev, width), jnp.bfloat16),
            jax.ShapeDtypeStruct((1, rows_dev), jnp.float32),
        ],
        in_specs=[pl.BlockSpec(memory_space=pltpu.SMEM)] + [vmem] * (2 + inner + outer),
        out_specs=[vmem] * 4,
        scratch_shapes=[
            pltpu.VMEM((inner, rows), jnp.float32),
            pltpu.VMEM((rows, lanes), jnp.float32),
            pltpu.VMEM((k_dev, width), jnp.float32),
            pltpu.VMEM((k_dev, lanes), jnp.float32),
        ],
        compiler_params=pltpu.CompilerParams(vmem_limit_bytes=VMEM_LIMIT),
        cost_estimate=pl.CostEstimate(
            flops=4 * inner * rows * k_dev * width,
            bytes_accessed=2 * (inner * rows + 2 * k_dev) * width,
            transcendentals=inner * rows * k_dev,
        ),
        name="final_calc",
    )(place, lam, code, *emb, *parts)


def on_device(size, embeddings, codebook):
    inner = 4
    outer = size // inner
    place = lax.axis_index(AXIS).astype(jnp.int32).reshape(1)

    def swap(x, step):
        return lax.ppermute(x, AXIS, [(i, i ^ step) for i in range(size)])

    code_y = swap(codebook, 2)
    code_c = swap(codebook, 1)
    emb = [swap(embeddings, inner * j) for j in range(1, outer)]
    code_y, *emb = lax.optimization_barrier((code_y, *emb))
    stacked = stack(place, [embeddings] + emb, inner)
    code = [codebook, code_c, code_y, swap(code_y, 1)]
    stacked_y = swap(stacked, 2)
    lam, parts = rows_calc(place, stacked, code, outer)

    stacked_y, lam = lax.optimization_barrier((stacked_y, lam))
    parts = [parts[0]] + [swap(parts[j], inner * j) for j in range(1, outer)]
    lam = lax.all_to_all(lam, AXIS, 0, 0)
    every_emb = [stacked, swap(stacked, 1), stacked_y, swap(stacked_y, 1)]
    shift, occupancy, soft, own_lse = final_calc(place, lam, codebook, every_emb, parts)
    return shift, occupancy.reshape(-1), soft, own_lse.reshape(-1)


def solution(mesh):
    specs = P(("groups", AXIS), None)
    flat = P(("groups", AXIS))
    return jax.shard_map(
        functools.partial(on_device, mesh.shape[AXIS]),
        mesh=mesh,
        in_specs=(specs, specs),
        out_specs=(specs, flat, specs, flat),
        check_vma=False,
    )
```

```python
import functools
import math

import jax
import jax.numpy as jnp
from jax import lax
from jax.experimental import pallas as pl
from jax.experimental.pallas import tpu as pltpu
from jax.sharding import PartitionSpec as P

AXIS = "blk"
LOG2E = math.log2(math.e)
LN2 = math.log(2.0)
VMEM_LIMIT = 16 * 1024 * 1024


def nt_dot(a, b):
    return lax.dot_general(a, b, (((1,), (1,)), ((), ())), preferred_element_type=jnp.float32)


def norm_column(code, scale):
    c = code.astype(jnp.float32)
    return (0.5 * scale) * jnp.sum(c * c, axis=1, keepdims=True)


def tiles(rows, tile, body):
    count = rows // tile
    if count <= 4:
        for t in range(count):
            body(t * tile)
    else:
        pl.loop(0, count)(lambda t: body(pl.multiple_of(t * tile, tile)))


def stack_kernel(inner, place_ref, own_ref, *refs):
    blocks, out_ref, sem = refs[:-2], refs[-2], refs[-1]
    rows_dev = own_ref.shape[0]
    place = place_ref[0] // inner

    def spot(j):
        return pl.ds(pl.multiple_of((place ^ j) * rows_dev, rows_dev), rows_dev)

    own = pltpu.make_async_copy(own_ref, out_ref.at[spot(0)], sem)
    own.start()
    for j, block in enumerate(blocks):
        out_ref[spot(j + 1), :] = block[...]
    own.wait()


def stack(place, own, blocks, inner):
    rows_dev, width = own.shape
    count = 1 + len(blocks)
    vmem = pl.BlockSpec(memory_space=pltpu.VMEM)
    return pl.pallas_call(
        functools.partial(stack_kernel, inner),
        out_shape=jax.ShapeDtypeStruct((count * rows_dev, width), own.dtype),
        in_specs=[pl.BlockSpec(memory_space=pltpu.SMEM), pl.BlockSpec(memory_space=pltpu.HBM)]
        + [vmem] * len(blocks),
        out_specs=vmem,
        scratch_shapes=[pltpu.SemaphoreType.DMA(())],
        compiler_params=pltpu.CompilerParams(vmem_limit_bytes=VMEM_LIMIT),
        cost_estimate=pl.CostEstimate(
            flops=0, bytes_accessed=4 * count * rows_dev * width, transcendentals=0
        ),
        name="stack",
    )(place, own, *blocks)


def rows_kernel(outer, inner, tile, scale, place_ref, stacked_ref, *refs):
    code = refs[:inner]
    lam_ref = refs[inner]
    parts = refs[inner + 1 : inner + 1 + outer]
    code_t, scores, total = refs[inner + 1 + outer :]
    rows = stacked_ref.shape[0]
    rows_dev = rows // outer
    k_dev = code[0].shape[0]
    place = place_ref[0] // inner
    norms = []
    for k in range(inner):
        block = code[k][...]
        code_t[:, k * k_dev : (k + 1) * k_dev] = block.T
        norms.append(norm_column(block, scale))

    def one_tile(start):
        rows_here = stacked_ref[pl.ds(start, tile), :]
        top = None
        for k in range(inner):
            s = scale * nt_dot(code[k][...], rows_here) - norms[k]
            scores[k * k_dev : (k + 1) * k_dev, :] = s
            m = jnp.max(s, axis=0, keepdims=True)
            top = m if top is None else jnp.maximum(top, m)
        mass = jnp.zeros((1, tile), jnp.float32)
        acc = jnp.zeros((code_t.shape[0], tile), jnp.float32)
        for k in range(inner):
            p = jnp.exp2(scores[k * k_dev : (k + 1) * k_dev, :] - top)
            mass = mass + jnp.sum(p, axis=0, keepdims=True)
            acc = acc + jnp.dot(
                code_t[:, k * k_dev : (k + 1) * k_dev],
                p.astype(jnp.bfloat16),
                preferred_element_type=jnp.float32,
            )
        lam = LN2 * (top + jnp.log2(mass))
        lam_ref[:, :, pl.ds(start, tile)] = jnp.broadcast_to(
            lam.reshape(1, 1, tile), (lam_ref.shape[0], 1, tile)
        )
        total[pl.ds(start, tile), :] = (acc * (1.0 / mass)).T.astype(jnp.bfloat16)

    tiles(rows, tile, one_tile)
    for j in range(outer):
        spot = pl.multiple_of((place ^ j) * rows_dev, rows_dev)
        parts[j][...] = total[pl.ds(spot, rows_dev), :]


def rows_calc(place, stacked, code, outer):
    inner = len(code)
    rows, width = stacked.shape
    rows_dev = rows // outer
    k_dev = code[0].shape[0]
    entries = inner * k_dev
    tile = math.gcd(rows, 256)
    vmem = pl.BlockSpec(memory_space=pltpu.VMEM)
    out = pl.pallas_call(
        functools.partial(rows_kernel, outer, inner, tile, LOG2E * 3.0 / math.sqrt(width)),
        out_shape=[jax.ShapeDtypeStruct((outer * inner, 1, rows), jnp.float32)]
        + [jax.ShapeDtypeStruct((rows_dev, width), jnp.bfloat16)] * outer,
        in_specs=[pl.BlockSpec(memory_space=pltpu.SMEM)] + [vmem] * (1 + inner),
        out_specs=[vmem] * (outer + 1),
        scratch_shapes=[
            pltpu.VMEM((width, entries), jnp.bfloat16),
            pltpu.VMEM((entries, tile), jnp.float32),
            pltpu.VMEM((rows, width), jnp.bfloat16),
        ],
        compiler_params=pltpu.CompilerParams(vmem_limit_bytes=VMEM_LIMIT),
        cost_estimate=pl.CostEstimate(
            flops=4 * rows * entries * width,
            bytes_accessed=2 * (rows + entries) * width,
            transcendentals=rows * entries,
        ),
        name="rows_calc",
    )(place, stacked, *code)
    return out[0], out[1:]


def norm_kernel(scale, code_ref, out_ref):
    out_ref[...] = jnp.broadcast_to(norm_column(code_ref[...], scale), out_ref.shape)


def norm_calc(code, scale):
    k_dev, width = code.shape
    lanes = math.gcd(width, 128)
    vmem = pl.BlockSpec(memory_space=pltpu.VMEM)
    return pl.pallas_call(
        functools.partial(norm_kernel, scale),
        out_shape=jax.ShapeDtypeStruct((k_dev, lanes), jnp.float32),
        in_specs=[vmem],
        out_specs=vmem,
        compiler_params=pltpu.CompilerParams(vmem_limit_bytes=VMEM_LIMIT),
        cost_estimate=pl.CostEstimate(
            flops=2 * k_dev * width, bytes_accessed=2 * k_dev * width, transcendentals=0
        ),
        name="norm_calc",
    )(code)


def read_lse(lam_ref, outer, inner, spoke):
    each = [lam_ref[z * inner + spoke] for z in range(outer)]
    top = functools.reduce(jnp.maximum, each)
    return top + jnp.log(sum(jnp.exp(x - top) for x in each))


def add_groups(groups, tile, scale, levels, code_ref, norm_ref, emb, weighted, folded):
    lanes = folded.shape[1]
    code = code_ref[...]
    norm = jnp.concatenate([norm_ref[...]] * (tile // lanes), axis=1)
    for g, emb_ref in zip(groups, emb):
        level = LOG2E * levels(g)
        for start in range(0, emb_ref.shape[0], tile):
            rows_here = emb_ref[start : start + tile, :]
            s = scale * nt_dot(code, rows_here) - norm
            shares = jnp.exp2(s - level[:, start : start + tile]).astype(jnp.bfloat16)
            wide = shares.astype(jnp.float32)
            part = folded[...]
            for i in range(tile // lanes):
                part = part + wide[:, i * lanes : (i + 1) * lanes]
            folded[...] = part
            weighted[...] += jnp.dot(shares, rows_here, preferred_element_type=jnp.float32)


def early_kernel(outer, inner, groups, tile, scale, place_ref, lam_ref, code_ref, norm_ref, *refs):
    emb = refs[: len(groups)]
    parts = refs[len(groups) : len(groups) + outer]
    weighted, folded, soft_ref, own_ref, columns = refs[len(groups) + outer :]
    rows_dev, width = parts[0].shape
    rows, lanes = columns.shape
    place, spoke = place_ref[0] // inner, place_ref[0] % inner
    weighted[...] = jnp.zeros_like(weighted)
    folded[...] = jnp.zeros_like(folded)
    levels = lambda g: read_lse(lam_ref, outer, inner, spoke ^ g)
    add_groups(groups, tile, scale, levels, code_ref, norm_ref, emb, weighted, folded)

    spot = pl.multiple_of(place * rows_dev, rows_dev)
    mine = levels(0)

    def own_rows(line):
        columns[...] = jnp.broadcast_to(line, (lanes, rows)).T
        return columns[pl.ds(spot, rows_dev), :]

    total = jnp.zeros((rows_dev, width), jnp.float32)
    for j in range(outer):
        w = own_rows(jnp.exp(lam_ref[(place ^ j) * inner + spoke] - mine))
        w = jnp.concatenate([w] * (width // lanes), axis=1)
        total = total + w * parts[j][...].astype(jnp.float32)
    soft_ref[...] = total.astype(jnp.bfloat16)
    own_ref[...] = own_rows(mine).T[:1, :]


def late_kernel(outer, inner, groups, tile, scale, place_ref, lam_ref, code_ref, norm_ref, *refs):
    emb = refs[: len(groups)]
    weighted_in, folded_in, shift_ref, occ_ref, weighted, folded = refs[len(groups) :]
    k_dev = code_ref.shape[0]
    rows_dev = emb[0].shape[0] // outer
    spoke = place_ref[0] % inner
    weighted[...] = weighted_in[...]
    folded[...] = folded_in[...]
    levels = lambda g: read_lse(lam_ref, outer, inner, spoke ^ g)
    add_groups(groups, tile, scale, levels, code_ref, norm_ref, emb, weighted, folded)
    masses = jnp.sum(folded[...], axis=1, keepdims=True)
    prior = rows_dev / k_dev
    shift_ref[...] = (
        (weighted[...] - masses * code_ref[...].astype(jnp.float32)) / (masses + prior)
    ).astype(jnp.bfloat16)
    spread = jnp.broadcast_to(masses * (k_dev / rows_dev), folded.shape).T
    occ_ref[...] = spread[:1, :]


def columns_calc(place, lam, code, norm, groups, emb, inner, parts=(), sums=()):
    k_dev, width = code.shape
    rows = emb[0].shape[0]
    outer = lam.shape[0] // inner
    rows_dev = rows // outer
    tile = math.gcd(rows, 256)
    lanes = norm.shape[1]
    totals = [((k_dev, width), jnp.float32), ((k_dev, lanes), jnp.float32)]
    if parts:
        body, out = early_kernel, totals + [((rows_dev, width), jnp.bfloat16), ((1, rows_dev), jnp.float32)]
        scratch = [pltpu.VMEM((rows, lanes), jnp.float32)]
    else:
        body, out = late_kernel, [((k_dev, width), jnp.bfloat16), ((1, k_dev), jnp.float32)]
        scratch = [pltpu.VMEM(*x) for x in totals]
    extra = [*parts, *sums]
    vmem = pl.BlockSpec(memory_space=pltpu.VMEM)
    return pl.pallas_call(
        functools.partial(body, outer, inner, groups, tile, LOG2E * 3.0 / math.sqrt(width)),
        out_shape=[jax.ShapeDtypeStruct(*x) for x in out],
        in_specs=[pl.BlockSpec(memory_space=pltpu.SMEM)] + [vmem] * (3 + len(emb) + len(extra)),
        out_specs=[vmem] * len(out),
        scratch_shapes=scratch,
        compiler_params=pltpu.CompilerParams(vmem_limit_bytes=VMEM_LIMIT),
        cost_estimate=pl.CostEstimate(
            flops=(64 if parts else 4) * len(emb) * rows * k_dev * width,
            bytes_accessed=2 * (len(emb) * rows + 2 * k_dev) * width,
            transcendentals=len(emb) * rows * k_dev,
        ),
        name="columns_calc",
    )(place, lam, code, norm, *emb, *extra)


def after(x, y):
    return lax.optimization_barrier((x, y))[0]


def on_device(size, embeddings, codebook):
    inner = 4
    outer = size // inner
    place = lax.axis_index(AXIS).astype(jnp.int32).reshape(1)

    def swap(x, step):
        return lax.ppermute(x, AXIS, [(i, i ^ step) for i in range(size)])

    code_y = swap(codebook, 2)
    code_c = swap(codebook, 1)
    emb = [swap(embeddings, inner * j) for j in range(1, outer)]
    code_y, *emb = lax.optimization_barrier((code_y, *emb))
    stacked = stack(place, embeddings, emb, inner)
    stacked_y = swap(stacked, 2)
    stacked_c = swap(stacked, 1)
    code = [codebook, code_c, code_y, swap(code_y, 1)]
    lam, parts = rows_calc(place, stacked, code, outer)

    parts = [parts[0]] + [swap(parts[j], inner * j) for j in range(1, outer)]
    lam = lax.all_to_all(lam, AXIS, 0, 0)
    norm = norm_calc(codebook, LOG2E * 3.0 / math.sqrt(codebook.shape[1]))
    stacked_yc = swap(stacked_y, 1)
    weighted, folded, soft, own_lse = columns_calc(
        place, lam, codebook, norm, (0, 1, 2), [stacked, stacked_c, stacked_y], inner, parts=parts
    )
    shift, occupancy = columns_calc(
        place, lam, codebook, norm, (3,), [stacked_yc], inner, sums=(weighted, folded)
    )
    return shift, occupancy.reshape(-1), soft, own_lse.reshape(-1)


def solution(mesh):
    specs = P(("groups", AXIS), None)
    flat = P(("groups", AXIS))
    return jax.shard_map(
        functools.partial(on_device, mesh.shape[AXIS]),
        mesh=mesh,
        in_specs=(specs, specs),
        out_specs=(specs, flat, specs, flat),
        check_vma=False,
    )
```

```python
import functools
import math

import jax
import jax.numpy as jnp
from jax import lax
from jax.experimental import pallas as pl
from jax.experimental.pallas import tpu as pltpu
from jax.sharding import PartitionSpec as P

AXIS = "blk"
LOG2E = math.log2(math.e)
LN2 = math.log(2.0)
VMEM_LIMIT = 20 * 1024 * 1024
EARLY = 64


def nt_dot(a, b):
    return lax.dot_general(a, b, (((1,), (1,)), ((), ())), preferred_element_type=jnp.float32)


def norm_column(code, scale):
    c = code.astype(jnp.float32)
    return (0.5 * scale) * jnp.sum(c * c, axis=1, keepdims=True)


def tiles(rows, tile, body):
    count = rows // tile
    if count <= 4:
        for t in range(count):
            body(t * tile, t * tile)
    else:
        pl.loop(0, count)(lambda t: body(pl.multiple_of(t * tile, tile), 0))


def keep_kernel(x_ref, out_ref):
    out_ref[...] = x_ref[...]


def keep(x):
    vmem = pl.BlockSpec(memory_space=pltpu.VMEM)
    return pl.pallas_call(
        keep_kernel,
        out_shape=jax.ShapeDtypeStruct(x.shape, x.dtype),
        in_specs=[vmem],
        out_specs=vmem,
        compiler_params=pltpu.CompilerParams(vmem_limit_bytes=VMEM_LIMIT),
        cost_estimate=pl.CostEstimate(flops=0, bytes_accessed=4 * x.size, transcendentals=0),
        name="keep",
    )(x)


def stack_kernel(inner, place_ref, *refs):
    blocks, out_ref = refs[:-1], refs[-1]
    rows_dev = blocks[0].shape[0]
    place = place_ref[0] // inner
    for j, block in enumerate(blocks):
        spot = pl.multiple_of((place ^ j) * rows_dev, rows_dev)
        out_ref[pl.ds(spot, rows_dev), :] = block[...]


def stack(place, blocks, inner):
    rows_dev, width = blocks[0].shape
    vmem = pl.BlockSpec(memory_space=pltpu.VMEM)
    return pl.pallas_call(
        functools.partial(stack_kernel, inner),
        out_shape=jax.ShapeDtypeStruct((len(blocks) * rows_dev, width), blocks[0].dtype),
        in_specs=[pl.BlockSpec(memory_space=pltpu.SMEM)] + [vmem] * len(blocks),
        out_specs=vmem,
        compiler_params=pltpu.CompilerParams(vmem_limit_bytes=VMEM_LIMIT),
        cost_estimate=pl.CostEstimate(
            flops=0, bytes_accessed=4 * len(blocks) * rows_dev * width, transcendentals=0
        ),
        name="stack",
    )(place, *blocks)


def fold_lanes(op, x, lanes):
    parts = [x[:, i : i + lanes] for i in range(0, x.shape[1], lanes)]
    return functools.reduce(op, parts)


def rows_kernel(outer, inner, tile, scale, place_ref, stacked_ref, *refs):
    code = refs[:inner]
    lam_ref = refs[inner]
    parts = refs[inner + 1 : inner + 1 + outer]
    scores, total = refs[inner + 1 + outer :]
    rows, width = stacked_ref.shape
    rows_dev = rows // outer
    k_dev = code[0].shape[0]
    lanes = math.gcd(k_dev, 128)
    place = place_ref[0] // inner
    norms = [
        jnp.broadcast_to(norm_column(code[k][...], scale), (k_dev, lanes)).T[:1, :]
        for k in range(inner)
    ]

    def one_tile(start, slot):
        rows_here = stacked_ref[pl.ds(start, tile), :]
        top = None
        for k in range(inner):
            s = scale * nt_dot(rows_here, code[k][...]) - norms[k]
            scores[slot : slot + tile, k * k_dev : (k + 1) * k_dev] = s
            m = fold_lanes(jnp.maximum, s, lanes)
            top = m if top is None else jnp.maximum(top, m)
        top = jnp.max(top, axis=1, keepdims=True)
        mass = jnp.zeros((tile, lanes), jnp.float32)
        acc = jnp.zeros((tile, width), jnp.float32)
        for k in range(inner):
            p = jnp.exp2(scores[slot : slot + tile, k * k_dev : (k + 1) * k_dev] - top)
            mass = mass + fold_lanes(jnp.add, p, lanes)
            acc = acc + jnp.dot(
                p.astype(jnp.bfloat16), code[k][...], preferred_element_type=jnp.float32
            )
        mass = jnp.sum(mass, axis=1, keepdims=True)
        lam = jnp.broadcast_to(LN2 * (top + jnp.log2(mass)), (tile, lanes)).T[:1, :]
        lam_ref[:, :, pl.ds(start, tile)] = jnp.broadcast_to(
            lam.reshape(1, 1, tile), (lam_ref.shape[0], 1, tile)
        )
        total[pl.ds(start, tile), :] = (acc * (1.0 / mass)).astype(jnp.bfloat16)

    tiles(rows, tile, one_tile)
    for j in range(outer):
        spot = pl.multiple_of((place ^ j) * rows_dev, rows_dev)
        parts[j][...] = total[pl.ds(spot, rows_dev), :]


def rows_calc(place, stacked, code, outer):
    inner = len(code)
    rows, width = stacked.shape
    rows_dev = rows // outer
    entries = inner * code[0].shape[0]
    tile = math.gcd(rows, 256)
    vmem = pl.BlockSpec(memory_space=pltpu.VMEM)
    out = pl.pallas_call(
        functools.partial(rows_kernel, outer, inner, tile, LOG2E * 3.0 / math.sqrt(width)),
        out_shape=[jax.ShapeDtypeStruct((outer * inner, 1, rows), jnp.float32)]
        + [jax.ShapeDtypeStruct((rows_dev, width), jnp.bfloat16)] * outer,
        in_specs=[pl.BlockSpec(memory_space=pltpu.SMEM)] + [vmem] * (1 + inner),
        out_specs=[vmem] * (outer + 1),
        scratch_shapes=[
            pltpu.VMEM((min(rows, 4 * tile), entries), jnp.float32),
            pltpu.VMEM((rows, width), jnp.bfloat16),
        ],
        compiler_params=pltpu.CompilerParams(vmem_limit_bytes=VMEM_LIMIT),
        cost_estimate=pl.CostEstimate(
            flops=4 * rows * entries * width,
            bytes_accessed=2 * (rows + entries) * width,
            transcendentals=rows * entries,
        ),
        name="rows_calc",
    )(place, stacked, *code)
    return out[0], out[1:]


def norm_kernel(scale, code_ref, out_ref):
    out_ref[...] = jnp.broadcast_to(norm_column(code_ref[...], scale), out_ref.shape)


def norm_calc(code, scale):
    k_dev, width = code.shape
    lanes = math.gcd(width, 128)
    vmem = pl.BlockSpec(memory_space=pltpu.VMEM)
    return pl.pallas_call(
        functools.partial(norm_kernel, scale),
        out_shape=jax.ShapeDtypeStruct((k_dev, lanes), jnp.float32),
        in_specs=[vmem],
        out_specs=vmem,
        compiler_params=pltpu.CompilerParams(vmem_limit_bytes=VMEM_LIMIT),
        cost_estimate=pl.CostEstimate(
            flops=2 * k_dev * width, bytes_accessed=2 * k_dev * width, transcendentals=0
        ),
        name="norm_calc",
    )(code)


def read_lse(lam_ref, outer, inner, spoke):
    each = [lam_ref[z * inner + spoke] for z in range(outer)]
    top = functools.reduce(jnp.maximum, each)
    return top + jnp.log(sum(jnp.exp(x - top) for x in each))


def add_groups(groups, tile, scale, levels, code_ref, norm_ref, emb, weighted, folded):
    lanes = folded.shape[1]
    code = code_ref[...]
    norm = jnp.concatenate([norm_ref[...]] * (tile // lanes), axis=1)
    for g, emb_ref in zip(groups, emb):
        level = LOG2E * levels(g)
        for start in range(0, emb_ref.shape[0], tile):
            rows_here = emb_ref[start : start + tile, :]
            s = scale * nt_dot(code, rows_here) - norm
            shares = jnp.exp2(s - level[:, start : start + tile]).astype(jnp.bfloat16)
            wide = shares.astype(jnp.float32)
            part = folded[...]
            for i in range(tile // lanes):
                part = part + wide[:, i * lanes : (i + 1) * lanes]
            folded[...] = part
            weighted[...] += jnp.dot(shares, rows_here, preferred_element_type=jnp.float32)


def early_kernel(outer, inner, groups, tile, scale, place_ref, lam_ref, code_ref, norm_ref, *refs):
    emb = refs[: len(groups)]
    weighted, folded = refs[len(groups) :]
    spoke = place_ref[0] % inner
    weighted[...] = jnp.zeros_like(weighted)
    folded[...] = jnp.zeros_like(folded)
    levels = lambda g: read_lse(lam_ref, outer, inner, spoke ^ g)
    add_groups(groups, tile, scale, levels, code_ref, norm_ref, emb, weighted, folded)


def late_kernel(outer, inner, groups, tile, scale, place_ref, lam_ref, code_ref, norm_ref, *refs):
    emb = refs[: len(groups)]
    weighted_in, folded_in, shift_ref, occ_ref, weighted, folded = refs[len(groups) :]
    k_dev = code_ref.shape[0]
    rows_dev = emb[0].shape[0] // outer
    spoke = place_ref[0] % inner
    weighted[...] = weighted_in[...]
    folded[...] = folded_in[...]
    levels = lambda g: read_lse(lam_ref, outer, inner, spoke ^ g)
    add_groups(groups, tile, scale, levels, code_ref, norm_ref, emb, weighted, folded)
    masses = jnp.sum(folded[...], axis=1, keepdims=True)
    prior = rows_dev / k_dev
    shift_ref[...] = (
        (weighted[...] - masses * code_ref[...].astype(jnp.float32)) / (masses + prior)
    ).astype(jnp.bfloat16)
    spread = jnp.broadcast_to(masses * (k_dev / rows_dev), folded.shape).T
    occ_ref[...] = spread[:1, :]


def columns_calc(place, lam, code, norm, groups, emb, inner, sums=()):
    k_dev, width = code.shape
    rows = emb[0].shape[0]
    outer = lam.shape[0] // inner
    tile = math.gcd(rows, 768)
    lanes = norm.shape[1]
    totals = [((k_dev, width), jnp.float32), ((k_dev, lanes), jnp.float32)]
    if sums:
        body, out = late_kernel, [((k_dev, width), jnp.bfloat16), ((1, k_dev), jnp.float32)]
        scratch = [pltpu.VMEM(*x) for x in totals]
    else:
        body, out, scratch = early_kernel, totals, []
    vmem = pl.BlockSpec(memory_space=pltpu.VMEM)
    return pl.pallas_call(
        functools.partial(body, outer, inner, groups, tile, LOG2E * 3.0 / math.sqrt(width)),
        out_shape=[jax.ShapeDtypeStruct(*x) for x in out],
        in_specs=[pl.BlockSpec(memory_space=pltpu.SMEM)] + [vmem] * (3 + len(emb) + len(sums)),
        out_specs=[vmem] * len(out),
        scratch_shapes=scratch,
        compiler_params=pltpu.CompilerParams(vmem_limit_bytes=VMEM_LIMIT),
        cost_estimate=pl.CostEstimate(
            flops=(4 if sums else EARLY) * len(emb) * rows * k_dev * width,
            bytes_accessed=2 * (len(emb) * rows + 2 * k_dev) * width,
            transcendentals=len(emb) * rows * k_dev,
        ),
        name="columns_calc",
    )(place, lam, code, norm, *emb, *sums)


def combine_kernel(outer, inner, place_ref, lam_ref, *refs):
    parts, (soft_ref, own_ref, columns) = refs[:outer], refs[outer:]
    rows_dev, width = parts[0].shape
    rows, lanes = columns.shape
    place, spoke = place_ref[0] // inner, place_ref[0] % inner
    spot = pl.multiple_of(place * rows_dev, rows_dev)
    mine = read_lse(lam_ref, outer, inner, spoke)

    def own_rows(line):
        columns[...] = jnp.broadcast_to(line, (lanes, rows)).T
        return columns[pl.ds(spot, rows_dev), :]

    total = jnp.zeros((rows_dev, width), jnp.float32)
    for j in range(outer):
        w = own_rows(jnp.exp(lam_ref[(place ^ j) * inner + spoke] - mine))
        w = jnp.concatenate([w] * (width // lanes), axis=1)
        total = total + w * parts[j][...].astype(jnp.float32)
    soft_ref[...] = total.astype(jnp.bfloat16)
    own_ref[...] = own_rows(mine).T[:1, :]


def combine(place, lam, parts):
    outer = len(parts)
    inner = lam.shape[0] // outer
    rows_dev, width = parts[0].shape
    lanes = math.gcd(width, 128)
    vmem = pl.BlockSpec(memory_space=pltpu.VMEM)
    return pl.pallas_call(
        functools.partial(combine_kernel, outer, inner),
        out_shape=[
            jax.ShapeDtypeStruct((rows_dev, width), jnp.bfloat16),
            jax.ShapeDtypeStruct((1, rows_dev), jnp.float32),
        ],
        in_specs=[pl.BlockSpec(memory_space=pltpu.SMEM)] + [vmem] * (outer + 1),
        out_specs=[vmem] * 2,
        scratch_shapes=[pltpu.VMEM((outer * rows_dev, lanes), jnp.float32)],
        compiler_params=pltpu.CompilerParams(vmem_limit_bytes=VMEM_LIMIT),
        cost_estimate=pl.CostEstimate(
            flops=2 * outer * rows_dev * width,
            bytes_accessed=2 * outer * rows_dev * width,
            transcendentals=0,
        ),
        name="combine",
    )(place, lam, *parts)


def after(x, y):
    return lax.optimization_barrier((x, y))[0]


def on_device(size, embeddings, codebook):
    inner = 4
    outer = size // inner
    place = lax.axis_index(AXIS).astype(jnp.int32).reshape(1)

    def swap(x, step):
        return lax.ppermute(x, AXIS, [(i, i ^ step) for i in range(size)])

    code_y = swap(codebook, 2)
    code_c = swap(codebook, 1)
    emb = [swap(embeddings, inner * j) for j in range(1, outer)]
    code_y, *emb = lax.optimization_barrier((code_y, keep(embeddings), *emb))
    stacked = stack(place, emb, inner)
    stacked_y = swap(stacked, 2)
    stacked_c = swap(stacked, 1)
    code = [codebook, code_c, code_y, swap(code_y, 1)]
    lam, parts = rows_calc(place, stacked, code, outer)

    order = sorted(range(1, outer), key=lambda j: j < 2)
    sent = {j: swap(parts[j], inner * j) for j in order}
    lam = lax.all_to_all(lam, AXIS, 0, 0)
    norm = norm_calc(codebook, LOG2E * 3.0 / math.sqrt(codebook.shape[1]))
    stacked_yc = swap(stacked_y, 1)
    sums = columns_calc(
        place, lam, codebook, norm, (0, 1, 2), [stacked, stacked_c, stacked_y], inner
    )
    shift, occupancy = columns_calc(
        place, lam, codebook, norm, (3,), [stacked_yc], inner, sums
    )
    parts = [after(parts[0], occupancy)] + [sent[j] for j in range(1, outer)]
    soft, own_lse = combine(place, lam, parts)
    return shift, occupancy.reshape(-1), soft, own_lse.reshape(-1)


def solution(mesh):
    specs = P(("groups", AXIS), None)
    flat = P(("groups", AXIS))
    return jax.shard_map(
        functools.partial(on_device, mesh.shape[AXIS]),
        mesh=mesh,
        in_specs=(specs, specs),
        out_specs=(specs, flat, specs, flat),
        check_vma=False,
    )
```

```python
import functools
import math

import jax
import jax.numpy as jnp
from jax import lax
from jax.experimental import pallas as pl
from jax.experimental.pallas import tpu as pltpu
from jax.sharding import PartitionSpec as P

AXIS = "blk"
LOG2E = math.log2(math.e)
LN2 = math.log(2.0)
VMEM_LIMIT = 20 * 1024 * 1024
EARLY = 64
STACK = 1 << 32


def nt_dot(a, b):
    return lax.dot_general(a, b, (((1,), (1,)), ((), ())), preferred_element_type=jnp.float32)


def norm_column(code, scale):
    c = code.astype(jnp.float32)
    return (0.5 * scale) * jnp.sum(c * c, axis=1, keepdims=True)


def tiles(rows, tile, body):
    count = rows // tile
    if count <= 4:
        for t in range(count):
            body(t * tile, t * tile)
    else:
        pl.loop(0, count)(lambda t: body(pl.multiple_of(t * tile, tile), 0))


def keep_kernel(x_ref, out_ref):
    out_ref[...] = x_ref[...]


def keep(x):
    vmem = pl.BlockSpec(memory_space=pltpu.VMEM)
    return pl.pallas_call(
        keep_kernel,
        out_shape=jax.ShapeDtypeStruct(x.shape, x.dtype),
        in_specs=[vmem],
        out_specs=vmem,
        compiler_params=pltpu.CompilerParams(vmem_limit_bytes=VMEM_LIMIT),
        cost_estimate=pl.CostEstimate(flops=0, bytes_accessed=4 * x.size, transcendentals=0),
        name="keep",
    )(x)


def stack_kernel(inner, steps, place_ref, *refs):
    blocks, out_ref = refs[: len(steps)], refs[-1]
    rows_dev = blocks[0].shape[0]
    place = place_ref[0] // inner
    for j, block in zip(steps, blocks):
        spot = pl.multiple_of((place ^ j) * rows_dev, rows_dev)
        out_ref[pl.ds(spot, rows_dev), :] = block[...]


def stack(place, blocks, steps, inner, shape, into=()):
    vmem = pl.BlockSpec(memory_space=pltpu.VMEM)
    return pl.pallas_call(
        functools.partial(stack_kernel, inner, steps),
        out_shape=jax.ShapeDtypeStruct(shape, blocks[0].dtype),
        in_specs=[pl.BlockSpec(memory_space=pltpu.SMEM)] + [vmem] * (len(blocks) + len(into)),
        out_specs=vmem,
        input_output_aliases={1 + len(blocks): 0} if into else {},
        compiler_params=pltpu.CompilerParams(vmem_limit_bytes=VMEM_LIMIT),
        cost_estimate=pl.CostEstimate(
            flops=0 if into else STACK, bytes_accessed=4 * shape[0] * shape[1], transcendentals=0
        ),
        name="stack",
    )(place, *blocks, *into)


def fold_lanes(op, x, lanes):
    parts = [x[:, i : i + lanes] for i in range(0, x.shape[1], lanes)]
    return functools.reduce(op, parts)


def rows_kernel(outer, inner, tile, scale, place_ref, stacked_ref, *refs):
    code = refs[:inner]
    lam_ref = refs[inner]
    parts = refs[inner + 1 : inner + 1 + outer]
    scores, total = refs[inner + 1 + outer :]
    rows, width = stacked_ref.shape
    rows_dev = rows // outer
    k_dev = code[0].shape[0]
    lanes = math.gcd(k_dev, 128)
    place = place_ref[0] // inner
    norms = [
        jnp.broadcast_to(norm_column(code[k][...], scale), (k_dev, lanes)).T[:1, :]
        for k in range(inner)
    ]

    def one_tile(start, slot):
        rows_here = stacked_ref[pl.ds(start, tile), :]
        top = None
        for k in range(inner):
            s = scale * nt_dot(rows_here, code[k][...]) - norms[k]
            scores[slot : slot + tile, k * k_dev : (k + 1) * k_dev] = s
            m = fold_lanes(jnp.maximum, s, lanes)
            top = m if top is None else jnp.maximum(top, m)
        top = jnp.max(top, axis=1, keepdims=True)
        mass = jnp.zeros((tile, lanes), jnp.float32)
        acc = jnp.zeros((tile, width), jnp.float32)
        for k in range(inner):
            p = jnp.exp2(scores[slot : slot + tile, k * k_dev : (k + 1) * k_dev] - top)
            mass = mass + fold_lanes(jnp.add, p, lanes)
            acc = acc + jnp.dot(
                p.astype(jnp.bfloat16), code[k][...], preferred_element_type=jnp.float32
            )
        mass = jnp.sum(mass, axis=1, keepdims=True)
        lam = jnp.broadcast_to(LN2 * (top + jnp.log2(mass)), (tile, lanes)).T[:1, :]
        lam_ref[:, :, pl.ds(start, tile)] = jnp.broadcast_to(
            lam.reshape(1, 1, tile), (lam_ref.shape[0], 1, tile)
        )
        total[pl.ds(start, tile), :] = (acc * (1.0 / mass)).astype(jnp.bfloat16)

    tiles(rows, tile, one_tile)
    for j in range(outer):
        spot = pl.multiple_of((place ^ j) * rows_dev, rows_dev)
        parts[j][...] = total[pl.ds(spot, rows_dev), :]


def rows_calc(place, stacked, code, outer):
    inner = len(code)
    rows, width = stacked.shape
    rows_dev = rows // outer
    entries = inner * code[0].shape[0]
    tile = math.gcd(rows, 256)
    vmem = pl.BlockSpec(memory_space=pltpu.VMEM)
    out = pl.pallas_call(
        functools.partial(rows_kernel, outer, inner, tile, LOG2E * 3.0 / math.sqrt(width)),
        out_shape=[jax.ShapeDtypeStruct((outer * inner, 1, rows), jnp.float32)]
        + [jax.ShapeDtypeStruct((rows_dev, width), jnp.bfloat16)] * outer,
        in_specs=[pl.BlockSpec(memory_space=pltpu.SMEM)] + [vmem] * (1 + inner),
        out_specs=[vmem] * (outer + 1),
        scratch_shapes=[
            pltpu.VMEM((min(rows, 4 * tile), entries), jnp.float32),
            pltpu.VMEM((rows, width), jnp.bfloat16),
        ],
        compiler_params=pltpu.CompilerParams(vmem_limit_bytes=VMEM_LIMIT),
        cost_estimate=pl.CostEstimate(
            flops=4 * rows * entries * width,
            bytes_accessed=2 * (rows + entries) * width,
            transcendentals=rows * entries,
        ),
        name="rows_calc",
    )(place, stacked, *code)
    return out[0], out[1:]


def norm_kernel(scale, code_ref, out_ref):
    out_ref[...] = jnp.broadcast_to(norm_column(code_ref[...], scale), out_ref.shape)


def norm_calc(code, scale):
    k_dev, width = code.shape
    lanes = math.gcd(width, 128)
    vmem = pl.BlockSpec(memory_space=pltpu.VMEM)
    return pl.pallas_call(
        functools.partial(norm_kernel, scale),
        out_shape=jax.ShapeDtypeStruct((k_dev, lanes), jnp.float32),
        in_specs=[vmem],
        out_specs=vmem,
        compiler_params=pltpu.CompilerParams(vmem_limit_bytes=VMEM_LIMIT),
        cost_estimate=pl.CostEstimate(
            flops=2 * k_dev * width, bytes_accessed=2 * k_dev * width, transcendentals=0
        ),
        name="norm_calc",
    )(code)


def read_lse(lam_ref, outer, inner, spoke):
    each = [lam_ref[z * inner + spoke] for z in range(outer)]
    top = functools.reduce(jnp.maximum, each)
    return top + jnp.log(sum(jnp.exp(x - top) for x in each))


def add_groups(groups, tile, scale, levels, code_ref, norm_ref, emb, weighted, folded):
    lanes = folded.shape[1]
    code = code_ref[...]
    norm = jnp.concatenate([norm_ref[...]] * (tile // lanes), axis=1)
    for g, emb_ref in zip(groups, emb):
        level = LOG2E * levels(g)
        for start in range(0, emb_ref.shape[0], tile):
            rows_here = emb_ref[start : start + tile, :]
            s = scale * nt_dot(code, rows_here) - norm
            shares = jnp.exp2(s - level[:, start : start + tile]).astype(jnp.bfloat16)
            wide = shares.astype(jnp.float32)
            part = folded[...]
            for i in range(tile // lanes):
                part = part + wide[:, i * lanes : (i + 1) * lanes]
            folded[...] = part
            weighted[...] += jnp.dot(shares, rows_here, preferred_element_type=jnp.float32)


def early_kernel(outer, inner, groups, tile, scale, place_ref, lam_ref, code_ref, norm_ref, *refs):
    emb = refs[: len(groups)]
    weighted, folded = refs[len(groups) :]
    spoke = place_ref[0] % inner
    weighted[...] = jnp.zeros_like(weighted)
    folded[...] = jnp.zeros_like(folded)
    levels = lambda g: read_lse(lam_ref, outer, inner, spoke ^ g)
    add_groups(groups, tile, scale, levels, code_ref, norm_ref, emb, weighted, folded)


def late_kernel(outer, inner, groups, tile, scale, place_ref, lam_ref, code_ref, norm_ref, *refs):
    emb = refs[: len(groups)]
    weighted_in, folded_in, shift_ref, occ_ref, weighted, folded = refs[len(groups) :]
    k_dev = code_ref.shape[0]
    rows_dev = emb[0].shape[0] // outer
    spoke = place_ref[0] % inner
    weighted[...] = weighted_in[...]
    folded[...] = folded_in[...]
    levels = lambda g: read_lse(lam_ref, outer, inner, spoke ^ g)
    add_groups(groups, tile, scale, levels, code_ref, norm_ref, emb, weighted, folded)
    masses = jnp.sum(folded[...], axis=1, keepdims=True)
    prior = rows_dev / k_dev
    shift_ref[...] = (
        (weighted[...] - masses * code_ref[...].astype(jnp.float32)) / (masses + prior)
    ).astype(jnp.bfloat16)
    spread = jnp.broadcast_to(masses * (k_dev / rows_dev), folded.shape).T
    occ_ref[...] = spread[:1, :]


def columns_calc(place, lam, code, norm, groups, emb, inner, sums=()):
    k_dev, width = code.shape
    rows = emb[0].shape[0]
    outer = lam.shape[0] // inner
    tile = math.gcd(rows, 768)
    lanes = norm.shape[1]
    totals = [((k_dev, width), jnp.float32), ((k_dev, lanes), jnp.float32)]
    if sums:
        body, out = late_kernel, [((k_dev, width), jnp.bfloat16), ((1, k_dev), jnp.float32)]
        scratch = [pltpu.VMEM(*x) for x in totals]
    else:
        body, out, scratch = early_kernel, totals, []
    vmem = pl.BlockSpec(memory_space=pltpu.VMEM)
    return pl.pallas_call(
        functools.partial(body, outer, inner, groups, tile, LOG2E * 3.0 / math.sqrt(width)),
        out_shape=[jax.ShapeDtypeStruct(*x) for x in out],
        in_specs=[pl.BlockSpec(memory_space=pltpu.SMEM)] + [vmem] * (3 + len(emb) + len(sums)),
        out_specs=[vmem] * len(out),
        scratch_shapes=scratch,
        compiler_params=pltpu.CompilerParams(vmem_limit_bytes=VMEM_LIMIT),
        cost_estimate=pl.CostEstimate(
            flops=(4 if sums else EARLY) * len(emb) * rows * k_dev * width,
            bytes_accessed=2 * (len(emb) * rows + 2 * k_dev) * width,
            transcendentals=len(emb) * rows * k_dev,
        ),
        name="columns_calc",
    )(place, lam, code, norm, *emb, *sums)


def combine_kernel(outer, inner, order, place_ref, lam_ref, *refs):
    parts, (soft_ref, own_ref, columns) = refs[:outer], refs[outer:]
    rows_dev, width = parts[0].shape
    rows, lanes = columns.shape
    place, spoke = place_ref[0] // inner, place_ref[0] % inner
    spot = pl.multiple_of(place * rows_dev, rows_dev)
    mine = read_lse(lam_ref, outer, inner, spoke)

    def own_rows(line):
        columns[...] = jnp.broadcast_to(line, (lanes, rows)).T
        return columns[pl.ds(spot, rows_dev), :]

    total = jnp.zeros((rows_dev, width), jnp.float32)
    for j, part in zip(order, parts):
        w = own_rows(jnp.exp(lam_ref[(place ^ j) * inner + spoke] - mine))
        w = jnp.concatenate([w] * (width // lanes), axis=1)
        total = total + w * part[...].astype(jnp.float32)
    soft_ref[...] = total.astype(jnp.bfloat16)
    own_ref[...] = own_rows(mine).T[:1, :]


def combine(place, lam, parts, order):
    outer = len(parts)
    inner = lam.shape[0] // outer
    rows_dev, width = parts[0].shape
    lanes = math.gcd(width, 128)
    vmem = pl.BlockSpec(memory_space=pltpu.VMEM)
    return pl.pallas_call(
        functools.partial(combine_kernel, outer, inner, order),
        out_shape=[
            jax.ShapeDtypeStruct((rows_dev, width), jnp.bfloat16),
            jax.ShapeDtypeStruct((1, rows_dev), jnp.float32),
        ],
        in_specs=[pl.BlockSpec(memory_space=pltpu.SMEM)] + [vmem] * (outer + 1),
        out_specs=[vmem] * 2,
        scratch_shapes=[pltpu.VMEM((outer * rows_dev, lanes), jnp.float32)],
        compiler_params=pltpu.CompilerParams(vmem_limit_bytes=VMEM_LIMIT),
        cost_estimate=pl.CostEstimate(
            flops=2 * outer * rows_dev * width,
            bytes_accessed=2 * outer * rows_dev * width,
            transcendentals=0,
        ),
        name="combine",
    )(place, lam, *parts)


def after(x, y):
    return lax.optimization_barrier((x, y))[0]


def on_device(size, embeddings, codebook):
    inner = 4
    outer = size // inner
    place = lax.axis_index(AXIS).astype(jnp.int32).reshape(1)

    def swap(x, step):
        return lax.ppermute(x, AXIS, [(i, i ^ step) for i in range(size)])

    code_y = swap(codebook, 2)
    code_c = swap(codebook, 1)
    emb = [swap(embeddings, inner * j) for j in range(1, outer)]
    shape = (outer * embeddings.shape[0], embeddings.shape[1])
    steps = (0,) + tuple(range(2, outer))
    far = stack(place, [keep(embeddings)] + emb[1:], steps, inner, shape)
    code_y, near, far = lax.optimization_barrier((code_y, emb[0], far))
    stacked = stack(place, [near], (1,), inner, shape, (far,))
    stacked_y = swap(stacked, 2)
    stacked_c = swap(stacked, 1)
    code = [codebook, code_c, code_y, swap(code_y, 1)]
    lam, parts = rows_calc(place, stacked, code, outer)

    order = (*range(2, outer), 1, 0)
    sent = [swap(parts[j], inner * j) for j in order[:-1]]
    lam = lax.all_to_all(lam, AXIS, 0, 0)
    norm = norm_calc(codebook, LOG2E * 3.0 / math.sqrt(codebook.shape[1]))
    stacked_yc = swap(stacked_y, 1)
    sums = columns_calc(
        place, lam, codebook, norm, (0, 1, 2), [stacked, stacked_c, stacked_y], inner
    )
    shift, occupancy = columns_calc(
        place, lam, codebook, norm, (3,), [stacked_yc], inner, sums
    )
    soft, own_lse = combine(place, lam, sent + [after(parts[0], occupancy)], order)
    return shift, occupancy.reshape(-1), soft, own_lse.reshape(-1)


def solution(mesh):
    specs = P(("groups", AXIS), None)
    flat = P(("groups", AXIS))
    return jax.shard_map(
        functools.partial(on_device, mesh.shape[AXIS]),
        mesh=mesh,
        in_specs=(specs, specs),
        out_specs=(specs, flat, specs, flat),
        check_vma=False,
    )
```

```python
import functools
import math

import jax
import jax.numpy as jnp
from jax import lax
from jax.experimental import pallas as pl
from jax.experimental.pallas import tpu as pltpu
from jax.sharding import PartitionSpec as P

AXIS = "blk"
LOG2E = math.log2(math.e)
LN2 = math.log(2.0)
VMEM_LIMIT = 20 * 1024 * 1024
EARLY = 64
STACK = 3 << 29


def nt_dot(a, b):
    return lax.dot_general(a, b, (((1,), (1,)), ((), ())), preferred_element_type=jnp.float32)


def norm_column(code, scale):
    c = code.astype(jnp.float32)
    return (0.5 * scale) * jnp.sum(c * c, axis=1, keepdims=True)


def tiles(rows, tile, body):
    count = rows // tile
    if count <= 4:
        for t in range(count):
            body(t * tile, t * tile)
    else:
        pl.loop(0, count)(lambda t: body(pl.multiple_of(t * tile, tile), 0))


def keep_kernel(x_ref, out_ref):
    out_ref[...] = x_ref[...]


def keep(x):
    vmem = pl.BlockSpec(memory_space=pltpu.VMEM)
    return pl.pallas_call(
        keep_kernel,
        out_shape=jax.ShapeDtypeStruct(x.shape, x.dtype),
        in_specs=[vmem],
        out_specs=vmem,
        compiler_params=pltpu.CompilerParams(vmem_limit_bytes=VMEM_LIMIT),
        cost_estimate=pl.CostEstimate(flops=0, bytes_accessed=4 * x.size, transcendentals=0),
        name="keep",
    )(x)


def stack_kernel(inner, steps, place_ref, *refs):
    blocks, out_ref = refs[: len(steps)], refs[-1]
    rows_dev = blocks[0].shape[0]
    place = place_ref[0] // inner
    for j, block in zip(steps, blocks):
        spot = pl.multiple_of((place ^ j) * rows_dev, rows_dev)
        out_ref[pl.ds(spot, rows_dev), :] = block[...]


def stack(place, blocks, steps, inner, shape, into=()):
    vmem = pl.BlockSpec(memory_space=pltpu.VMEM)
    return pl.pallas_call(
        functools.partial(stack_kernel, inner, steps),
        out_shape=jax.ShapeDtypeStruct(shape, blocks[0].dtype),
        in_specs=[pl.BlockSpec(memory_space=pltpu.SMEM)] + [vmem] * (len(blocks) + len(into)),
        out_specs=vmem,
        input_output_aliases={1 + len(blocks): 0} if into else {},
        compiler_params=pltpu.CompilerParams(vmem_limit_bytes=VMEM_LIMIT),
        cost_estimate=pl.CostEstimate(
            flops=0 if into else STACK, bytes_accessed=4 * shape[0] * shape[1], transcendentals=0
        ),
        name="stack",
    )(place, *blocks, *into)


def fold_lanes(op, x, lanes):
    parts = [x[:, i : i + lanes] for i in range(0, x.shape[1], lanes)]
    return functools.reduce(op, parts)


def rows_kernel(outer, inner, tile, scale, place_ref, stacked_ref, *refs):
    code = refs[:inner]
    lam_ref = refs[inner]
    parts = refs[inner + 1 : inner + 1 + outer]
    scores, total = refs[inner + 1 + outer :]
    rows, width = stacked_ref.shape
    rows_dev = rows // outer
    k_dev = code[0].shape[0]
    lanes = math.gcd(k_dev, 128)
    place = place_ref[0] // inner
    norms = [
        jnp.broadcast_to(norm_column(code[k][...], scale), (k_dev, lanes)).T[:1, :]
        for k in range(inner)
    ]

    def one_tile(start, slot):
        rows_here = stacked_ref[pl.ds(start, tile), :]
        top = None
        for k in range(inner):
            s = scale * nt_dot(rows_here, code[k][...]) - norms[k]
            scores[slot : slot + tile, k * k_dev : (k + 1) * k_dev] = s
            m = fold_lanes(jnp.maximum, s, lanes)
            top = m if top is None else jnp.maximum(top, m)
        top = jnp.max(top, axis=1, keepdims=True)
        mass = jnp.zeros((tile, lanes), jnp.float32)
        acc = jnp.zeros((tile, width), jnp.float32)
        for k in range(inner):
            p = jnp.exp2(scores[slot : slot + tile, k * k_dev : (k + 1) * k_dev] - top)
            mass = mass + fold_lanes(jnp.add, p, lanes)
            acc = acc + jnp.dot(
                p.astype(jnp.bfloat16), code[k][...], preferred_element_type=jnp.float32
            )
        mass = jnp.sum(mass, axis=1, keepdims=True)
        lam = jnp.broadcast_to(LN2 * (top + jnp.log2(mass)), (tile, lanes)).T[:1, :]
        lam_ref[:, :, pl.ds(start, tile)] = jnp.broadcast_to(
            lam.reshape(1, 1, tile), (lam_ref.shape[0], 1, tile)
        )
        total[pl.ds(start, tile), :] = (acc * (1.0 / mass)).astype(jnp.bfloat16)

    tiles(rows, tile, one_tile)
    for j in range(outer):
        spot = pl.multiple_of((place ^ j) * rows_dev, rows_dev)
        parts[j][...] = total[pl.ds(spot, rows_dev), :]


def rows_calc(place, stacked, code, outer):
    inner = len(code)
    rows, width = stacked.shape
    rows_dev = rows // outer
    entries = inner * code[0].shape[0]
    tile = math.gcd(rows, 256)
    vmem = pl.BlockSpec(memory_space=pltpu.VMEM)
    out = pl.pallas_call(
        functools.partial(rows_kernel, outer, inner, tile, LOG2E * 3.0 / math.sqrt(width)),
        out_shape=[jax.ShapeDtypeStruct((outer * inner, 1, rows), jnp.float32)]
        + [jax.ShapeDtypeStruct((rows_dev, width), jnp.bfloat16)] * outer,
        in_specs=[pl.BlockSpec(memory_space=pltpu.SMEM)] + [vmem] * (1 + inner),
        out_specs=[vmem] * (outer + 1),
        scratch_shapes=[
            pltpu.VMEM((min(rows, 4 * tile), entries), jnp.float32),
            pltpu.VMEM((rows, width), jnp.bfloat16),
        ],
        compiler_params=pltpu.CompilerParams(vmem_limit_bytes=VMEM_LIMIT),
        cost_estimate=pl.CostEstimate(
            flops=4 * rows * entries * width,
            bytes_accessed=2 * (rows + entries) * width,
            transcendentals=rows * entries,
        ),
        name="rows_calc",
    )(place, stacked, *code)
    return out[0], out[1:]


def norm_kernel(scale, code_ref, out_ref):
    out_ref[...] = jnp.broadcast_to(norm_column(code_ref[...], scale), out_ref.shape)


def norm_calc(code, scale):
    k_dev, width = code.shape
    lanes = math.gcd(width, 128)
    vmem = pl.BlockSpec(memory_space=pltpu.VMEM)
    return pl.pallas_call(
        functools.partial(norm_kernel, scale),
        out_shape=jax.ShapeDtypeStruct((k_dev, lanes), jnp.float32),
        in_specs=[vmem],
        out_specs=vmem,
        compiler_params=pltpu.CompilerParams(vmem_limit_bytes=VMEM_LIMIT),
        cost_estimate=pl.CostEstimate(
            flops=2 * k_dev * width, bytes_accessed=2 * k_dev * width, transcendentals=0
        ),
        name="norm_calc",
    )(code)


def read_lse(lam_ref, outer, inner, spoke):
    each = [lam_ref[z * inner + spoke] for z in range(outer)]
    top = functools.reduce(jnp.maximum, each)
    return top + jnp.log(sum(jnp.exp(x - top) for x in each))


def add_groups(groups, tile, scale, levels, code_ref, norm_ref, emb, weighted, folded):
    lanes = folded.shape[1]
    code = code_ref[...]
    norm = jnp.concatenate([norm_ref[...]] * (tile // lanes), axis=1)
    for g, emb_ref in zip(groups, emb):
        level = LOG2E * levels(g)
        for start in range(0, emb_ref.shape[0], tile):
            rows_here = emb_ref[start : start + tile, :]
            s = scale * nt_dot(code, rows_here) - norm
            shares = jnp.exp2(s - level[:, start : start + tile]).astype(jnp.bfloat16)
            wide = shares.astype(jnp.float32)
            part = folded[...]
            for i in range(tile // lanes):
                part = part + wide[:, i * lanes : (i + 1) * lanes]
            folded[...] = part
            weighted[...] += jnp.dot(shares, rows_here, preferred_element_type=jnp.float32)


def early_kernel(outer, inner, groups, tile, scale, place_ref, lam_ref, code_ref, norm_ref, *refs):
    emb = refs[: len(groups)]
    weighted, folded = refs[len(groups) :]
    spoke = place_ref[0] % inner
    weighted[...] = jnp.zeros_like(weighted)
    folded[...] = jnp.zeros_like(folded)
    levels = lambda g: read_lse(lam_ref, outer, inner, spoke ^ g)
    add_groups(groups, tile, scale, levels, code_ref, norm_ref, emb, weighted, folded)


def late_kernel(outer, inner, groups, tile, scale, place_ref, lam_ref, code_ref, norm_ref, *refs):
    emb = refs[: len(groups)]
    weighted_in, folded_in, shift_ref, occ_ref, weighted, folded = refs[len(groups) :]
    k_dev = code_ref.shape[0]
    rows_dev = emb[0].shape[0] // outer
    spoke = place_ref[0] % inner
    weighted[...] = weighted_in[...]
    folded[...] = folded_in[...]
    levels = lambda g: read_lse(lam_ref, outer, inner, spoke ^ g)
    add_groups(groups, tile, scale, levels, code_ref, norm_ref, emb, weighted, folded)
    masses = jnp.sum(folded[...], axis=1, keepdims=True)
    prior = rows_dev / k_dev
    shift_ref[...] = (
        (weighted[...] - masses * code_ref[...].astype(jnp.float32)) / (masses + prior)
    ).astype(jnp.bfloat16)
    spread = jnp.broadcast_to(masses * (k_dev / rows_dev), folded.shape).T
    occ_ref[...] = spread[:1, :]


def columns_calc(place, lam, code, norm, groups, emb, inner, sums=()):
    k_dev, width = code.shape
    rows = emb[0].shape[0]
    outer = lam.shape[0] // inner
    tile = math.gcd(rows, 768)
    lanes = norm.shape[1]
    totals = [((k_dev, width), jnp.float32), ((k_dev, lanes), jnp.float32)]
    if sums:
        body, out = late_kernel, [((k_dev, width), jnp.bfloat16), ((1, k_dev), jnp.float32)]
        scratch = [pltpu.VMEM(*x) for x in totals]
    else:
        body, out, scratch = early_kernel, totals, []
    vmem = pl.BlockSpec(memory_space=pltpu.VMEM)
    return pl.pallas_call(
        functools.partial(body, outer, inner, groups, tile, LOG2E * 3.0 / math.sqrt(width)),
        out_shape=[jax.ShapeDtypeStruct(*x) for x in out],
        in_specs=[pl.BlockSpec(memory_space=pltpu.SMEM)] + [vmem] * (3 + len(emb) + len(sums)),
        out_specs=[vmem] * len(out),
        scratch_shapes=scratch,
        compiler_params=pltpu.CompilerParams(vmem_limit_bytes=VMEM_LIMIT),
        cost_estimate=pl.CostEstimate(
            flops=(4 if sums else EARLY) * len(emb) * rows * k_dev * width,
            bytes_accessed=2 * (len(emb) * rows + 2 * k_dev) * width,
            transcendentals=len(emb) * rows * k_dev,
        ),
        name="columns_calc",
    )(place, lam, code, norm, *emb, *sums)


def combine_kernel(outer, inner, order, place_ref, lam_ref, *refs):
    parts, (soft_ref, own_ref) = refs[:outer], refs[outer:]
    rows_dev, width = parts[0].shape
    rows = lam_ref.shape[2]
    place, spoke = place_ref[0] // inner, place_ref[0] % inner
    mine = read_lse(lam_ref, outer, inner, spoke)
    lines = [jnp.exp(lam_ref[(place ^ j) * inner + spoke] - mine) for j in order] + [mine]
    lines += [mine] * (-len(lines) % 8)
    near = pltpu.roll(jnp.concatenate(lines, axis=0), rows - place * rows_dev, 1)
    near = near[:, : min(rows, -(-rows_dev // 128) * 128)]
    columns = near.T
    total = jnp.zeros((rows_dev, width), jnp.float32)
    for i, part in enumerate(parts):
        total = total + columns[:rows_dev, i : i + 1] * part[...].astype(jnp.float32)
    soft_ref[...] = total.astype(jnp.bfloat16)
    own_ref[...] = near[outer : outer + 1, :rows_dev]


def combine(place, lam, parts, order):
    outer = len(parts)
    inner = lam.shape[0] // outer
    rows_dev, width = parts[0].shape
    vmem = pl.BlockSpec(memory_space=pltpu.VMEM)
    return pl.pallas_call(
        functools.partial(combine_kernel, outer, inner, order),
        out_shape=[
            jax.ShapeDtypeStruct((rows_dev, width), jnp.bfloat16),
            jax.ShapeDtypeStruct((1, rows_dev), jnp.float32),
        ],
        in_specs=[pl.BlockSpec(memory_space=pltpu.SMEM)] + [vmem] * (outer + 1),
        out_specs=[vmem] * 2,
        compiler_params=pltpu.CompilerParams(vmem_limit_bytes=VMEM_LIMIT),
        cost_estimate=pl.CostEstimate(
            flops=2 * outer * rows_dev * width,
            bytes_accessed=2 * outer * rows_dev * width,
            transcendentals=0,
        ),
        name="combine",
    )(place, lam, *parts)


def after(x, y):
    return lax.optimization_barrier((x, y))[0]


def on_device(size, embeddings, codebook):
    inner = 4
    outer = size // inner
    place = lax.axis_index(AXIS).astype(jnp.int32).reshape(1)

    def swap(x, step):
        return lax.ppermute(x, AXIS, [(i, i ^ step) for i in range(size)])

    code_y = swap(codebook, 2)
    code_c = swap(codebook, 1)
    shape = (outer * embeddings.shape[0], embeddings.shape[1])
    steps = (*range(2, outer), 1, 0)
    stacked = stack(place, [keep(embeddings) if i == 0 else swap(embeddings, inner * i) for i in steps], steps, inner, shape)
    stacked_y = swap(stacked, 2)
    stacked_c = swap(stacked, 1)
    code = [codebook, code_c, code_y, swap(code_y, 1)]
    lam, parts = rows_calc(place, stacked, code, outer)

    order = (*range(2, outer), 1, 0)
    sent = [swap(parts[j], inner * j) for j in order[:-1]]
    lam = lax.all_to_all(lam, AXIS, 0, 0)
    norm = norm_calc(codebook, LOG2E * 3.0 / math.sqrt(codebook.shape[1]))
    stacked_yc = swap(stacked_y, 1)
    sums = columns_calc(
        place, lam, codebook, norm, (0, 1, 2), [stacked, stacked_c, stacked_y], inner
    )
    shift, occupancy = columns_calc(
        place, lam, codebook, norm, (3,), [stacked_yc], inner, sums
    )
    soft, own_lse = combine(place, lam, sent + [after(parts[0], occupancy)], order)
    return shift, occupancy.reshape(-1), soft, own_lse.reshape(-1)


def solution(mesh):
    specs = P(("groups", AXIS), None)
    flat = P(("groups", AXIS))
    return jax.shard_map(
        functools.partial(on_device, mesh.shape[AXIS]),
        mesh=mesh,
        in_specs=(specs, specs),
        out_specs=(specs, flat, specs, flat),
        check_vma=False,
    )
```

```python
import functools
import math

import jax
import jax.numpy as jnp
from jax import lax
from jax.experimental import pallas as pl
from jax.experimental.pallas import tpu as pltpu
from jax.sharding import PartitionSpec as P

AXIS = "blk"
LOG2E = math.log2(math.e)
LN2 = math.log(2.0)
VMEM_LIMIT = 20 * 1024 * 1024
EARLY = 64
STACK = 3 << 29


def nt_dot(a, b):
    return lax.dot_general(a, b, (((1,), (1,)), ((), ())), preferred_element_type=jnp.float32)


def norm_column(code, scale):
    c = code.astype(jnp.float32)
    return (0.5 * scale) * jnp.sum(c * c, axis=1, keepdims=True)


def keep_kernel(x_ref, out_ref):
    out_ref[...] = x_ref[...]


def keep(x):
    vmem = pl.BlockSpec(memory_space=pltpu.VMEM)
    return pl.pallas_call(
        keep_kernel,
        out_shape=jax.ShapeDtypeStruct(x.shape, x.dtype),
        in_specs=[vmem],
        out_specs=vmem,
        compiler_params=pltpu.CompilerParams(vmem_limit_bytes=VMEM_LIMIT),
        cost_estimate=pl.CostEstimate(flops=0, bytes_accessed=4 * x.size, transcendentals=0),
        name="keep",
    )(x)


def stack_kernel(inner, steps, place_ref, *refs):
    blocks, out_ref = refs[: len(steps)], refs[-1]
    rows_dev = blocks[0].shape[0]
    place = place_ref[0] // inner
    for j, block in zip(steps, blocks):
        spot = pl.multiple_of((place ^ j) * rows_dev, rows_dev)
        out_ref[pl.ds(spot, rows_dev), :] = block[...]


def stack(place, blocks, steps, inner, shape, into=()):
    vmem = pl.BlockSpec(memory_space=pltpu.VMEM)
    return pl.pallas_call(
        functools.partial(stack_kernel, inner, steps),
        out_shape=jax.ShapeDtypeStruct(shape, blocks[0].dtype),
        in_specs=[pl.BlockSpec(memory_space=pltpu.SMEM)] + [vmem] * (len(blocks) + len(into)),
        out_specs=vmem,
        input_output_aliases={1 + len(blocks): 0} if into else {},
        compiler_params=pltpu.CompilerParams(vmem_limit_bytes=VMEM_LIMIT),
        cost_estimate=pl.CostEstimate(
            flops=0 if into else STACK, bytes_accessed=4 * shape[0] * shape[1], transcendentals=0
        ),
        name="stack",
    )(place, *blocks, *into)


def fold_lanes(op, x, lanes):
    parts = [x[:, i : i + lanes] for i in range(0, x.shape[1], lanes)]
    return functools.reduce(op, parts)


def rows_kernel(outer, inner, tile, scale, place_ref, stacked_ref, *refs):
    code = refs[:inner]
    lam_ref = refs[inner]
    parts = refs[inner + 1 : inner + 1 + outer]
    scores, total = refs[inner + 1 + outer :]
    rows, width = stacked_ref.shape
    rows_dev = rows // outer
    k_dev = code[0].shape[0]
    lanes = math.gcd(k_dev, 128)
    place = place_ref[0] // inner
    norms = [
        jnp.broadcast_to(norm_column(code[k][...], scale), (k_dev, lanes)).T[:1, :]
        for k in range(inner)
    ]

    def first_half(start, slot):
        rows_here = stacked_ref[pl.ds(start, tile), :]
        top = None
        for k in range(inner):
            s = scale * nt_dot(rows_here, code[k][...]) - norms[k]
            scores[slot : slot + tile, k * k_dev : (k + 1) * k_dev] = s
            m = fold_lanes(jnp.maximum, s, lanes)
            top = m if top is None else jnp.maximum(top, m)
        return jnp.max(top, axis=1, keepdims=True)

    def second_half(start, slot, top):
        mass = jnp.zeros((tile, lanes), jnp.float32)
        acc = jnp.zeros((tile, width), jnp.float32)
        for k in range(inner):
            p = jnp.exp2(scores[slot : slot + tile, k * k_dev : (k + 1) * k_dev] - top)
            mass = mass + fold_lanes(jnp.add, p, lanes)
            acc = acc + jnp.dot(
                p.astype(jnp.bfloat16), code[k][...], preferred_element_type=jnp.float32
            )
        mass = jnp.sum(mass, axis=1, keepdims=True)
        lam = jnp.broadcast_to(LN2 * (top + jnp.log2(mass)), (tile, lanes)).T[:1, :]
        lam_ref[:, :, pl.ds(start, tile)] = jnp.broadcast_to(
            lam.reshape(1, 1, tile), (lam_ref.shape[0], 1, tile)
        )
        total[pl.ds(start, tile), :] = (acc * (1.0 / mass)).astype(jnp.bfloat16)

    count = rows // tile
    if count <= 4:
        top = first_half(0, 0)
        for t in range(count):
            here = top
            if t + 1 < count:
                top = first_half((t + 1) * tile, (t + 1) * tile)
            second_half(t * tile, t * tile, here)
    else:

        @pl.loop(0, count)
        def one_tile(t):
            start = pl.multiple_of(t * tile, tile)
            second_half(start, 0, first_half(start, 0))

    for j in range(outer):
        spot = pl.multiple_of((place ^ j) * rows_dev, rows_dev)
        parts[j][...] = total[pl.ds(spot, rows_dev), :]


def rows_calc(place, stacked, code, outer):
    inner = len(code)
    rows, width = stacked.shape
    rows_dev = rows // outer
    entries = inner * code[0].shape[0]
    tile = math.gcd(rows, 256)
    vmem = pl.BlockSpec(memory_space=pltpu.VMEM)
    out = pl.pallas_call(
        functools.partial(rows_kernel, outer, inner, tile, LOG2E * 3.0 / math.sqrt(width)),
        out_shape=[jax.ShapeDtypeStruct((outer * inner, 1, rows), jnp.float32)]
        + [jax.ShapeDtypeStruct((rows_dev, width), jnp.bfloat16)] * outer,
        in_specs=[pl.BlockSpec(memory_space=pltpu.SMEM)] + [vmem] * (1 + inner),
        out_specs=[vmem] * (outer + 1),
        scratch_shapes=[
            pltpu.VMEM((min(rows, 4 * tile), entries), jnp.float32),
            pltpu.VMEM((rows, width), jnp.bfloat16),
        ],
        compiler_params=pltpu.CompilerParams(vmem_limit_bytes=VMEM_LIMIT),
        cost_estimate=pl.CostEstimate(
            flops=4 * rows * entries * width,
            bytes_accessed=2 * (rows + entries) * width,
            transcendentals=rows * entries,
        ),
        name="rows_calc",
    )(place, stacked, *code)
    return out[0], out[1:]


def norm_kernel(scale, code_ref, out_ref):
    out_ref[...] = jnp.broadcast_to(norm_column(code_ref[...], scale), out_ref.shape)


def norm_calc(code, scale):
    k_dev, width = code.shape
    lanes = math.gcd(width, 128)
    vmem = pl.BlockSpec(memory_space=pltpu.VMEM)
    return pl.pallas_call(
        functools.partial(norm_kernel, scale),
        out_shape=jax.ShapeDtypeStruct((k_dev, lanes), jnp.float32),
        in_specs=[vmem],
        out_specs=vmem,
        compiler_params=pltpu.CompilerParams(vmem_limit_bytes=VMEM_LIMIT),
        cost_estimate=pl.CostEstimate(
            flops=2 * k_dev * width, bytes_accessed=2 * k_dev * width, transcendentals=0
        ),
        name="norm_calc",
    )(code)


def read_lse(lam_ref, outer, inner, spoke):
    each = [lam_ref[z * inner + spoke] for z in range(outer)]
    top = functools.reduce(jnp.maximum, each)
    return top + jnp.log(sum(jnp.exp(x - top) for x in each))


def add_groups(groups, tile, scale, levels, code_ref, norm_ref, emb, weighted, folded):
    lanes = folded.shape[1]
    code = code_ref[...]
    norm = jnp.concatenate([norm_ref[...]] * (tile // lanes), axis=1)
    for g, emb_ref in zip(groups, emb):
        level = LOG2E * levels(g)
        for start in range(0, emb_ref.shape[0], tile):
            rows_here = emb_ref[start : start + tile, :]
            s = scale * nt_dot(code, rows_here) - norm
            shares = jnp.exp2(s - level[:, start : start + tile]).astype(jnp.bfloat16)
            wide = shares.astype(jnp.float32)
            part = folded[...]
            for i in range(tile // lanes):
                part = part + wide[:, i * lanes : (i + 1) * lanes]
            folded[...] = part
            weighted[...] += jnp.dot(shares, rows_here, preferred_element_type=jnp.float32)


def early_kernel(outer, inner, groups, tile, scale, place_ref, lam_ref, code_ref, norm_ref, *refs):
    emb = refs[: len(groups)]
    weighted, folded = refs[len(groups) :]
    spoke = place_ref[0] % inner
    weighted[...] = jnp.zeros_like(weighted)
    folded[...] = jnp.zeros_like(folded)
    levels = lambda g: read_lse(lam_ref, outer, inner, spoke ^ g)
    add_groups(groups, tile, scale, levels, code_ref, norm_ref, emb, weighted, folded)


def late_kernel(outer, inner, groups, tile, scale, place_ref, lam_ref, code_ref, norm_ref, *refs):
    emb = refs[: len(groups)]
    weighted_in, folded_in, shift_ref, occ_ref, weighted, folded = refs[len(groups) :]
    k_dev = code_ref.shape[0]
    rows_dev = emb[0].shape[0] // outer
    spoke = place_ref[0] % inner
    weighted[...] = weighted_in[...]
    folded[...] = folded_in[...]
    levels = lambda g: read_lse(lam_ref, outer, inner, spoke ^ g)
    add_groups(groups, tile, scale, levels, code_ref, norm_ref, emb, weighted, folded)
    masses = jnp.sum(folded[...], axis=1, keepdims=True)
    share = 1.0 / (masses + rows_dev / k_dev)
    shift_ref[...] = (
        (weighted[...] - masses * code_ref[...].astype(jnp.float32)) * share
    ).astype(jnp.bfloat16)
    spread = jnp.broadcast_to(masses * (k_dev / rows_dev), folded.shape).T
    occ_ref[...] = spread[:1, :]


def columns_calc(place, lam, code, norm, groups, emb, inner, sums=()):
    k_dev, width = code.shape
    rows = emb[0].shape[0]
    outer = lam.shape[0] // inner
    tile = math.gcd(rows, 768)
    lanes = norm.shape[1]
    totals = [((k_dev, width), jnp.float32), ((k_dev, lanes), jnp.float32)]
    if sums:
        body, out = late_kernel, [((k_dev, width), jnp.bfloat16), ((1, k_dev), jnp.float32)]
        scratch = [pltpu.VMEM(*x) for x in totals]
    else:
        body, out, scratch = early_kernel, totals, []
    vmem = pl.BlockSpec(memory_space=pltpu.VMEM)
    return pl.pallas_call(
        functools.partial(body, outer, inner, groups, tile, LOG2E * 3.0 / math.sqrt(width)),
        out_shape=[jax.ShapeDtypeStruct(*x) for x in out],
        in_specs=[pl.BlockSpec(memory_space=pltpu.SMEM)] + [vmem] * (3 + len(emb) + len(sums)),
        out_specs=[vmem] * len(out),
        scratch_shapes=scratch,
        compiler_params=pltpu.CompilerParams(vmem_limit_bytes=VMEM_LIMIT),
        cost_estimate=pl.CostEstimate(
            flops=(4 if sums else EARLY) * len(emb) * rows * k_dev * width,
            bytes_accessed=2 * (len(emb) * rows + 2 * k_dev) * width,
            transcendentals=len(emb) * rows * k_dev,
        ),
        name="columns_calc",
    )(place, lam, code, norm, *emb, *sums)


def combine_kernel(outer, inner, order, place_ref, lam_ref, *refs):
    parts, (soft_ref, own_ref) = refs[:outer], refs[outer:]
    rows_dev, width = parts[0].shape
    rows = lam_ref.shape[2]
    place, spoke = place_ref[0] // inner, place_ref[0] % inner
    mine = read_lse(lam_ref, outer, inner, spoke)
    lines = [jnp.exp(lam_ref[(place ^ j) * inner + spoke] - mine) for j in order] + [mine]
    lines += [mine] * (-len(lines) % 8)
    near = pltpu.roll(jnp.concatenate(lines, axis=0), rows - place * rows_dev, 1)
    near = near[:, : min(rows, -(-rows_dev // 128) * 128)]
    columns = near.T
    total = jnp.zeros((rows_dev, width), jnp.float32)
    for i, part in enumerate(parts):
        total = total + columns[:rows_dev, i : i + 1] * part[...].astype(jnp.float32)
    soft_ref[...] = total.astype(jnp.bfloat16)
    own_ref[...] = near[outer : outer + 1, :rows_dev]


def combine(place, lam, parts, order):
    outer = len(parts)
    inner = lam.shape[0] // outer
    rows_dev, width = parts[0].shape
    vmem = pl.BlockSpec(memory_space=pltpu.VMEM)
    return pl.pallas_call(
        functools.partial(combine_kernel, outer, inner, order),
        out_shape=[
            jax.ShapeDtypeStruct((rows_dev, width), jnp.bfloat16),
            jax.ShapeDtypeStruct((1, rows_dev), jnp.float32),
        ],
        in_specs=[pl.BlockSpec(memory_space=pltpu.SMEM)] + [vmem] * (outer + 1),
        out_specs=[vmem] * 2,
        compiler_params=pltpu.CompilerParams(vmem_limit_bytes=VMEM_LIMIT),
        cost_estimate=pl.CostEstimate(
            flops=2 * outer * rows_dev * width,
            bytes_accessed=2 * outer * rows_dev * width,
            transcendentals=0,
        ),
        name="combine",
    )(place, lam, *parts)


def after(x, y):
    return lax.optimization_barrier((x, y))[0]


def on_device(size, embeddings, codebook):
    inner = 4
    outer = size // inner
    place = lax.axis_index(AXIS).astype(jnp.int32).reshape(1)

    def swap(x, step):
        return lax.ppermute(x, AXIS, [(i, i ^ step) for i in range(size)])

    code_y = swap(codebook, 2)
    code_c = swap(codebook, 1)
    shape = (outer * embeddings.shape[0], embeddings.shape[1])
    steps = (*range(2, outer), 1, 0)
    stacked = stack(place, [keep(embeddings) if i == 0 else swap(embeddings, inner * i) for i in steps], steps, inner, shape)
    stacked_y = swap(stacked, 2)
    stacked_c = swap(stacked, 1)
    code = [codebook, code_c, code_y, swap(code_y, 1)]
    lam, parts = rows_calc(place, stacked, code, outer)

    order = (*range(2, outer), 1, 0)
    sent = [swap(parts[j], inner * j) for j in order[:-1]]
    lam = after(lax.all_to_all(lam, AXIS, 0, 0), sent[0])
    norm = norm_calc(codebook, LOG2E * 3.0 / math.sqrt(codebook.shape[1]))
    stacked_yc = swap(stacked_y, 1)
    sums = columns_calc(
        place, lam, codebook, norm, (0, 1, 2), [stacked, stacked_c, stacked_y], inner
    )
    shift, occupancy = columns_calc(
        place, lam, codebook, norm, (3,), [stacked_yc], inner, sums
    )
    soft, own_lse = combine(place, lam, sent + [after(parts[0], occupancy)], order)
    return shift, occupancy.reshape(-1), soft, own_lse.reshape(-1)


def solution(mesh):
    specs = P(("groups", AXIS), None)
    flat = P(("groups", AXIS))
    return jax.shard_map(
        functools.partial(on_device, mesh.shape[AXIS]),
        mesh=mesh,
        in_specs=(specs, specs),
        out_specs=(specs, flat, specs, flat),
        check_vma=False,
    )
```

```python
import functools
import math

import jax
import jax.numpy as jnp
from jax import lax
from jax.experimental import pallas as pl
from jax.experimental.pallas import tpu as pltpu
from jax.sharding import PartitionSpec as P

AXIS = "blk"
LOG2E = math.log2(math.e)
LN2 = math.log(2.0)
VMEM_LIMIT = 20 * 1024 * 1024
EARLY = 64
STACK = 3 << 29


def nt_dot(a, b):
    return lax.dot_general(a, b, (((1,), (1,)), ((), ())), preferred_element_type=jnp.float32)


def norm_column(code, scale):
    c = code.astype(jnp.float32)
    return (0.5 * scale) * jnp.sum(c * c, axis=1, keepdims=True)


def keep_kernel(*refs):
    half = len(refs) // 2
    for x_ref, out_ref in zip(refs[:half], refs[half:]):
        out_ref[...] = x_ref[...]


def keep(*arrays):
    vmem = pl.BlockSpec(memory_space=pltpu.VMEM)
    return pl.pallas_call(
        keep_kernel,
        out_shape=[jax.ShapeDtypeStruct(x.shape, x.dtype) for x in arrays],
        in_specs=[vmem] * len(arrays),
        out_specs=[vmem] * len(arrays),
        compiler_params=pltpu.CompilerParams(vmem_limit_bytes=VMEM_LIMIT),
        cost_estimate=pl.CostEstimate(
            flops=0, bytes_accessed=4 * sum(x.size for x in arrays), transcendentals=0
        ),
        name="keep",
    )(*arrays)


def stack_kernel(inner, steps, place_ref, *refs):
    blocks, out_ref = refs[: len(steps)], refs[-1]
    rows_dev = blocks[0].shape[0]
    place = place_ref[0] // inner
    for j, block in zip(steps, blocks):
        spot = pl.multiple_of((place ^ j) * rows_dev, rows_dev)
        out_ref[pl.ds(spot, rows_dev), :] = block[...]


def stack(place, blocks, steps, inner, shape):
    vmem = pl.BlockSpec(memory_space=pltpu.VMEM)
    return pl.pallas_call(
        functools.partial(stack_kernel, inner, steps),
        out_shape=jax.ShapeDtypeStruct(shape, blocks[0].dtype),
        in_specs=[pl.BlockSpec(memory_space=pltpu.SMEM)] + [vmem] * len(blocks),
        out_specs=vmem,
        compiler_params=pltpu.CompilerParams(vmem_limit_bytes=VMEM_LIMIT),
        cost_estimate=pl.CostEstimate(
            flops=STACK, bytes_accessed=4 * shape[0] * shape[1], transcendentals=0
        ),
        name="stack",
    )(place, *blocks)


def fold_lanes(op, x, lanes):
    parts = [x[:, i : i + lanes] for i in range(0, x.shape[1], lanes)]
    return functools.reduce(op, parts)


def rows_kernel(outer, inner, tile, scale, place_ref, stacked_ref, *refs):
    code = refs[:inner]
    lam_ref = refs[inner]
    parts = refs[inner + 1 : inner + 1 + outer]
    scores, total = refs[inner + 1 + outer :]
    rows, width = stacked_ref.shape
    rows_dev = rows // outer
    k_dev = code[0].shape[0]
    lanes = math.gcd(k_dev, 128)
    place = place_ref[0] // inner
    norms = [
        jnp.broadcast_to(norm_column(code[k][...], scale), (k_dev, lanes)).T[:1, :]
        for k in range(inner)
    ]

    def first_half(start, slot):
        rows_here = stacked_ref[pl.ds(start, tile), :]
        top = None
        for k in range(inner):
            s = scale * nt_dot(rows_here, code[k][...]) - norms[k]
            scores[slot : slot + tile, k * k_dev : (k + 1) * k_dev] = s
            m = fold_lanes(jnp.maximum, s, lanes)
            top = m if top is None else jnp.maximum(top, m)
        return jnp.max(top, axis=1, keepdims=True)

    def second_half(start, slot, top):
        mass = jnp.zeros((tile, lanes), jnp.float32)
        acc = jnp.zeros((tile, width), jnp.float32)
        for k in range(inner):
            p = jnp.exp2(scores[slot : slot + tile, k * k_dev : (k + 1) * k_dev] - top)
            mass = mass + fold_lanes(jnp.add, p, lanes)
            acc = acc + jnp.dot(
                p.astype(jnp.bfloat16), code[k][...], preferred_element_type=jnp.float32
            )
        mass = jnp.sum(mass, axis=1, keepdims=True)
        lam = jnp.broadcast_to(LN2 * (top + jnp.log2(mass)), (tile, lanes)).T[:1, :]
        lam_ref[:, :, pl.ds(start, tile)] = jnp.broadcast_to(
            lam.reshape(1, 1, tile), (lam_ref.shape[0], 1, tile)
        )
        total[pl.ds(start, tile), :] = (acc * (1.0 / mass)).astype(jnp.bfloat16)

    count = rows // tile
    if count <= 4:
        top = first_half(0, 0)
        for t in range(count):
            here = top
            if t + 1 < count:
                top = first_half((t + 1) * tile, (t + 1) * tile)
            second_half(t * tile, t * tile, here)
    else:

        @pl.loop(0, count)
        def one_tile(t):
            start = pl.multiple_of(t * tile, tile)
            second_half(start, 0, first_half(start, 0))

    for j in range(outer):
        spot = pl.multiple_of((place ^ j) * rows_dev, rows_dev)
        parts[j][...] = total[pl.ds(spot, rows_dev), :]


def rows_calc(place, stacked, code, outer):
    inner = len(code)
    rows, width = stacked.shape
    rows_dev = rows // outer
    entries = inner * code[0].shape[0]
    tile = math.gcd(rows, 256)
    vmem = pl.BlockSpec(memory_space=pltpu.VMEM)
    out = pl.pallas_call(
        functools.partial(rows_kernel, outer, inner, tile, LOG2E * 3.0 / math.sqrt(width)),
        out_shape=[jax.ShapeDtypeStruct((outer * inner, 1, rows), jnp.float32)]
        + [jax.ShapeDtypeStruct((rows_dev, width), jnp.bfloat16)] * outer,
        in_specs=[pl.BlockSpec(memory_space=pltpu.SMEM)] + [vmem] * (1 + inner),
        out_specs=[vmem] * (outer + 1),
        scratch_shapes=[
            pltpu.VMEM((min(rows, 4 * tile), entries), jnp.float32),
            pltpu.VMEM((rows, width), jnp.bfloat16),
        ],
        compiler_params=pltpu.CompilerParams(vmem_limit_bytes=VMEM_LIMIT),
        cost_estimate=pl.CostEstimate(
            flops=4 * rows * entries * width,
            bytes_accessed=2 * (rows + entries) * width,
            transcendentals=rows * entries,
        ),
        name="rows_calc",
    )(place, stacked, *code)
    return out[0], out[1:]


def norm_kernel(scale, code_ref, out_ref):
    out_ref[...] = jnp.broadcast_to(norm_column(code_ref[...], scale), out_ref.shape)


def norm_calc(code, scale):
    k_dev, width = code.shape
    lanes = math.gcd(width, 128)
    vmem = pl.BlockSpec(memory_space=pltpu.VMEM)
    return pl.pallas_call(
        functools.partial(norm_kernel, scale),
        out_shape=jax.ShapeDtypeStruct((k_dev, lanes), jnp.float32),
        in_specs=[vmem],
        out_specs=vmem,
        compiler_params=pltpu.CompilerParams(vmem_limit_bytes=VMEM_LIMIT),
        cost_estimate=pl.CostEstimate(
            flops=2 * k_dev * width, bytes_accessed=2 * k_dev * width, transcendentals=0
        ),
        name="norm_calc",
    )(code)


def read_lse(lam_ref, outer, inner, spoke):
    each = [lam_ref[z * inner + spoke] for z in range(outer)]
    top = functools.reduce(jnp.maximum, each)
    return top + jnp.log(sum(jnp.exp(x - top) for x in each))


def add_groups(groups, tile, scale, levels, code_ref, norm_ref, emb, weighted, folded):
    lanes = folded.shape[1]
    code = code_ref[...]
    norm = jnp.concatenate([norm_ref[...]] * (tile // lanes), axis=1)
    for g, emb_ref in zip(groups, emb):
        level = LOG2E * levels(g)
        for start in range(0, emb_ref.shape[0], tile):
            rows_here = emb_ref[start : start + tile, :]
            s = scale * nt_dot(code, rows_here) - norm
            shares = jnp.exp2(s - level[:, start : start + tile]).astype(jnp.bfloat16)
            wide = shares.astype(jnp.float32)
            part = folded[...]
            for i in range(tile // lanes):
                part = part + wide[:, i * lanes : (i + 1) * lanes]
            folded[...] = part
            weighted[...] += jnp.dot(shares, rows_here, preferred_element_type=jnp.float32)


def early_kernel(outer, inner, groups, tile, scale, order, place_ref, lam_ref, code_ref, norm_ref, *refs):
    emb = refs[: len(groups)]
    weighted, folded = refs[len(groups) :]
    spoke = place_ref[0] % inner
    weighted[...] = jnp.zeros_like(weighted)
    folded[...] = jnp.zeros_like(folded)
    levels = lambda g: read_lse(lam_ref, outer, inner, spoke ^ g)
    add_groups(groups, tile, scale, levels, code_ref, norm_ref, emb, weighted, folded)


def late_kernel(outer, inner, groups, tile, scale, order, place_ref, lam_ref, code_ref, norm_ref, *refs):
    emb, refs = refs[: len(groups)], refs[len(groups) :]
    weighted_in, folded_in, parts, refs = refs[0], refs[1], refs[2 : 2 + outer], refs[2 + outer :]
    shift_ref, occ_ref, soft_ref, own_ref, weighted, folded = refs
    k_dev = code_ref.shape[0]
    rows_dev, width = parts[0].shape
    rows = lam_ref.shape[2]
    place, spoke = place_ref[0] // inner, place_ref[0] % inner
    weighted[...] = weighted_in[...]
    folded[...] = folded_in[...]
    levels = lambda g: read_lse(lam_ref, outer, inner, spoke ^ g)
    add_groups(groups, tile, scale, levels, code_ref, norm_ref, emb, weighted, folded)
    masses = jnp.sum(folded[...], axis=1, keepdims=True)
    share = 1.0 / (masses + rows_dev / k_dev)
    shift_ref[...] = (
        (weighted[...] - masses * code_ref[...].astype(jnp.float32)) * share
    ).astype(jnp.bfloat16)
    spread = jnp.broadcast_to(masses * (k_dev / rows_dev), folded.shape).T
    occ_ref[...] = spread[:1, :]

    mine = levels(0)
    lines = [jnp.exp(lam_ref[(place ^ j) * inner + spoke] - mine) for j in order] + [mine]
    lines += [mine] * (-len(lines) % 8)
    near = pltpu.roll(jnp.concatenate(lines, axis=0), rows - place * rows_dev, 1)
    near = near[:, : min(rows, -(-rows_dev // 128) * 128)]
    columns = near.T
    total = jnp.zeros((rows_dev, width), jnp.float32)
    for i, part in enumerate(parts):
        total = total + columns[:rows_dev, i : i + 1] * part[...].astype(jnp.float32)
    soft_ref[...] = total.astype(jnp.bfloat16)
    own_ref[...] = near[outer : outer + 1, :rows_dev]


def columns_calc(place, lam, code, norm, groups, emb, inner, sums=(), parts=(), order=()):
    k_dev, width = code.shape
    rows = emb[0].shape[0]
    outer = lam.shape[0] // inner
    tile = math.gcd(rows, 768)
    lanes = norm.shape[1]
    totals = [((k_dev, width), jnp.float32), ((k_dev, lanes), jnp.float32)]
    if sums:
        body = late_kernel
        rows_dev = parts[0].shape[0]
        out = [
            ((k_dev, width), jnp.bfloat16),
            ((1, k_dev), jnp.float32),
            ((rows_dev, width), jnp.bfloat16),
            ((1, rows_dev), jnp.float32),
        ]
        scratch = [pltpu.VMEM(*x) for x in totals]
    else:
        body, out, scratch = early_kernel, totals, []
    vmem = pl.BlockSpec(memory_space=pltpu.VMEM)
    return pl.pallas_call(
        functools.partial(
            body, outer, inner, groups, tile, LOG2E * 3.0 / math.sqrt(width), order
        ),
        out_shape=[jax.ShapeDtypeStruct(*x) for x in out],
        in_specs=[pl.BlockSpec(memory_space=pltpu.SMEM)]
        + [vmem] * (3 + len(emb) + len(sums) + len(parts)),
        out_specs=[vmem] * len(out),
        scratch_shapes=scratch,
        compiler_params=pltpu.CompilerParams(vmem_limit_bytes=VMEM_LIMIT),
        cost_estimate=pl.CostEstimate(
            flops=(4 if sums else EARLY) * len(emb) * rows * k_dev * width,
            bytes_accessed=2 * (len(emb) * rows + 2 * k_dev) * width,
            transcendentals=len(emb) * rows * k_dev,
        ),
        name="columns_calc",
    )(place, lam, code, norm, *emb, *sums, *parts)


def after(x, y):
    return lax.optimization_barrier((x, y))[0]


def on_device(size, embeddings, codebook):
    inner = 4
    outer = size // inner
    place = lax.axis_index(AXIS).astype(jnp.int32).reshape(1)

    def swap(x, step):
        return lax.ppermute(x, AXIS, [(i, i ^ step) for i in range(size)])

    code_y = swap(codebook, 2)
    code_c = swap(codebook, 1)
    shape = (outer * embeddings.shape[0], embeddings.shape[1])
    order = (*range(2, outer), 1, 0)
    own_rows, own_code = keep(embeddings, codebook)
    blocks = [swap(embeddings, inner * j) for j in order[:-1]] + [own_rows]
    stacked = stack(place, blocks, order, inner, shape)
    stacked_y = swap(stacked, 2)
    stacked_c = swap(stacked, 1)
    code = [own_code, code_c, code_y, swap(code_y, 1)]
    lam, parts = rows_calc(place, stacked, code, outer)

    sent = [swap(parts[j], inner * j) for j in order[:-1]]
    lam = lax.all_to_all(lam, AXIS, 0, 0)
    for part in sent[: outer - 2]:
        lam = after(lam, part)
    norm = norm_calc(own_code, LOG2E * 3.0 / math.sqrt(codebook.shape[1]))
    stacked_yc = swap(stacked_y, 1)
    sums = columns_calc(
        place, lam, own_code, norm, (0, 1, 2), [stacked, stacked_c, stacked_y], inner
    )
    shift, occupancy, soft, own_lse = columns_calc(
        place, lam, own_code, norm, (3,), [stacked_yc], inner, sums, sent + [parts[0]], order
    )
    return shift, occupancy.reshape(-1), soft, own_lse.reshape(-1)


def solution(mesh):
    specs = P(("groups", AXIS), None)
    flat = P(("groups", AXIS))
    return jax.shard_map(
        functools.partial(on_device, mesh.shape[AXIS]),
        mesh=mesh,
        in_specs=(specs, specs),
        out_specs=(specs, flat, specs, flat),
        check_vma=False,
    )
```

```python
import functools
import math

import jax
import jax.numpy as jnp
from jax import lax
from jax.experimental import pallas as pl
from jax.experimental.pallas import tpu as pltpu
from jax.sharding import PartitionSpec as P

AXIS = "blk"
LOG2E = math.log2(math.e)
LN2 = math.log(2.0)
VMEM_LIMIT = 20 * 1024 * 1024
EARLY = 64
STACK = 3 << 29


def nt_dot(a, b):
    return lax.dot_general(a, b, (((1,), (1,)), ((), ())), preferred_element_type=jnp.float32)


def norm_column(code, scale):
    c = code.astype(jnp.float32)
    return (0.5 * scale) * jnp.sum(c * c, axis=1, keepdims=True)


def keep_kernel(*refs):
    half = len(refs) // 2
    for x_ref, out_ref in zip(refs[:half], refs[half:]):
        out_ref[...] = x_ref[...]


def keep(*arrays):
    vmem = pl.BlockSpec(memory_space=pltpu.VMEM)
    return pl.pallas_call(
        keep_kernel,
        out_shape=[jax.ShapeDtypeStruct(x.shape, x.dtype) for x in arrays],
        in_specs=[vmem] * len(arrays),
        out_specs=[vmem] * len(arrays),
        compiler_params=pltpu.CompilerParams(vmem_limit_bytes=VMEM_LIMIT),
        cost_estimate=pl.CostEstimate(
            flops=0, bytes_accessed=4 * sum(x.size for x in arrays), transcendentals=0
        ),
        name="keep",
    )(*arrays)


def stack_kernel(inner, steps, place_ref, *refs):
    blocks, out_ref = refs[: len(steps)], refs[-1]
    rows_dev = blocks[0].shape[0]
    place = place_ref[0] // inner
    for j, block in zip(steps, blocks):
        spot = pl.multiple_of((place ^ j) * rows_dev, rows_dev)
        out_ref[pl.ds(spot, rows_dev), :] = block[...]


def stack(place, blocks, steps, inner, shape):
    vmem = pl.BlockSpec(memory_space=pltpu.VMEM)
    return pl.pallas_call(
        functools.partial(stack_kernel, inner, steps),
        out_shape=jax.ShapeDtypeStruct(shape, blocks[0].dtype),
        in_specs=[pl.BlockSpec(memory_space=pltpu.SMEM)] + [vmem] * len(blocks),
        out_specs=vmem,
        compiler_params=pltpu.CompilerParams(vmem_limit_bytes=VMEM_LIMIT),
        cost_estimate=pl.CostEstimate(
            flops=STACK, bytes_accessed=4 * shape[0] * shape[1], transcendentals=0
        ),
        name="stack",
    )(place, *blocks)


def fold_lanes(op, x, lanes):
    parts = [x[:, i : i + lanes] for i in range(0, x.shape[1], lanes)]
    return functools.reduce(op, parts)


def rows_tiles(scale, rows_ref, offset, code, norms, scores, total, put):
    count_rows, width = total.shape
    lanes = math.gcd(code[0].shape[0], 128)
    k_dev = code[0].shape[0]
    tile = math.gcd(count_rows, 384)
    inner = len(code)

    def first_half(start, slot):
        rows_here = rows_ref[pl.ds(pl.multiple_of(offset + start, tile), tile), :]
        top = None
        for k in range(inner):
            s = scale * nt_dot(rows_here, code[k][...]) - norms[k]
            scores[slot : slot + tile, k * k_dev : (k + 1) * k_dev] = s
            m = fold_lanes(jnp.maximum, s, lanes)
            top = m if top is None else jnp.maximum(top, m)
        return jnp.max(top, axis=1, keepdims=True)

    def second_half(start, slot, top):
        mass = jnp.zeros((tile, lanes), jnp.float32)
        acc = jnp.zeros((tile, width), jnp.float32)
        for k in range(inner):
            p = jnp.exp2(scores[slot : slot + tile, k * k_dev : (k + 1) * k_dev] - top)
            mass = mass + fold_lanes(jnp.add, p, lanes)
            acc = acc + jnp.dot(
                p.astype(jnp.bfloat16), code[k][...], preferred_element_type=jnp.float32
            )
        mass = jnp.sum(mass, axis=1, keepdims=True)
        put(start, tile, jnp.broadcast_to(LN2 * (top + jnp.log2(mass)), (tile, lanes)).T[:1, :])
        total[pl.ds(start, tile), :] = (acc * (1.0 / mass)).astype(jnp.bfloat16)

    if count_rows == tile:
        second_half(0, 0, first_half(0, 0))
    else:

        @pl.loop(0, count_rows // tile)
        def one_tile(t):
            start = pl.multiple_of(t * tile, tile)
            second_half(start, 0, first_half(start, 0))


def near_kernel(half, inner, scale, place_ref, *refs):
    blocks, code, refs = refs[:half], refs[half : half + inner], refs[half + inner :]
    lam_ref, norm_ref, parts, (rows_ref, scores, total) = refs[0], refs[1], refs[2:-3], refs[-3:]
    rows_dev = blocks[0].shape[0]
    k_dev = code[0].shape[0]
    lanes = math.gcd(k_dev, 128)
    place = place_ref[0] // inner

    def spot(j):
        return pl.ds(pl.multiple_of(((place ^ j) % half) * rows_dev, rows_dev), rows_dev)

    for j, block in enumerate(blocks):
        rows_ref[spot(j), :] = block[...]
    norms = []
    for k in range(inner):
        column = norm_column(code[k][...], scale)
        norms.append(jnp.broadcast_to(column, (k_dev, lanes)).T[:1, :])
        norm_ref[:, k * k_dev : (k + 1) * k_dev] = norms[k]

    def put(start, tile, lam):
        lam_ref[:, pl.ds(start, tile)] = lam

    rows_tiles(scale, rows_ref, 0, code, norms, scores, total, put)
    for j in range(half):
        parts[j][...] = total[spot(j), :]


def far_kernel(half, inner, scale, place_ref, rows_ref, near_ref, norm_ref, *refs):
    code, refs = refs[:inner], refs[inner:]
    lam_ref, parts, (scores, total) = refs[0], refs[1:-2], refs[-2:]
    k_dev = code[0].shape[0]
    count, rows_dev = lam_ref.shape[0], parts[0].shape[0]
    span = half * rows_dev
    place = place_ref[0] // inner
    side = place // half
    near, far = side * span, (1 - side) * span
    norms = [norm_ref[:, k * k_dev : (k + 1) * k_dev] for k in range(inner)]
    step = math.gcd(span, 128)
    lam_ref[:, :, pl.ds(pl.multiple_of(near, step), span)] = jnp.broadcast_to(
        near_ref[...].reshape(1, 1, span), (count, 1, span)
    )

    def put(start, tile, lam):
        lam_ref[:, :, pl.ds(pl.multiple_of(far + start, step), tile)] = jnp.broadcast_to(
            lam.reshape(1, 1, tile), (count, 1, tile)
        )

    rows_tiles(scale, rows_ref, far, code, norms, scores, total, put)
    for j in range(half):
        spot = pl.multiple_of(((place ^ j) % half) * rows_dev, rows_dev)
        parts[j][...] = total[pl.ds(spot, rows_dev), :]


def rows_call(body, half, code, shape, out, scratch, operands, name):
    rows_dev, width = shape
    span = half * rows_dev
    entries = len(code) * code[0].shape[0]
    vmem = pl.BlockSpec(memory_space=pltpu.VMEM)
    return pl.pallas_call(
        functools.partial(body, half, len(code), LOG2E * 3.0 / math.sqrt(width)),
        out_shape=out + [jax.ShapeDtypeStruct(shape, jnp.bfloat16)] * half,
        in_specs=[pl.BlockSpec(memory_space=pltpu.SMEM)] + [vmem] * (len(operands) - 1),
        out_specs=[vmem] * (len(out) + half),
        scratch_shapes=scratch
        + [
            pltpu.VMEM((math.gcd(span, 384), entries), jnp.float32),
            pltpu.VMEM((span, width), jnp.bfloat16),
        ],
        compiler_params=pltpu.CompilerParams(vmem_limit_bytes=VMEM_LIMIT),
        cost_estimate=pl.CostEstimate(
            flops=4 * span * entries * width,
            bytes_accessed=2 * (span + entries) * width,
            transcendentals=span * entries,
        ),
        name=name,
    )(*operands)


def near_rows(place, blocks, code):
    half, shape = len(blocks), blocks[0].shape
    span = half * shape[0]
    entries = len(code) * code[0].shape[0]
    out = [
        jax.ShapeDtypeStruct((1, span), jnp.float32),
        jax.ShapeDtypeStruct((1, entries), jnp.float32),
    ]
    scratch = [pltpu.VMEM((span, shape[1]), jnp.bfloat16)]
    operands = [place, *blocks, *code]
    got = rows_call(near_kernel, half, code, shape, out, scratch, operands, "near_rows")
    return got[0], got[1], got[2:]


def far_rows(place, stacked, near, norms, code, half):
    rows, width = stacked.shape
    shape = (rows // (2 * half), width)
    out = [jax.ShapeDtypeStruct((2 * half * len(code), 1, rows), jnp.float32)]
    operands = [place, stacked, near, norms, *code]
    got = rows_call(far_kernel, half, code, shape, out, [], operands, "far_rows")
    return got[0], got[1:]


def norm_kernel(scale, code_ref, out_ref):
    out_ref[...] = jnp.broadcast_to(norm_column(code_ref[...], scale), out_ref.shape)


def norm_calc(code, scale):
    k_dev, width = code.shape
    lanes = math.gcd(width, 128)
    vmem = pl.BlockSpec(memory_space=pltpu.VMEM)
    return pl.pallas_call(
        functools.partial(norm_kernel, scale),
        out_shape=jax.ShapeDtypeStruct((k_dev, lanes), jnp.float32),
        in_specs=[vmem],
        out_specs=vmem,
        compiler_params=pltpu.CompilerParams(vmem_limit_bytes=VMEM_LIMIT),
        cost_estimate=pl.CostEstimate(
            flops=2 * k_dev * width, bytes_accessed=2 * k_dev * width, transcendentals=0
        ),
        name="norm_calc",
    )(code)


def read_lse(lam_ref, outer, inner, spoke):
    each = [lam_ref[z * inner + spoke] for z in range(outer)]
    top = functools.reduce(jnp.maximum, each)
    return top + jnp.log(sum(jnp.exp(x - top) for x in each))


def add_groups(groups, tile, scale, levels, code_ref, norm_ref, emb, weighted, folded):
    lanes = folded.shape[1]
    code = code_ref[...]
    norm = jnp.concatenate([norm_ref[...]] * (tile // lanes), axis=1)
    for g, emb_ref in zip(groups, emb):
        level = LOG2E * levels(g)
        for start in range(0, emb_ref.shape[0], tile):
            rows_here = emb_ref[start : start + tile, :]
            s = scale * nt_dot(code, rows_here) - norm
            shares = jnp.exp2(s - level[:, start : start + tile]).astype(jnp.bfloat16)
            wide = shares.astype(jnp.float32)
            part = folded[...]
            for i in range(tile // lanes):
                part = part + wide[:, i * lanes : (i + 1) * lanes]
            folded[...] = part
            weighted[...] += jnp.dot(shares, rows_here, preferred_element_type=jnp.float32)


def early_kernel(outer, inner, groups, tile, scale, order, place_ref, lam_ref, code_ref, norm_ref, *refs):
    emb = refs[: len(groups)]
    weighted, folded = refs[len(groups) :]
    spoke = place_ref[0] % inner
    weighted[...] = jnp.zeros_like(weighted)
    folded[...] = jnp.zeros_like(folded)
    levels = lambda g: read_lse(lam_ref, outer, inner, spoke ^ g)
    add_groups(groups, tile, scale, levels, code_ref, norm_ref, emb, weighted, folded)


def late_kernel(outer, inner, groups, tile, scale, order, place_ref, lam_ref, code_ref, norm_ref, *refs):
    emb, refs = refs[: len(groups)], refs[len(groups) :]
    weighted_in, folded_in, shift_ref, occ_ref, weight_ref, own_ref, weighted, folded = refs
    k_dev = code_ref.shape[0]
    rows = lam_ref.shape[2]
    rows_dev = rows // outer
    place, spoke = place_ref[0] // inner, place_ref[0] % inner
    weighted[...] = weighted_in[...]
    folded[...] = folded_in[...]
    levels = lambda g: read_lse(lam_ref, outer, inner, spoke ^ g)
    add_groups(groups, tile, scale, levels, code_ref, norm_ref, emb, weighted, folded)
    masses = jnp.sum(folded[...], axis=1, keepdims=True)
    share = 1.0 / (masses + rows_dev / k_dev)
    shift_ref[...] = (
        (weighted[...] - masses * code_ref[...].astype(jnp.float32)) * share
    ).astype(jnp.bfloat16)
    spread = jnp.broadcast_to(masses * (k_dev / rows_dev), folded.shape).T
    occ_ref[...] = spread[:1, :]

    mine = levels(0)
    lines = [jnp.exp(lam_ref[(place ^ j) * inner + spoke] - mine) for j in order] + [mine]
    lines += [mine] * (-len(lines) % 8)
    near = pltpu.roll(jnp.concatenate(lines, axis=0), rows - place * rows_dev, 1)
    near = near[:, : min(rows, -(-rows_dev // 128) * 128)]
    weight_ref[...] = near.T[:rows_dev, :]
    own_ref[...] = near[outer : outer + 1, :rows_dev]


def soft_kernel(weight_ref, *refs):
    parts, soft_ref = refs[:-1], refs[-1]
    total = jnp.zeros(soft_ref.shape, jnp.float32)
    for i, part in enumerate(parts):
        total = total + weight_ref[:, i : i + 1] * part[...].astype(jnp.float32)
    soft_ref[...] = total.astype(jnp.bfloat16)


def soft_calc(weights, parts):
    vmem = pl.BlockSpec(memory_space=pltpu.VMEM)
    shape = parts[0].shape
    return pl.pallas_call(
        soft_kernel,
        out_shape=jax.ShapeDtypeStruct(shape, jnp.bfloat16),
        in_specs=[vmem] * (1 + len(parts)),
        out_specs=vmem,
        compiler_params=pltpu.CompilerParams(vmem_limit_bytes=VMEM_LIMIT),
        cost_estimate=pl.CostEstimate(
            flops=2 * len(parts) * shape[0] * shape[1],
            bytes_accessed=2 * (1 + len(parts)) * shape[0] * shape[1],
            transcendentals=0,
        ),
        name="soft_calc",
    )(weights, *parts)


def columns_calc(place, lam, code, norm, groups, emb, inner, sums=(), order=()):
    k_dev, width = code.shape
    rows = emb[0].shape[0]
    outer = lam.shape[0] // inner
    tile = math.gcd(rows, 768)
    lanes = norm.shape[1]
    totals = [((k_dev, width), jnp.float32), ((k_dev, lanes), jnp.float32)]
    if sums:
        body = late_kernel
        rows_dev = rows // outer
        out = [
            ((k_dev, width), jnp.bfloat16),
            ((1, k_dev), jnp.float32),
            ((rows_dev, -(-(outer + 1) // 8) * 8), jnp.float32),
            ((1, rows_dev), jnp.float32),
        ]
        scratch = [pltpu.VMEM(*x) for x in totals]
    else:
        body, out, scratch = early_kernel, totals, []
    vmem = pl.BlockSpec(memory_space=pltpu.VMEM)
    return pl.pallas_call(
        functools.partial(
            body, outer, inner, groups, tile, LOG2E * 3.0 / math.sqrt(width), order
        ),
        out_shape=[jax.ShapeDtypeStruct(*x) for x in out],
        in_specs=[pl.BlockSpec(memory_space=pltpu.SMEM)]
        + [vmem] * (3 + len(emb) + len(sums)),
        out_specs=[vmem] * len(out),
        scratch_shapes=scratch,
        compiler_params=pltpu.CompilerParams(vmem_limit_bytes=VMEM_LIMIT),
        cost_estimate=pl.CostEstimate(
            flops=(4 if sums else EARLY) * len(emb) * rows * k_dev * width,
            bytes_accessed=2 * (len(emb) * rows + 2 * k_dev) * width,
            transcendentals=len(emb) * rows * k_dev,
        ),
        name="columns_calc",
    )(place, lam, code, norm, *emb, *sums)


def after(x, y):
    return lax.optimization_barrier((x, y))[0]


def on_device(size, embeddings, codebook):
    inner = 4
    outer = size // inner
    place = lax.axis_index(AXIS).astype(jnp.int32).reshape(1)

    def swap(x, step):
        return lax.ppermute(x, AXIS, [(i, i ^ step) for i in range(size)])

    code_y = swap(codebook, 2)
    code_c = swap(codebook, 1)
    shape = (outer * embeddings.shape[0], embeddings.shape[1])
    half = outer // 2
    order = (*range(half, outer), *range(1, half), 0)
    own_rows, own_code = keep(embeddings, codebook)
    arrived = {0: own_rows}
    step = outer // 2
    first = swap(embeddings, inner * step)
    for j in range(1, half):
        arrived[j] = swap(embeddings, inner * j)
    waits = [arrived[j] for j in range(1, half)] + [first]
    code_y, *waits = lax.optimization_barrier((code_y, *waits))
    arrived.update({j + 1: w for j, w in enumerate(waits[:-1])})
    arrived[step] = waits[-1]
    for j in range(1, half):
        arrived[step + j] = swap(arrived[step], inner * j)
    code = [own_code, code_c, code_y, swap(code_y, 1)]
    near, norms, near_parts = near_rows(place, [arrived[j] for j in range(half)], code)
    arrived[0] = after(own_rows, near)
    stacked = stack(place, [arrived[j] for j in order], order, inner, shape)
    stacked_y = swap(stacked, 2)
    stacked_c = swap(stacked, 1)
    lam, far_parts = far_rows(place, stacked, near, norms, code, half)
    parts = [*near_parts, *far_parts]

    sent = [swap(parts[j], inner * j) for j in order[:-1]]
    lam = lax.all_to_all(lam, AXIS, 0, 0)
    lam = after(lam, sent[0])
    norm = norm_calc(own_code, LOG2E * 3.0 / math.sqrt(codebook.shape[1]))
    stacked_yc = swap(stacked_y, 1)
    sums = columns_calc(
        place, lam, own_code, norm, (0, 1, 2), [stacked, stacked_c, stacked_y], inner
    )
    shift, occupancy, weights, own_lse = columns_calc(
        place, lam, own_code, norm, (3,), [stacked_yc], inner, sums, order
    )
    soft = soft_calc(weights, [*sent, parts[0]])
    return shift, occupancy.reshape(-1), soft, own_lse.reshape(-1)


def solution(mesh):
    specs = P(("groups", AXIS), None)
    flat = P(("groups", AXIS))
    return jax.shard_map(
        functools.partial(on_device, mesh.shape[AXIS]),
        mesh=mesh,
        in_specs=(specs, specs),
        out_specs=(specs, flat, specs, flat),
        check_vma=False,
    )
```

```python
import functools
import math

import jax
import jax.numpy as jnp
from jax import lax
from jax.experimental import pallas as pl
from jax.experimental.pallas import tpu as pltpu
from jax.sharding import PartitionSpec as P

AXIS = "blk"
LOG2E = math.log2(math.e)
LN2 = math.log(2.0)
VMEM_LIMIT = 20 * 1024 * 1024
EARLY = 64
STACK = 3 << 29


def nt_dot(a, b):
    return lax.dot_general(a, b, (((1,), (1,)), ((), ())), preferred_element_type=jnp.float32)


def norm_column(code, scale):
    c = code.astype(jnp.float32)
    return (0.5 * scale) * jnp.sum(c * c, axis=1, keepdims=True)


def keep_kernel(*refs):
    half = len(refs) // 2
    for x_ref, out_ref in zip(refs[:half], refs[half:]):
        out_ref[...] = x_ref[...]


def keep(*arrays):
    vmem = pl.BlockSpec(memory_space=pltpu.VMEM)
    return pl.pallas_call(
        keep_kernel,
        out_shape=[jax.ShapeDtypeStruct(x.shape, x.dtype) for x in arrays],
        in_specs=[vmem] * len(arrays),
        out_specs=[vmem] * len(arrays),
        compiler_params=pltpu.CompilerParams(vmem_limit_bytes=VMEM_LIMIT),
        cost_estimate=pl.CostEstimate(
            flops=0, bytes_accessed=4 * sum(x.size for x in arrays), transcendentals=0
        ),
        name="keep",
    )(*arrays)


def stack_kernel(inner, steps, place_ref, *refs):
    blocks, out_ref = refs[: len(steps)], refs[-1]
    rows_dev = blocks[0].shape[0]
    place = place_ref[0] // inner
    for j, block in zip(steps, blocks):
        spot = pl.multiple_of((place ^ j) * rows_dev, rows_dev)
        out_ref[pl.ds(spot, rows_dev), :] = block[...]


def stack(place, blocks, steps, inner, shape):
    vmem = pl.BlockSpec(memory_space=pltpu.VMEM)
    return pl.pallas_call(
        functools.partial(stack_kernel, inner, steps),
        out_shape=jax.ShapeDtypeStruct(shape, blocks[0].dtype),
        in_specs=[pl.BlockSpec(memory_space=pltpu.SMEM)] + [vmem] * len(blocks),
        out_specs=vmem,
        compiler_params=pltpu.CompilerParams(vmem_limit_bytes=VMEM_LIMIT),
        cost_estimate=pl.CostEstimate(
            flops=STACK, bytes_accessed=4 * shape[0] * shape[1], transcendentals=0
        ),
        name="stack",
    )(place, *blocks)


def fold_lanes(op, x, lanes):
    parts = [x[:, i : i + lanes] for i in range(0, x.shape[1], lanes)]
    return functools.reduce(op, parts)


def rows_kernel(outer, inner, tile, scale, place_ref, stacked_ref, *refs):
    code = refs[:inner]
    lam_ref = refs[inner]
    parts = refs[inner + 1 : inner + 1 + outer]
    scores, total = refs[inner + 1 + outer :]
    rows, width = stacked_ref.shape
    rows_dev = rows // outer
    k_dev = code[0].shape[0]
    lanes = math.gcd(k_dev, 128)
    place = place_ref[0] // inner
    norms = [
        jnp.broadcast_to(norm_column(code[k][...], scale), (k_dev, lanes)).T[:1, :]
        for k in range(inner)
    ]

    def first_half(start, slot):
        rows_here = stacked_ref[pl.ds(start, tile), :]
        top = None
        for k in range(inner):
            s = scale * nt_dot(rows_here, code[k][...]) - norms[k]
            scores[slot : slot + tile, k * k_dev : (k + 1) * k_dev] = s
            m = fold_lanes(jnp.maximum, s, lanes)
            top = m if top is None else jnp.maximum(top, m)
        return jnp.max(top, axis=1, keepdims=True)

    def second_half(start, slot, top):
        mass = jnp.zeros((tile, lanes), jnp.float32)
        acc = jnp.zeros((tile, width), jnp.float32)
        for k in range(inner):
            p = jnp.exp2(scores[slot : slot + tile, k * k_dev : (k + 1) * k_dev] - top)
            mass = mass + fold_lanes(jnp.add, p, lanes)
            acc = acc + jnp.dot(
                p.astype(jnp.bfloat16), code[k][...], preferred_element_type=jnp.float32
            )
        mass = jnp.sum(mass, axis=1, keepdims=True)
        lam = jnp.broadcast_to(LN2 * (top + jnp.log2(mass)), (tile, lanes)).T[:1, :]
        lam_ref[:, :, pl.ds(start, tile)] = jnp.broadcast_to(
            lam.reshape(1, 1, tile), (lam_ref.shape[0], 1, tile)
        )
        total[pl.ds(start, tile), :] = (acc * (1.0 / mass)).astype(jnp.bfloat16)

    count = rows // tile
    if count <= 4:
        top = first_half(0, 0)
        for t in range(count):
            here = top
            if t + 1 < count:
                top = first_half((t + 1) * tile, (t + 1) * tile)
            second_half(t * tile, t * tile, here)
    else:

        @pl.loop(0, count)
        def one_tile(t):
            start = pl.multiple_of(t * tile, tile)
            second_half(start, 0, first_half(start, 0))

    for j in range(outer):
        spot = pl.multiple_of((place ^ j) * rows_dev, rows_dev)
        parts[j][...] = total[pl.ds(spot, rows_dev), :]


def rows_calc(place, stacked, code, outer):
    inner = len(code)
    rows, width = stacked.shape
    rows_dev = rows // outer
    entries = inner * code[0].shape[0]
    tile = math.gcd(rows, 256)
    vmem = pl.BlockSpec(memory_space=pltpu.VMEM)
    out = pl.pallas_call(
        functools.partial(rows_kernel, outer, inner, tile, LOG2E * 3.0 / math.sqrt(width)),
        out_shape=[jax.ShapeDtypeStruct((outer * inner, 1, rows), jnp.float32)]
        + [jax.ShapeDtypeStruct((rows_dev, width), jnp.bfloat16)] * outer,
        in_specs=[pl.BlockSpec(memory_space=pltpu.SMEM)] + [vmem] * (1 + inner),
        out_specs=[vmem] * (outer + 1),
        scratch_shapes=[
            pltpu.VMEM((min(rows, 4 * tile), entries), jnp.float32),
            pltpu.VMEM((rows, width), jnp.bfloat16),
        ],
        compiler_params=pltpu.CompilerParams(vmem_limit_bytes=VMEM_LIMIT),
        cost_estimate=pl.CostEstimate(
            flops=4 * rows * entries * width,
            bytes_accessed=2 * (rows + entries) * width,
            transcendentals=rows * entries,
        ),
        name="rows_calc",
    )(place, stacked, *code)
    return out[0], out[1:]


def norm_kernel(scale, code_ref, out_ref):
    out_ref[...] = jnp.broadcast_to(norm_column(code_ref[...], scale), out_ref.shape)


def norm_calc(code, scale):
    k_dev, width = code.shape
    lanes = math.gcd(width, 128)
    vmem = pl.BlockSpec(memory_space=pltpu.VMEM)
    return pl.pallas_call(
        functools.partial(norm_kernel, scale),
        out_shape=jax.ShapeDtypeStruct((k_dev, lanes), jnp.float32),
        in_specs=[vmem],
        out_specs=vmem,
        compiler_params=pltpu.CompilerParams(vmem_limit_bytes=VMEM_LIMIT),
        cost_estimate=pl.CostEstimate(
            flops=2 * k_dev * width, bytes_accessed=2 * k_dev * width, transcendentals=0
        ),
        name="norm_calc",
    )(code)


def read_lse(lam_ref, outer, inner, spoke):
    each = [lam_ref[z * inner + spoke] for z in range(outer)]
    top = functools.reduce(jnp.maximum, each)
    return top + jnp.log(sum(jnp.exp(x - top) for x in each))


def add_groups(groups, tile, scale, levels, code_ref, norm_ref, emb, weighted, folded):
    lanes = folded.shape[1]
    code = code_ref[...]
    norm = jnp.concatenate([norm_ref[...]] * (tile // lanes), axis=1)
    for g, emb_ref in zip(groups, emb):
        level = LOG2E * levels(g)
        for start in range(0, emb_ref.shape[0], tile):
            rows_here = emb_ref[start : start + tile, :]
            s = scale * nt_dot(code, rows_here) - norm
            shares = jnp.exp2(s - level[:, start : start + tile]).astype(jnp.bfloat16)
            wide = shares.astype(jnp.float32)
            part = folded[...]
            for i in range(tile // lanes):
                part = part + wide[:, i * lanes : (i + 1) * lanes]
            folded[...] = part
            weighted[...] += jnp.dot(shares, rows_here, preferred_element_type=jnp.float32)


def early_kernel(outer, inner, groups, tile, scale, order, place_ref, lam_ref, code_ref, norm_ref, *refs):
    emb = refs[: len(groups)]
    weighted, folded = refs[len(groups) :]
    spoke = place_ref[0] % inner
    weighted[...] = jnp.zeros_like(weighted)
    folded[...] = jnp.zeros_like(folded)
    levels = lambda g: read_lse(lam_ref, outer, inner, spoke ^ g)
    add_groups(groups, tile, scale, levels, code_ref, norm_ref, emb, weighted, folded)


def late_kernel(outer, inner, groups, tile, scale, order, place_ref, lam_ref, code_ref, norm_ref, *refs):
    emb, refs = refs[: len(groups)], refs[len(groups) :]
    weighted_in, folded_in, shift_ref, occ_ref, weight_ref, own_ref, weighted, folded = refs
    k_dev = code_ref.shape[0]
    rows = lam_ref.shape[2]
    rows_dev = rows // outer
    place, spoke = place_ref[0] // inner, place_ref[0] % inner
    weighted[...] = weighted_in[...]
    folded[...] = folded_in[...]
    levels = lambda g: read_lse(lam_ref, outer, inner, spoke ^ g)
    add_groups(groups, tile, scale, levels, code_ref, norm_ref, emb, weighted, folded)
    masses = jnp.sum(folded[...], axis=1, keepdims=True)
    share = 1.0 / (masses + rows_dev / k_dev)
    shift_ref[...] = (
        (weighted[...] - masses * code_ref[...].astype(jnp.float32)) * share
    ).astype(jnp.bfloat16)
    spread = jnp.broadcast_to(masses * (k_dev / rows_dev), folded.shape).T
    occ_ref[...] = spread[:1, :]

    mine = levels(0)
    lines = [jnp.exp(lam_ref[(place ^ j) * inner + spoke] - mine) for j in order] + [mine]
    lines += [mine] * (-len(lines) % 8)
    near = pltpu.roll(jnp.concatenate(lines, axis=0), rows - place * rows_dev, 1)
    near = near[:, : min(rows, -(-rows_dev // 128) * 128)]
    weight_ref[...] = near.T[:rows_dev, :]
    own_ref[...] = near[outer : outer + 1, :rows_dev]


def soft_kernel(weight_ref, *refs):
    parts, soft_ref = refs[:-1], refs[-1]
    total = jnp.zeros(soft_ref.shape, jnp.float32)
    for i, part in enumerate(parts):
        total = total + weight_ref[:, i : i + 1] * part[...].astype(jnp.float32)
    soft_ref[...] = total.astype(jnp.bfloat16)


def soft_calc(weights, parts):
    vmem = pl.BlockSpec(memory_space=pltpu.VMEM)
    shape = parts[0].shape
    return pl.pallas_call(
        soft_kernel,
        out_shape=jax.ShapeDtypeStruct(shape, jnp.bfloat16),
        in_specs=[vmem] * (1 + len(parts)),
        out_specs=vmem,
        compiler_params=pltpu.CompilerParams(vmem_limit_bytes=VMEM_LIMIT),
        cost_estimate=pl.CostEstimate(
            flops=2 * len(parts) * shape[0] * shape[1],
            bytes_accessed=2 * (1 + len(parts)) * shape[0] * shape[1],
            transcendentals=0,
        ),
        name="soft_calc",
    )(weights, *parts)


def columns_calc(place, lam, code, norm, groups, emb, inner, sums=(), order=()):
    k_dev, width = code.shape
    rows = emb[0].shape[0]
    outer = lam.shape[0] // inner
    tile = math.gcd(rows, 768)
    lanes = norm.shape[1]
    totals = [((k_dev, width), jnp.float32), ((k_dev, lanes), jnp.float32)]
    if sums:
        body = late_kernel
        rows_dev = rows // outer
        out = [
            ((k_dev, width), jnp.bfloat16),
            ((1, k_dev), jnp.float32),
            ((rows_dev, -(-(outer + 1) // 8) * 8), jnp.float32),
            ((1, rows_dev), jnp.float32),
        ]
        scratch = [pltpu.VMEM(*x) for x in totals]
    else:
        body, out, scratch = early_kernel, totals, []
    vmem = pl.BlockSpec(memory_space=pltpu.VMEM)
    return pl.pallas_call(
        functools.partial(
            body, outer, inner, groups, tile, LOG2E * 3.0 / math.sqrt(width), order
        ),
        out_shape=[jax.ShapeDtypeStruct(*x) for x in out],
        in_specs=[pl.BlockSpec(memory_space=pltpu.SMEM)]
        + [vmem] * (3 + len(emb) + len(sums)),
        out_specs=[vmem] * len(out),
        scratch_shapes=scratch,
        compiler_params=pltpu.CompilerParams(vmem_limit_bytes=VMEM_LIMIT),
        cost_estimate=pl.CostEstimate(
            flops=(4 if sums else EARLY) * len(emb) * rows * k_dev * width,
            bytes_accessed=2 * (len(emb) * rows + 2 * k_dev) * width,
            transcendentals=len(emb) * rows * k_dev,
        ),
        name="columns_calc",
    )(place, lam, code, norm, *emb, *sums)


def after(x, y):
    return lax.optimization_barrier((x, y))[0]


def on_device(size, embeddings, codebook):
    inner = 4
    outer = size // inner
    place = lax.axis_index(AXIS).astype(jnp.int32).reshape(1)

    def swap(x, step):
        return lax.ppermute(x, AXIS, [(i, i ^ step) for i in range(size)])

    code_y = swap(codebook, 2)
    code_c = swap(codebook, 1)
    shape = (outer * embeddings.shape[0], embeddings.shape[1])
    order = (*range(2, outer), 1, 0)
    own_rows, own_code = keep(embeddings, codebook)
    blocks = [swap(embeddings, inner * j) for j in order[:-1]] + [own_rows]
    stacked = stack(place, blocks, order, inner, shape)
    stacked_y = swap(stacked, 2)
    stacked_c = swap(stacked, 1)
    code = [own_code, code_c, code_y, swap(code_y, 1)]
    lam, parts = rows_calc(place, stacked, code, outer)

    sent = [swap(parts[j], inner * j) for j in order[:-1]]
    lam = lax.all_to_all(lam, AXIS, 0, 0)
    lam = after(lam, sent[0])
    norm = norm_calc(own_code, LOG2E * 3.0 / math.sqrt(codebook.shape[1]))
    stacked_yc = swap(stacked_y, 1)
    sums = columns_calc(
        place, lam, own_code, norm, (0, 1, 2), [stacked, stacked_c, stacked_y], inner
    )
    shift, occupancy, weights, own_lse = columns_calc(
        place, lam, own_code, norm, (3,), [stacked_yc], inner, sums, order
    )
    soft = soft_calc(weights, [*sent, parts[0]])
    return shift, occupancy.reshape(-1), soft, own_lse.reshape(-1)


def solution(mesh):
    specs = P(("groups", AXIS), None)
    flat = P(("groups", AXIS))
    return jax.shard_map(
        functools.partial(on_device, mesh.shape[AXIS]),
        mesh=mesh,
        in_specs=(specs, specs),
        out_specs=(specs, flat, specs, flat),
        check_vma=False,
    )
```

```python
import functools
import math

import jax
import jax.numpy as jnp
from jax import lax
from jax.experimental import pallas as pl
from jax.experimental.pallas import tpu as pltpu
from jax.sharding import PartitionSpec as P

AXIS = "blk"
LOG2E = math.log2(math.e)
LN2 = math.log(2.0)
VMEM_LIMIT = 20 * 1024 * 1024
EARLY = 64
STACK = 3 << 29


def nt_dot(a, b):
    return lax.dot_general(a, b, (((1,), (1,)), ((), ())), preferred_element_type=jnp.float32)


def norm_column(code, scale):
    c = code.astype(jnp.float32)
    return (0.5 * scale) * jnp.sum(c * c, axis=1, keepdims=True)


def keep_kernel(*refs):
    half = len(refs) // 2
    for x_ref, out_ref in zip(refs[:half], refs[half:]):
        out_ref[...] = x_ref[...]


def keep(*arrays):
    vmem = pl.BlockSpec(memory_space=pltpu.VMEM)
    return pl.pallas_call(
        keep_kernel,
        out_shape=[jax.ShapeDtypeStruct(x.shape, x.dtype) for x in arrays],
        in_specs=[vmem] * len(arrays),
        out_specs=[vmem] * len(arrays),
        compiler_params=pltpu.CompilerParams(vmem_limit_bytes=VMEM_LIMIT),
        cost_estimate=pl.CostEstimate(
            flops=0, bytes_accessed=4 * sum(x.size for x in arrays), transcendentals=0
        ),
        name="keep",
    )(*arrays)


def stack_kernel(inner, steps, place_ref, *refs):
    blocks, out_ref = refs[: len(steps)], refs[-1]
    rows_dev = blocks[0].shape[0]
    place = place_ref[0] // inner
    for j, block in zip(steps, blocks):
        spot = pl.multiple_of((place ^ j) * rows_dev, rows_dev)
        out_ref[pl.ds(spot, rows_dev), :] = block[...]


def stack(place, blocks, steps, inner, shape):
    vmem = pl.BlockSpec(memory_space=pltpu.VMEM)
    return pl.pallas_call(
        functools.partial(stack_kernel, inner, steps),
        out_shape=jax.ShapeDtypeStruct(shape, blocks[0].dtype),
        in_specs=[pl.BlockSpec(memory_space=pltpu.SMEM)] + [vmem] * len(blocks),
        out_specs=vmem,
        compiler_params=pltpu.CompilerParams(vmem_limit_bytes=VMEM_LIMIT),
        cost_estimate=pl.CostEstimate(
            flops=STACK, bytes_accessed=4 * shape[0] * shape[1], transcendentals=0
        ),
        name="stack",
    )(place, *blocks)


def fold_lanes(op, x, lanes):
    parts = [x[:, i : i + lanes] for i in range(0, x.shape[1], lanes)]
    return functools.reduce(op, parts)


def rows_kernel(outer, inner, tile, scale, place_ref, stacked_ref, *refs):
    code = refs[:inner]
    lam_ref = refs[inner]
    parts = refs[inner + 1 : inner + 1 + outer]
    scores, total = refs[inner + 1 + outer :]
    rows, width = stacked_ref.shape
    rows_dev = rows // outer
    k_dev = code[0].shape[0]
    lanes = math.gcd(k_dev, 128)
    place = place_ref[0] // inner
    norms = [
        jnp.broadcast_to(norm_column(code[k][...], scale), (k_dev, lanes)).T[:1, :]
        for k in range(inner)
    ]

    def first_half(start, slot):
        rows_here = stacked_ref[pl.ds(start, tile), :]
        top = None
        for k in range(inner):
            s = scale * nt_dot(rows_here, code[k][...]) - norms[k]
            scores[slot : slot + tile, k * k_dev : (k + 1) * k_dev] = s
            m = fold_lanes(jnp.maximum, s, lanes)
            top = m if top is None else jnp.maximum(top, m)
        return jnp.max(top, axis=1, keepdims=True)

    def second_half(start, slot, top):
        mass = jnp.zeros((tile, lanes), jnp.float32)
        acc = jnp.zeros((tile, width), jnp.float32)
        for k in range(inner):
            p = jnp.exp2(scores[slot : slot + tile, k * k_dev : (k + 1) * k_dev] - top)
            mass = mass + fold_lanes(jnp.add, p, lanes)
            acc = acc + jnp.dot(
                p.astype(jnp.bfloat16), code[k][...], preferred_element_type=jnp.float32
            )
        mass = jnp.sum(mass, axis=1, keepdims=True)
        lam = jnp.broadcast_to(LN2 * (top + jnp.log2(mass)), (tile, lanes)).T[:1, :]
        lam_ref[:, :, pl.ds(start, tile)] = jnp.broadcast_to(
            lam.reshape(1, 1, tile), (lam_ref.shape[0], 1, tile)
        )
        total[pl.ds(start, tile), :] = (acc * (1.0 / mass)).astype(jnp.bfloat16)

    count = rows // tile
    if count <= 4:
        top = first_half(0, 0)
        for t in range(count):
            here = top
            if t + 1 < count:
                top = first_half((t + 1) * tile, (t + 1) * tile)
            second_half(t * tile, t * tile, here)
    else:

        @pl.loop(0, count)
        def one_tile(t):
            start = pl.multiple_of(t * tile, tile)
            second_half(start, 0, first_half(start, 0))

    for j in range(outer):
        spot = pl.multiple_of((place ^ j) * rows_dev, rows_dev)
        parts[j][...] = total[pl.ds(spot, rows_dev), :]


def rows_calc(place, stacked, code, outer):
    inner = len(code)
    rows, width = stacked.shape
    rows_dev = rows // outer
    entries = inner * code[0].shape[0]
    tile = math.gcd(rows, 256)
    vmem = pl.BlockSpec(memory_space=pltpu.VMEM)
    out = pl.pallas_call(
        functools.partial(rows_kernel, outer, inner, tile, LOG2E * 3.0 / math.sqrt(width)),
        out_shape=[jax.ShapeDtypeStruct((outer * inner, 1, rows), jnp.float32)]
        + [jax.ShapeDtypeStruct((rows_dev, width), jnp.bfloat16)] * outer,
        in_specs=[pl.BlockSpec(memory_space=pltpu.SMEM)] + [vmem] * (1 + inner),
        out_specs=[vmem] * (outer + 1),
        scratch_shapes=[
            pltpu.VMEM((min(rows, 4 * tile), entries), jnp.float32),
            pltpu.VMEM((rows, width), jnp.bfloat16),
        ],
        compiler_params=pltpu.CompilerParams(vmem_limit_bytes=VMEM_LIMIT),
        cost_estimate=pl.CostEstimate(
            flops=4 * rows * entries * width,
            bytes_accessed=2 * (rows + entries) * width,
            transcendentals=rows * entries,
        ),
        name="rows_calc",
    )(place, stacked, *code)
    return out[0], out[1:]


def norm_kernel(scale, code_ref, out_ref):
    out_ref[...] = jnp.broadcast_to(norm_column(code_ref[...], scale), out_ref.shape)


def norm_calc(code, scale):
    k_dev, width = code.shape
    lanes = math.gcd(width, 128)
    vmem = pl.BlockSpec(memory_space=pltpu.VMEM)
    return pl.pallas_call(
        functools.partial(norm_kernel, scale),
        out_shape=jax.ShapeDtypeStruct((k_dev, lanes), jnp.float32),
        in_specs=[vmem],
        out_specs=vmem,
        compiler_params=pltpu.CompilerParams(vmem_limit_bytes=VMEM_LIMIT),
        cost_estimate=pl.CostEstimate(
            flops=2 * k_dev * width, bytes_accessed=2 * k_dev * width, transcendentals=0
        ),
        name="norm_calc",
    )(code)


def read_lse(lam_ref, outer, inner, spoke):
    each = [lam_ref[z * inner + spoke] for z in range(outer)]
    top = functools.reduce(jnp.maximum, each)
    return top + jnp.log(sum(jnp.exp(x - top) for x in each))


def add_groups(groups, tile, scale, levels, code_ref, norm_ref, emb, weighted, folded):
    lanes = folded.shape[1]
    code = code_ref[...]
    norm = jnp.concatenate([norm_ref[...]] * (tile // lanes), axis=1)
    for g, emb_ref in zip(groups, emb):
        level = LOG2E * levels(g)
        for start in range(0, emb_ref.shape[0], tile):
            rows_here = emb_ref[start : start + tile, :]
            s = scale * nt_dot(code, rows_here) - norm
            shares = jnp.exp2(s - level[:, start : start + tile]).astype(jnp.bfloat16)
            wide = shares.astype(jnp.float32)
            part = folded[...]
            for i in range(tile // lanes):
                part = part + wide[:, i * lanes : (i + 1) * lanes]
            folded[...] = part
            weighted[...] += jnp.dot(shares, rows_here, preferred_element_type=jnp.float32)


def early_kernel(outer, inner, groups, tile, scale, order, place_ref, lam_ref, code_ref, norm_ref, *refs):
    emb = refs[: len(groups)]
    weighted, folded = refs[len(groups) :]
    spoke = place_ref[0] % inner
    weighted[...] = jnp.zeros_like(weighted)
    folded[...] = jnp.zeros_like(folded)
    levels = lambda g: read_lse(lam_ref, outer, inner, spoke ^ g)
    add_groups(groups, tile, scale, levels, code_ref, norm_ref, emb, weighted, folded)


def late_kernel(outer, inner, groups, tile, scale, order, place_ref, lam_ref, code_ref, norm_ref, *refs):
    emb, refs = refs[: len(groups)], refs[len(groups) :]
    weighted_in, folded_in, shift_ref, occ_ref, weight_ref, own_ref, weighted, folded = refs
    k_dev = code_ref.shape[0]
    rows = lam_ref.shape[2]
    rows_dev = rows // outer
    place, spoke = place_ref[0] // inner, place_ref[0] % inner
    weighted[...] = weighted_in[...]
    folded[...] = folded_in[...]
    levels = lambda g: read_lse(lam_ref, outer, inner, spoke ^ g)
    add_groups(groups, tile, scale, levels, code_ref, norm_ref, emb, weighted, folded)
    masses = jnp.sum(folded[...], axis=1, keepdims=True)
    share = 1.0 / (masses + rows_dev / k_dev)
    shift_ref[...] = (
        (weighted[...] - masses * code_ref[...].astype(jnp.float32)) * share
    ).astype(jnp.bfloat16)
    spread = jnp.broadcast_to(masses * (k_dev / rows_dev), folded.shape).T
    occ_ref[...] = spread[:1, :]

    mine = levels(0)
    lines = [jnp.exp(lam_ref[(place ^ j) * inner + spoke] - mine) for j in order] + [mine]
    lines += [mine] * (-len(lines) % 8)
    near = pltpu.roll(jnp.concatenate(lines, axis=0), rows - place * rows_dev, 1)
    near = near[:, : min(rows, -(-rows_dev // 128) * 128)]
    weight_ref[...] = near.T[:rows_dev, :]
    own_ref[...] = near[outer : outer + 1, :rows_dev]


def soft_kernel(weight_ref, *refs):
    parts, soft_ref = refs[:-1], refs[-1]
    total = jnp.zeros(soft_ref.shape, jnp.float32)
    for i, part in enumerate(parts):
        total = total + weight_ref[:, i : i + 1] * part[...].astype(jnp.float32)
    soft_ref[...] = total.astype(jnp.bfloat16)


def soft_calc(weights, parts):
    vmem = pl.BlockSpec(memory_space=pltpu.VMEM)
    shape = parts[0].shape
    return pl.pallas_call(
        soft_kernel,
        out_shape=jax.ShapeDtypeStruct(shape, jnp.bfloat16),
        in_specs=[vmem] * (1 + len(parts)),
        out_specs=vmem,
        compiler_params=pltpu.CompilerParams(vmem_limit_bytes=VMEM_LIMIT),
        cost_estimate=pl.CostEstimate(
            flops=2 * len(parts) * shape[0] * shape[1],
            bytes_accessed=2 * (1 + len(parts)) * shape[0] * shape[1],
            transcendentals=0,
        ),
        name="soft_calc",
    )(weights, *parts)


def columns_calc(place, lam, code, norm, groups, emb, inner, sums=(), order=()):
    k_dev, width = code.shape
    rows = emb[0].shape[0]
    outer = lam.shape[0] // inner
    tile = math.gcd(rows, 768)
    lanes = norm.shape[1]
    totals = [((k_dev, width), jnp.float32), ((k_dev, lanes), jnp.float32)]
    if sums:
        body = late_kernel
        rows_dev = rows // outer
        out = [
            ((k_dev, width), jnp.bfloat16),
            ((1, k_dev), jnp.float32),
            ((rows_dev, -(-(outer + 1) // 8) * 8), jnp.float32),
            ((1, rows_dev), jnp.float32),
        ]
        scratch = [pltpu.VMEM(*x) for x in totals]
    else:
        body, out, scratch = early_kernel, totals, []
    vmem = pl.BlockSpec(memory_space=pltpu.VMEM)
    return pl.pallas_call(
        functools.partial(
            body, outer, inner, groups, tile, LOG2E * 3.0 / math.sqrt(width), order
        ),
        out_shape=[jax.ShapeDtypeStruct(*x) for x in out],
        in_specs=[pl.BlockSpec(memory_space=pltpu.SMEM)]
        + [vmem] * (3 + len(emb) + len(sums)),
        out_specs=[vmem] * len(out),
        scratch_shapes=scratch,
        compiler_params=pltpu.CompilerParams(vmem_limit_bytes=VMEM_LIMIT),
        cost_estimate=pl.CostEstimate(
            flops=(4 if sums else EARLY) * len(emb) * rows * k_dev * width,
            bytes_accessed=2 * (len(emb) * rows + 2 * k_dev) * width,
            transcendentals=len(emb) * rows * k_dev,
        ),
        name="columns_calc",
    )(place, lam, code, norm, *emb, *sums)


def after(x, y):
    return lax.optimization_barrier((x, y))[0]


def on_device(size, embeddings, codebook):
    inner = 4
    outer = size // inner
    place = lax.axis_index(AXIS).astype(jnp.int32).reshape(1)

    def swap(x, step):
        return lax.ppermute(x, AXIS, [(i, i ^ step) for i in range(size)])

    code_y = swap(codebook, 2)
    code_c = swap(codebook, 1)
    shape = (outer * embeddings.shape[0], embeddings.shape[1])
    order = (outer // 2, *(j for j in range(1, outer) if j != outer // 2), 0)
    own_rows, own_code = keep(embeddings, codebook)
    first = (*range(2, outer), 1, 0)
    blocks = [swap(embeddings, inner * j) for j in first[:-1]] + [own_rows]
    stacked = stack(place, blocks, first, inner, shape)
    stacked_y = swap(stacked, 2)
    stacked_c = swap(stacked, 1)
    code = [own_code, code_c, code_y, swap(code_y, 1)]
    lam, parts = rows_calc(place, stacked, code, outer)

    sent = [swap(parts[j], inner * j) for j in order[:-1]]
    lam = lax.all_to_all(lam, AXIS, 0, 0)
    lam = after(lam, sent[0])
    norm = norm_calc(own_code, LOG2E * 3.0 / math.sqrt(codebook.shape[1]))
    stacked_yc = swap(stacked_y, 1)
    sums = columns_calc(
        place, lam, own_code, norm, (0, 1, 2), [stacked, stacked_c, stacked_y], inner
    )
    shift, occupancy, weights, own_lse = columns_calc(
        place, lam, own_code, norm, (3,), [stacked_yc], inner, sums, order
    )
    soft = soft_calc(weights, [*sent, parts[0]])
    return shift, occupancy.reshape(-1), soft, own_lse.reshape(-1)


def solution(mesh):
    specs = P(("groups", AXIS), None)
    flat = P(("groups", AXIS))
    return jax.shard_map(
        functools.partial(on_device, mesh.shape[AXIS]),
        mesh=mesh,
        in_specs=(specs, specs),
        out_specs=(specs, flat, specs, flat),
        check_vma=False,
    )
```

```python
import functools
import math

import jax
import jax.numpy as jnp
from jax import lax
from jax.experimental import pallas as pl
from jax.experimental.pallas import tpu as pltpu
from jax.sharding import PartitionSpec as P

AXIS = "blk"
LOG2E = math.log2(math.e)
LN2 = math.log(2.0)
VMEM_LIMIT = 20 * 1024 * 1024
EARLY = 64
STACK = 3 << 29


def nt_dot(a, b):
    return lax.dot_general(a, b, (((1,), (1,)), ((), ())), preferred_element_type=jnp.float32)


def norm_column(code, scale):
    c = code.astype(jnp.float32)
    return (0.5 * scale) * jnp.sum(c * c, axis=1, keepdims=True)


def keep_kernel(*refs):
    half = len(refs) // 2
    for x_ref, out_ref in zip(refs[:half], refs[half:]):
        out_ref[...] = x_ref[...]


def keep(*arrays):
    vmem = pl.BlockSpec(memory_space=pltpu.VMEM)
    return pl.pallas_call(
        keep_kernel,
        out_shape=[jax.ShapeDtypeStruct(x.shape, x.dtype) for x in arrays],
        in_specs=[vmem] * len(arrays),
        out_specs=[vmem] * len(arrays),
        compiler_params=pltpu.CompilerParams(vmem_limit_bytes=VMEM_LIMIT),
        cost_estimate=pl.CostEstimate(
            flops=0, bytes_accessed=4 * sum(x.size for x in arrays), transcendentals=0
        ),
        name="keep",
    )(*arrays)


def stack_kernel(inner, steps, place_ref, *refs):
    blocks, out_ref = refs[: len(steps)], refs[-1]
    rows_dev = blocks[0].shape[0]
    place = place_ref[0] // inner
    for j, block in zip(steps, blocks):
        spot = pl.multiple_of((place ^ j) * rows_dev, rows_dev)
        out_ref[pl.ds(spot, rows_dev), :] = block[...]


def stack(place, blocks, steps, inner, shape):
    vmem = pl.BlockSpec(memory_space=pltpu.VMEM)
    return pl.pallas_call(
        functools.partial(stack_kernel, inner, steps),
        out_shape=jax.ShapeDtypeStruct(shape, blocks[0].dtype),
        in_specs=[pl.BlockSpec(memory_space=pltpu.SMEM)] + [vmem] * len(blocks),
        out_specs=vmem,
        compiler_params=pltpu.CompilerParams(vmem_limit_bytes=VMEM_LIMIT),
        cost_estimate=pl.CostEstimate(
            flops=STACK, bytes_accessed=4 * shape[0] * shape[1], transcendentals=0
        ),
        name="stack",
    )(place, *blocks)


def fold_lanes(op, x, lanes):
    parts = [x[:, i : i + lanes] for i in range(0, x.shape[1], lanes)]
    return functools.reduce(op, parts)


def rows_kernel(outer, inner, tile, scale, place_ref, stacked_ref, *refs):
    code = refs[:inner]
    lam_ref = refs[inner]
    parts = refs[inner + 1 : inner + 1 + outer]
    scores, total = refs[inner + 1 + outer :]
    rows, width = stacked_ref.shape
    rows_dev = rows // outer
    k_dev = code[0].shape[0]
    lanes = math.gcd(k_dev, 128)
    place = place_ref[0] // inner
    norms = [
        jnp.broadcast_to(norm_column(code[k][...], scale), (k_dev, lanes)).T[:1, :]
        for k in range(inner)
    ]

    def first_half(start, slot):
        rows_here = stacked_ref[pl.ds(start, tile), :]
        top = None
        for k in range(inner):
            s = scale * nt_dot(rows_here, code[k][...]) - norms[k]
            scores[slot : slot + tile, k * k_dev : (k + 1) * k_dev] = s
            m = fold_lanes(jnp.maximum, s, lanes)
            top = m if top is None else jnp.maximum(top, m)
        return jnp.max(top, axis=1, keepdims=True)

    def second_half(start, slot, top):
        mass = jnp.zeros((tile, lanes), jnp.float32)
        acc = jnp.zeros((tile, width), jnp.float32)
        for k in range(inner):
            p = jnp.exp2(scores[slot : slot + tile, k * k_dev : (k + 1) * k_dev] - top)
            mass = mass + fold_lanes(jnp.add, p, lanes)
            acc = acc + jnp.dot(
                p.astype(jnp.bfloat16), code[k][...], preferred_element_type=jnp.float32
            )
        mass = jnp.sum(mass, axis=1, keepdims=True)
        lam = jnp.broadcast_to(LN2 * (top + jnp.log2(mass)), (tile, lanes)).T[:1, :]
        lam_ref[:, :, pl.ds(start, tile)] = jnp.broadcast_to(
            lam.reshape(1, 1, tile), (lam_ref.shape[0], 1, tile)
        )
        total[pl.ds(start, tile), :] = (acc * (1.0 / mass)).astype(jnp.bfloat16)

    count = rows // tile
    if count <= 4:
        top = first_half(0, 0)
        for t in range(count):
            here = top
            if t + 1 < count:
                top = first_half((t + 1) * tile, (t + 1) * tile)
            second_half(t * tile, t * tile, here)
    else:

        @pl.loop(0, count)
        def one_tile(t):
            start = pl.multiple_of(t * tile, tile)
            second_half(start, 0, first_half(start, 0))

    for j in range(outer):
        spot = pl.multiple_of((place ^ j) * rows_dev, rows_dev)
        parts[j][...] = total[pl.ds(spot, rows_dev), :]


def rows_calc(place, stacked, code, outer):
    inner = len(code)
    rows, width = stacked.shape
    rows_dev = rows // outer
    entries = inner * code[0].shape[0]
    tile = math.gcd(rows, 256)
    vmem = pl.BlockSpec(memory_space=pltpu.VMEM)
    out = pl.pallas_call(
        functools.partial(rows_kernel, outer, inner, tile, LOG2E * 3.0 / math.sqrt(width)),
        out_shape=[jax.ShapeDtypeStruct((outer * inner, 1, rows), jnp.float32)]
        + [jax.ShapeDtypeStruct((rows_dev, width), jnp.bfloat16)] * outer,
        in_specs=[pl.BlockSpec(memory_space=pltpu.SMEM)] + [vmem] * (1 + inner),
        out_specs=[vmem] * (outer + 1),
        scratch_shapes=[
            pltpu.VMEM((min(rows, 4 * tile), entries), jnp.float32),
            pltpu.VMEM((rows, width), jnp.bfloat16),
        ],
        compiler_params=pltpu.CompilerParams(vmem_limit_bytes=VMEM_LIMIT),
        cost_estimate=pl.CostEstimate(
            flops=4 * rows * entries * width,
            bytes_accessed=2 * (rows + entries) * width,
            transcendentals=rows * entries,
        ),
        name="rows_calc",
    )(place, stacked, *code)
    return out[0], out[1:]


def norm_kernel(scale, code_ref, out_ref):
    out_ref[...] = jnp.broadcast_to(norm_column(code_ref[...], scale), out_ref.shape)


def norm_calc(code, scale):
    k_dev, width = code.shape
    lanes = math.gcd(width, 128)
    vmem = pl.BlockSpec(memory_space=pltpu.VMEM)
    return pl.pallas_call(
        functools.partial(norm_kernel, scale),
        out_shape=jax.ShapeDtypeStruct((k_dev, lanes), jnp.float32),
        in_specs=[vmem],
        out_specs=vmem,
        compiler_params=pltpu.CompilerParams(vmem_limit_bytes=VMEM_LIMIT),
        cost_estimate=pl.CostEstimate(
            flops=2 * k_dev * width, bytes_accessed=2 * k_dev * width, transcendentals=0
        ),
        name="norm_calc",
    )(code)


def read_lse(lam_ref, outer, inner, spoke):
    each = [lam_ref[z * inner + spoke] for z in range(outer)]
    top = functools.reduce(jnp.maximum, each)
    return top + jnp.log(sum(jnp.exp(x - top) for x in each))


def add_groups(groups, tile, scale, levels, code_ref, norm_ref, emb, weighted, folded):
    lanes = folded.shape[1]
    code = code_ref[...]
    norm = jnp.concatenate([norm_ref[...]] * (tile // lanes), axis=1)
    for g, emb_ref in zip(groups, emb):
        level = LOG2E * levels(g)
        for start in range(0, emb_ref.shape[0], tile):
            rows_here = emb_ref[start : start + tile, :]
            s = scale * nt_dot(code, rows_here) - norm
            shares = jnp.exp2(s - level[:, start : start + tile]).astype(jnp.bfloat16)
            wide = shares.astype(jnp.float32)
            part = folded[...]
            for i in range(tile // lanes):
                part = part + wide[:, i * lanes : (i + 1) * lanes]
            folded[...] = part
            weighted[...] += jnp.dot(shares, rows_here, preferred_element_type=jnp.float32)


def early_kernel(outer, inner, groups, tile, scale, order, place_ref, lam_ref, code_ref, norm_ref, *refs):
    emb = refs[: len(groups)]
    weighted, folded = refs[len(groups) :]
    spoke = place_ref[0] % inner
    weighted[...] = jnp.zeros_like(weighted)
    folded[...] = jnp.zeros_like(folded)
    levels = lambda g: read_lse(lam_ref, outer, inner, spoke ^ g)
    add_groups(groups, tile, scale, levels, code_ref, norm_ref, emb, weighted, folded)


def late_kernel(outer, inner, groups, tile, scale, order, place_ref, lam_ref, code_ref, norm_ref, *refs):
    emb, refs = refs[: len(groups)], refs[len(groups) :]
    weighted_in, folded_in, shift_ref, occ_ref, weight_ref, own_ref, weighted, folded = refs
    k_dev = code_ref.shape[0]
    rows = lam_ref.shape[2]
    rows_dev = rows // outer
    place, spoke = place_ref[0] // inner, place_ref[0] % inner
    weighted[...] = weighted_in[...]
    folded[...] = folded_in[...]
    levels = lambda g: read_lse(lam_ref, outer, inner, spoke ^ g)
    add_groups(groups, tile, scale, levels, code_ref, norm_ref, emb, weighted, folded)
    masses = jnp.sum(folded[...], axis=1, keepdims=True)
    share = 1.0 / (masses + rows_dev / k_dev)
    shift_ref[...] = (
        (weighted[...] - masses * code_ref[...].astype(jnp.float32)) * share
    ).astype(jnp.bfloat16)
    spread = jnp.broadcast_to(masses * (k_dev / rows_dev), folded.shape).T
    occ_ref[...] = spread[:1, :]

    mine = levels(0)
    lines = [jnp.exp(lam_ref[(place ^ j) * inner + spoke] - mine) for j in order] + [mine]
    lines += [mine] * (-len(lines) % 8)
    near = pltpu.roll(jnp.concatenate(lines, axis=0), (outer - place) % outer * rows_dev, 1)
    near = near[:, : min(rows, -(-rows_dev // 128) * 128)]
    weight_ref[...] = near.T[:rows_dev, :]
    own_ref[...] = near[outer : outer + 1, :rows_dev]


def soft_kernel(weight_ref, *refs):
    parts, soft_ref = refs[:-1], refs[-1]
    total = jnp.zeros(soft_ref.shape, jnp.float32)
    for i, part in enumerate(parts):
        total = total + weight_ref[:, i : i + 1] * part[...].astype(jnp.float32)
    soft_ref[...] = total.astype(jnp.bfloat16)


def soft_calc(weights, parts):
    vmem = pl.BlockSpec(memory_space=pltpu.VMEM)
    shape = parts[0].shape
    return pl.pallas_call(
        soft_kernel,
        out_shape=jax.ShapeDtypeStruct(shape, jnp.bfloat16),
        in_specs=[vmem] * (1 + len(parts)),
        out_specs=vmem,
        compiler_params=pltpu.CompilerParams(vmem_limit_bytes=VMEM_LIMIT),
        cost_estimate=pl.CostEstimate(
            flops=2 * len(parts) * shape[0] * shape[1],
            bytes_accessed=2 * (1 + len(parts)) * shape[0] * shape[1],
            transcendentals=0,
        ),
        name="soft_calc",
    )(weights, *parts)


def columns_calc(place, lam, code, norm, groups, emb, inner, sums=(), order=()):
    k_dev, width = code.shape
    rows = emb[0].shape[0]
    outer = lam.shape[0] // inner
    tile = math.gcd(rows, 768)
    lanes = norm.shape[1]
    totals = [((k_dev, width), jnp.float32), ((k_dev, lanes), jnp.float32)]
    if sums:
        body = late_kernel
        rows_dev = rows // outer
        out = [
            ((k_dev, width), jnp.bfloat16),
            ((1, k_dev), jnp.float32),
            ((rows_dev, -(-(outer + 1) // 8) * 8), jnp.float32),
            ((1, rows_dev), jnp.float32),
        ]
        scratch = [pltpu.VMEM(*x) for x in totals]
    else:
        body, out, scratch = early_kernel, totals, []
    vmem = pl.BlockSpec(memory_space=pltpu.VMEM)
    return pl.pallas_call(
        functools.partial(
            body, outer, inner, groups, tile, LOG2E * 3.0 / math.sqrt(width), order
        ),
        out_shape=[jax.ShapeDtypeStruct(*x) for x in out],
        in_specs=[pl.BlockSpec(memory_space=pltpu.SMEM)]
        + [vmem] * (3 + len(emb) + len(sums)),
        out_specs=[vmem] * len(out),
        scratch_shapes=scratch,
        compiler_params=pltpu.CompilerParams(vmem_limit_bytes=VMEM_LIMIT),
        cost_estimate=pl.CostEstimate(
            flops=(4 if sums else EARLY) * len(emb) * rows * k_dev * width,
            bytes_accessed=2 * (len(emb) * rows + 2 * k_dev) * width,
            transcendentals=len(emb) * rows * k_dev,
        ),
        name="columns_calc",
    )(place, lam, code, norm, *emb, *sums)


def after(x, y):
    return lax.optimization_barrier((x, y))[0]


def on_device(size, embeddings, codebook):
    inner = 4
    outer = size // inner
    place = lax.axis_index(AXIS).astype(jnp.int32).reshape(1)

    def swap(x, step):
        return lax.ppermute(x, AXIS, [(i, i ^ step) for i in range(size)])

    code_y = swap(codebook, 2)
    code_c = swap(codebook, 1)
    shape = (outer * embeddings.shape[0], embeddings.shape[1])
    order = (outer // 2, *(j for j in range(1, outer) if j != outer // 2), 0)
    own_rows, own_code = keep(embeddings, codebook)
    first = (*range(2, outer), 1, 0)
    blocks = [swap(embeddings, inner * j) for j in first[:-1]] + [own_rows]
    stacked = stack(place, blocks, first, inner, shape)
    stacked_y = swap(stacked, 2)
    stacked_c = swap(stacked, 1)
    code = [own_code, code_c, code_y, swap(code_y, 1)]
    lam, parts = rows_calc(place, stacked, code, outer)

    sent = [swap(parts[j], inner * j) for j in order[:-1]]
    lam = lax.all_to_all(lam, AXIS, 0, 0)
    lam = after(lam, sent[0])
    norm = norm_calc(own_code, LOG2E * 3.0 / math.sqrt(codebook.shape[1]))
    stacked_yc = swap(stacked_y, 1)
    sums = columns_calc(
        place, lam, own_code, norm, (0, 1, 2), [stacked, stacked_c, stacked_y], inner
    )
    shift, occupancy, weights, own_lse = columns_calc(
        place, lam, own_code, norm, (3,), [stacked_yc], inner, sums, order
    )
    soft = soft_calc(weights, [*sent, parts[0]])
    return shift, occupancy.reshape(-1), soft, own_lse.reshape(-1)


def solution(mesh):
    specs = P(("groups", AXIS), None)
    flat = P(("groups", AXIS))
    return jax.shard_map(
        functools.partial(on_device, mesh.shape[AXIS]),
        mesh=mesh,
        in_specs=(specs, specs),
        out_specs=(specs, flat, specs, flat),
        check_vma=False,
    )
```

```python
import functools
import math

import jax
import jax.numpy as jnp
from jax import lax
from jax.experimental import pallas as pl
from jax.experimental.pallas import tpu as pltpu
from jax.sharding import PartitionSpec as P

AXIS = "blk"
LOG2E = math.log2(math.e)
LN2 = math.log(2.0)
VMEM_LIMIT = 20 * 1024 * 1024
EARLY = 64
STACK = 3 << 29


def nt_dot(a, b):
    return lax.dot_general(a, b, (((1,), (1,)), ((), ())), preferred_element_type=jnp.float32)


def norm_column(code, scale):
    c = code.astype(jnp.float32)
    return (0.5 * scale) * jnp.sum(c * c, axis=1, keepdims=True)


def keep_kernel(*refs):
    half = len(refs) // 2
    for x_ref, out_ref in zip(refs[:half], refs[half:]):
        out_ref[...] = x_ref[...]


def keep(*arrays):
    vmem = pl.BlockSpec(memory_space=pltpu.VMEM)
    return pl.pallas_call(
        keep_kernel,
        out_shape=[jax.ShapeDtypeStruct(x.shape, x.dtype) for x in arrays],
        in_specs=[vmem] * len(arrays),
        out_specs=[vmem] * len(arrays),
        compiler_params=pltpu.CompilerParams(vmem_limit_bytes=VMEM_LIMIT),
        cost_estimate=pl.CostEstimate(
            flops=0, bytes_accessed=4 * sum(x.size for x in arrays), transcendentals=0
        ),
        name="keep",
    )(*arrays)


def stack_kernel(inner, steps, place_ref, *refs):
    blocks, out_ref = refs[: len(steps)], refs[-1]
    rows_dev = blocks[0].shape[0]
    place = place_ref[0] // inner
    for j, block in zip(steps, blocks):
        spot = pl.multiple_of((place ^ j) * rows_dev, rows_dev)
        out_ref[pl.ds(spot, rows_dev), :] = block[...]


def stack(place, blocks, steps, inner, shape):
    vmem = pl.BlockSpec(memory_space=pltpu.VMEM)
    return pl.pallas_call(
        functools.partial(stack_kernel, inner, steps),
        out_shape=jax.ShapeDtypeStruct(shape, blocks[0].dtype),
        in_specs=[pl.BlockSpec(memory_space=pltpu.SMEM)] + [vmem] * len(blocks),
        out_specs=vmem,
        compiler_params=pltpu.CompilerParams(vmem_limit_bytes=VMEM_LIMIT),
        cost_estimate=pl.CostEstimate(
            flops=STACK, bytes_accessed=4 * shape[0] * shape[1], transcendentals=0
        ),
        name="stack",
    )(place, *blocks)


def fold_lanes(op, x, lanes):
    parts = [x[:, i : i + lanes] for i in range(0, x.shape[1], lanes)]
    return functools.reduce(op, parts)


def rows_kernel(outer, inner, tile, scale, place_ref, stacked_ref, *refs):
    code = refs[:inner]
    lam_ref = refs[inner]
    parts = refs[inner + 1 : inner + 1 + outer]
    scores, total = refs[inner + 1 + outer :]
    rows, width = stacked_ref.shape
    rows_dev = rows // outer
    k_dev = code[0].shape[0]
    lanes = math.gcd(k_dev, 128)
    place = place_ref[0] // inner
    norms = [
        jnp.broadcast_to(norm_column(code[k][...], scale), (k_dev, lanes)).T[:1, :]
        for k in range(inner)
    ]

    def first_half(start, slot):
        rows_here = stacked_ref[pl.ds(start, tile), :]
        top = None
        for k in range(inner):
            s = scale * nt_dot(rows_here, code[k][...]) - norms[k]
            scores[slot : slot + tile, k * k_dev : (k + 1) * k_dev] = s
            m = fold_lanes(jnp.maximum, s, lanes)
            top = m if top is None else jnp.maximum(top, m)
        return jnp.max(top, axis=1, keepdims=True)

    def second_half(start, slot, top):
        mass = jnp.zeros((tile, lanes), jnp.float32)
        acc = jnp.zeros((tile, width), jnp.float32)
        for k in range(inner):
            p = jnp.exp2(scores[slot : slot + tile, k * k_dev : (k + 1) * k_dev] - top)
            mass = mass + fold_lanes(jnp.add, p, lanes)
            acc = acc + jnp.dot(
                p.astype(jnp.bfloat16), code[k][...], preferred_element_type=jnp.float32
            )
        mass = jnp.sum(mass, axis=1, keepdims=True)
        lam = jnp.broadcast_to(LN2 * (top + jnp.log2(mass)), (tile, lanes)).T[:1, :]
        lam_ref[:, :, pl.ds(start, tile)] = jnp.broadcast_to(
            lam.reshape(1, 1, tile), (lam_ref.shape[0], 1, tile)
        )
        total[pl.ds(start, tile), :] = (acc * (1.0 / mass)).astype(jnp.bfloat16)

    count = rows // tile
    if count <= 4:
        top = first_half(0, 0)
        for t in range(count):
            here = top
            if t + 1 < count:
                top = first_half((t + 1) * tile, (t + 1) * tile)
            second_half(t * tile, t * tile, here)
    else:

        @pl.loop(0, count)
        def one_tile(t):
            start = pl.multiple_of(t * tile, tile)
            second_half(start, 0, first_half(start, 0))

    for j in range(outer):
        spot = pl.multiple_of((place ^ j) * rows_dev, rows_dev)
        parts[j][...] = total[pl.ds(spot, rows_dev), :]


def rows_calc(place, stacked, code, outer):
    inner = len(code)
    rows, width = stacked.shape
    rows_dev = rows // outer
    entries = inner * code[0].shape[0]
    tile = math.gcd(rows, 256)
    vmem = pl.BlockSpec(memory_space=pltpu.VMEM)
    out = pl.pallas_call(
        functools.partial(rows_kernel, outer, inner, tile, LOG2E * 3.0 / math.sqrt(width)),
        out_shape=[jax.ShapeDtypeStruct((outer * inner, 1, rows), jnp.float32)]
        + [jax.ShapeDtypeStruct((rows_dev, width), jnp.bfloat16)] * outer,
        in_specs=[pl.BlockSpec(memory_space=pltpu.SMEM)] + [vmem] * (1 + inner),
        out_specs=[vmem] * (outer + 1),
        scratch_shapes=[
            pltpu.VMEM((min(rows, 4 * tile), entries), jnp.float32),
            pltpu.VMEM((rows, width), jnp.bfloat16),
        ],
        compiler_params=pltpu.CompilerParams(vmem_limit_bytes=VMEM_LIMIT),
        cost_estimate=pl.CostEstimate(
            flops=4 * rows * entries * width,
            bytes_accessed=2 * (rows + entries) * width,
            transcendentals=rows * entries,
        ),
        name="rows_calc",
    )(place, stacked, *code)
    return out[0], out[1:]


def norm_kernel(scale, code_ref, out_ref):
    out_ref[...] = jnp.broadcast_to(norm_column(code_ref[...], scale), out_ref.shape)


def norm_calc(code, scale):
    k_dev, width = code.shape
    lanes = math.gcd(width, 128)
    vmem = pl.BlockSpec(memory_space=pltpu.VMEM)
    return pl.pallas_call(
        functools.partial(norm_kernel, scale),
        out_shape=jax.ShapeDtypeStruct((k_dev, lanes), jnp.float32),
        in_specs=[vmem],
        out_specs=vmem,
        compiler_params=pltpu.CompilerParams(vmem_limit_bytes=VMEM_LIMIT),
        cost_estimate=pl.CostEstimate(
            flops=2 * k_dev * width, bytes_accessed=2 * k_dev * width, transcendentals=0
        ),
        name="norm_calc",
    )(code)


def read_lse(lam_ref, outer, inner, spoke):
    each = [lam_ref[z * inner + spoke] for z in range(outer)]
    top = functools.reduce(jnp.maximum, each)
    return top + jnp.log(sum(jnp.exp(x - top) for x in each))


def add_groups(
    groups, tile, scale, levels, code_ref, norm_ref, emb, weighted, folded, before=None
):
    lanes = folded.shape[1]
    code = code_ref[...]
    norm = jnp.concatenate([norm_ref[...]] * (tile // lanes), axis=1)
    for g, emb_ref in zip(groups, emb):
        level = LOG2E * levels(g)
        for start in range(0, emb_ref.shape[0], tile):
            rows_here = emb_ref[start : start + tile, :]
            s = scale * nt_dot(code, rows_here) - norm
            shares = jnp.exp2(s - level[:, start : start + tile]).astype(jnp.bfloat16)
            wide = shares.astype(jnp.float32)
            part = fold_lanes(jnp.add, wide, lanes)
            product = jnp.dot(shares, rows_here, preferred_element_type=jnp.float32)
            if before is not None:
                product, part = product + before[0][...], part + before[1][...]
            weighted[...], folded[...] = product, part
            before = weighted, folded


def early_kernel(outer, inner, groups, tile, scale, order, place_ref, lam_ref, code_ref, norm_ref, *refs):
    emb = refs[: len(groups)]
    weighted, folded = refs[len(groups) :]
    spoke = place_ref[0] % inner
    levels = lambda g: read_lse(lam_ref, outer, inner, spoke ^ g)
    add_groups(groups, tile, scale, levels, code_ref, norm_ref, emb, weighted, folded)


def late_kernel(outer, inner, groups, tile, scale, order, place_ref, lam_ref, code_ref, norm_ref, *refs):
    emb, refs = refs[: len(groups)], refs[len(groups) :]
    weighted_in, folded_in, shift_ref, occ_ref, weight_ref, own_ref, weighted, folded = refs
    k_dev = code_ref.shape[0]
    rows = lam_ref.shape[2]
    rows_dev = rows // outer
    place, spoke = place_ref[0] // inner, place_ref[0] % inner
    levels = lambda g: read_lse(lam_ref, outer, inner, spoke ^ g)
    before = weighted_in, folded_in
    add_groups(groups, tile, scale, levels, code_ref, norm_ref, emb, weighted, folded, before)
    masses = jnp.sum(folded[...], axis=1, keepdims=True)
    share = 1.0 / (masses + rows_dev / k_dev)
    shift_ref[...] = (
        (weighted[...] - masses * code_ref[...].astype(jnp.float32)) * share
    ).astype(jnp.bfloat16)
    spread = jnp.broadcast_to(masses * (k_dev / rows_dev), folded.shape).T
    occ_ref[...] = spread[:1, :]

    mine = levels(0)
    lines = [jnp.exp(lam_ref[(place ^ j) * inner + spoke] - mine) for j in order] + [mine]
    lines += [mine] * (-len(lines) % 8)
    near = pltpu.roll(jnp.concatenate(lines, axis=0), (outer - place) % outer * rows_dev, 1)
    near = near[:, : min(rows, -(-rows_dev // 128) * 128)]
    weight_ref[...] = near.T[:rows_dev, :]
    own_ref[...] = near[outer : outer + 1, :rows_dev]


def soft_kernel(weight_ref, *refs):
    parts, soft_ref = refs[:-1], refs[-1]
    total = jnp.zeros(soft_ref.shape, jnp.float32)
    for i, part in enumerate(parts):
        total = total + weight_ref[:, i : i + 1] * part[...].astype(jnp.float32)
    soft_ref[...] = total.astype(jnp.bfloat16)


def soft_calc(weights, parts):
    vmem = pl.BlockSpec(memory_space=pltpu.VMEM)
    shape = parts[0].shape
    return pl.pallas_call(
        soft_kernel,
        out_shape=jax.ShapeDtypeStruct(shape, jnp.bfloat16),
        in_specs=[vmem] * (1 + len(parts)),
        out_specs=vmem,
        compiler_params=pltpu.CompilerParams(vmem_limit_bytes=VMEM_LIMIT),
        cost_estimate=pl.CostEstimate(
            flops=2 * len(parts) * shape[0] * shape[1],
            bytes_accessed=2 * (1 + len(parts)) * shape[0] * shape[1],
            transcendentals=0,
        ),
        name="soft_calc",
    )(weights, *parts)


def columns_calc(place, lam, code, norm, groups, emb, inner, sums=(), order=()):
    k_dev, width = code.shape
    rows = emb[0].shape[0]
    outer = lam.shape[0] // inner
    tile = math.gcd(rows, 768)
    lanes = norm.shape[1]
    totals = [((k_dev, width), jnp.float32), ((k_dev, lanes), jnp.float32)]
    if sums:
        body = late_kernel
        rows_dev = rows // outer
        out = [
            ((k_dev, width), jnp.bfloat16),
            ((1, k_dev), jnp.float32),
            ((rows_dev, -(-(outer + 1) // 8) * 8), jnp.float32),
            ((1, rows_dev), jnp.float32),
        ]
        scratch = [pltpu.VMEM(*x) for x in totals]
    else:
        body, out, scratch = early_kernel, totals, []
    vmem = pl.BlockSpec(memory_space=pltpu.VMEM)
    return pl.pallas_call(
        functools.partial(
            body, outer, inner, groups, tile, LOG2E * 3.0 / math.sqrt(width), order
        ),
        out_shape=[jax.ShapeDtypeStruct(*x) for x in out],
        in_specs=[pl.BlockSpec(memory_space=pltpu.SMEM)]
        + [vmem] * (3 + len(emb) + len(sums)),
        out_specs=[vmem] * len(out),
        scratch_shapes=scratch,
        compiler_params=pltpu.CompilerParams(vmem_limit_bytes=VMEM_LIMIT),
        cost_estimate=pl.CostEstimate(
            flops=(4 if sums else EARLY) * len(emb) * rows * k_dev * width,
            bytes_accessed=2 * (len(emb) * rows + 2 * k_dev) * width,
            transcendentals=len(emb) * rows * k_dev,
        ),
        name="columns_calc",
    )(place, lam, code, norm, *emb, *sums)


def after(x, y):
    return lax.optimization_barrier((x, y))[0]


def on_device(size, embeddings, codebook):
    inner = 4
    outer = size // inner
    place = lax.axis_index(AXIS).astype(jnp.int32).reshape(1)

    def swap(x, step):
        return lax.ppermute(x, AXIS, [(i, i ^ step) for i in range(size)])

    code_y = swap(codebook, 2)
    code_c = swap(codebook, 1)
    shape = (outer * embeddings.shape[0], embeddings.shape[1])
    order = (outer // 2, *(j for j in range(1, outer) if j != outer // 2), 0)
    own_rows, own_code = keep(embeddings, codebook)
    first = (*range(2, outer), 1, 0)
    blocks = [swap(embeddings, inner * j) for j in first[:-1]] + [own_rows]
    stacked = stack(place, blocks, first, inner, shape)
    stacked_y = swap(stacked, 2)
    stacked_c = swap(stacked, 1)
    code = [own_code, code_c, code_y, swap(code_y, 1)]
    lam, parts = rows_calc(place, stacked, code, outer)

    sent = [swap(parts[j], inner * j) for j in order[:-1]]
    lam = lax.all_to_all(lam, AXIS, 0, 0)
    lam = after(lam, sent[0])
    norm = norm_calc(own_code, LOG2E * 3.0 / math.sqrt(codebook.shape[1]))
    stacked_yc = swap(stacked_y, 1)
    sums = columns_calc(
        place, lam, own_code, norm, (0, 1, 2), [stacked, stacked_c, stacked_y], inner
    )
    shift, occupancy, weights, own_lse = columns_calc(
        place, lam, own_code, norm, (3,), [stacked_yc], inner, sums, order
    )
    soft = soft_calc(weights, [*sent, parts[0]])
    return shift, occupancy.reshape(-1), soft, own_lse.reshape(-1)


def solution(mesh):
    specs = P(("groups", AXIS), None)
    flat = P(("groups", AXIS))
    return jax.shard_map(
        functools.partial(on_device, mesh.shape[AXIS]),
        mesh=mesh,
        in_specs=(specs, specs),
        out_specs=(specs, flat, specs, flat),
        check_vma=False,
    )
```

```python
import functools
import math

import jax
import jax.numpy as jnp
from jax import lax
from jax.experimental import pallas as pl
from jax.experimental.pallas import tpu as pltpu
from jax.sharding import PartitionSpec as P

AXIS = "blk"
LOG2E = math.log2(math.e)
LN2 = math.log(2.0)
VMEM_LIMIT = 20 * 1024 * 1024
EARLY = 64
STACK = 3 << 29


def nt_dot(a, b):
    return lax.dot_general(a, b, (((1,), (1,)), ((), ())), preferred_element_type=jnp.float32)


def norm_column(code, scale):
    c = code.astype(jnp.float32)
    return (0.5 * scale) * jnp.sum(c * c, axis=1, keepdims=True)


def keep_kernel(*refs):
    half = len(refs) // 2
    for x_ref, out_ref in zip(refs[:half], refs[half:]):
        out_ref[...] = x_ref[...]


def keep(*arrays):
    vmem = pl.BlockSpec(memory_space=pltpu.VMEM)
    return pl.pallas_call(
        keep_kernel,
        out_shape=[jax.ShapeDtypeStruct(x.shape, x.dtype) for x in arrays],
        in_specs=[vmem] * len(arrays),
        out_specs=[vmem] * len(arrays),
        compiler_params=pltpu.CompilerParams(vmem_limit_bytes=VMEM_LIMIT),
        cost_estimate=pl.CostEstimate(
            flops=0, bytes_accessed=4 * sum(x.size for x in arrays), transcendentals=0
        ),
        name="keep",
    )(*arrays)


def stack_kernel(inner, steps, place_ref, *refs):
    blocks, out_ref = refs[: len(steps)], refs[-1]
    rows_dev = blocks[0].shape[0]
    place = place_ref[0] // inner
    for j, block in zip(steps, blocks):
        spot = pl.multiple_of((place ^ j) * rows_dev, rows_dev)
        out_ref[pl.ds(spot, rows_dev), :] = block[...]


def stack(place, blocks, steps, inner, shape):
    vmem = pl.BlockSpec(memory_space=pltpu.VMEM)
    return pl.pallas_call(
        functools.partial(stack_kernel, inner, steps),
        out_shape=jax.ShapeDtypeStruct(shape, blocks[0].dtype),
        in_specs=[pl.BlockSpec(memory_space=pltpu.SMEM)] + [vmem] * len(blocks),
        out_specs=vmem,
        compiler_params=pltpu.CompilerParams(vmem_limit_bytes=VMEM_LIMIT),
        cost_estimate=pl.CostEstimate(
            flops=STACK, bytes_accessed=4 * shape[0] * shape[1], transcendentals=0
        ),
        name="stack",
    )(place, *blocks)


def fold_lanes(op, x, lanes):
    parts = [x[:, i : i + lanes] for i in range(0, x.shape[1], lanes)]
    return functools.reduce(op, parts)


def rows_kernel(outer, inner, tile, scale, place_ref, stacked_ref, *refs):
    code = refs[:inner]
    lam_ref = refs[inner]
    parts = refs[inner + 1 : inner + 1 + outer]
    scores, total = refs[inner + 1 + outer :]
    rows, width = stacked_ref.shape
    rows_dev = rows // outer
    k_dev = code[0].shape[0]
    lanes = math.gcd(k_dev, 128)
    place = place_ref[0] // inner
    norms = [
        jnp.broadcast_to(norm_column(code[k][...], scale), (k_dev, lanes)).T[:1, :]
        for k in range(inner)
    ]

    def first_half(start, slot):
        rows_here = stacked_ref[pl.ds(start, tile), :]
        top = None
        for k in range(inner):
            s = scale * nt_dot(rows_here, code[k][...]) - norms[k]
            scores[slot : slot + tile, k * k_dev : (k + 1) * k_dev] = s
            m = fold_lanes(jnp.maximum, s, lanes)
            top = m if top is None else jnp.maximum(top, m)
        return jnp.max(top, axis=1, keepdims=True)

    def second_half(start, slot, top):
        mass = jnp.zeros((tile, lanes), jnp.float32)
        acc = jnp.zeros((tile, width), jnp.float32)
        for k in range(inner):
            p = jnp.exp2(scores[slot : slot + tile, k * k_dev : (k + 1) * k_dev] - top)
            mass = mass + fold_lanes(jnp.add, p, lanes)
            acc = acc + jnp.dot(
                p.astype(jnp.bfloat16), code[k][...], preferred_element_type=jnp.float32
            )
        mass = jnp.sum(mass, axis=1, keepdims=True)
        lam = jnp.broadcast_to(LN2 * (top + jnp.log2(mass)), (tile, lanes)).T[:1, :]
        lam_ref[:, :, pl.ds(start, tile)] = jnp.broadcast_to(
            lam.reshape(1, 1, tile), (lam_ref.shape[0], 1, tile)
        )
        total[pl.ds(start, tile), :] = (acc * (1.0 / mass)).astype(jnp.bfloat16)

    count = rows // tile
    if count <= 4:
        tops = [first_half(t * tile, t * tile) for t in range(count)]
        for t in range(count):
            second_half(t * tile, t * tile, tops[t])
    else:

        @pl.loop(0, count)
        def one_tile(t):
            start = pl.multiple_of(t * tile, tile)
            second_half(start, 0, first_half(start, 0))

    for j in range(outer):
        spot = pl.multiple_of((place ^ j) * rows_dev, rows_dev)
        parts[j][...] = total[pl.ds(spot, rows_dev), :]


def rows_calc(place, stacked, code, outer):
    inner = len(code)
    rows, width = stacked.shape
    rows_dev = rows // outer
    entries = inner * code[0].shape[0]
    tile = math.gcd(rows, 256)
    vmem = pl.BlockSpec(memory_space=pltpu.VMEM)
    out = pl.pallas_call(
        functools.partial(rows_kernel, outer, inner, tile, LOG2E * 3.0 / math.sqrt(width)),
        out_shape=[jax.ShapeDtypeStruct((outer * inner, 1, rows), jnp.float32)]
        + [jax.ShapeDtypeStruct((rows_dev, width), jnp.bfloat16)] * outer,
        in_specs=[pl.BlockSpec(memory_space=pltpu.SMEM)] + [vmem] * (1 + inner),
        out_specs=[vmem] * (outer + 1),
        scratch_shapes=[
            pltpu.VMEM((min(rows, 4 * tile), entries), jnp.float32),
            pltpu.VMEM((rows, width), jnp.bfloat16),
        ],
        compiler_params=pltpu.CompilerParams(vmem_limit_bytes=VMEM_LIMIT),
        cost_estimate=pl.CostEstimate(
            flops=4 * rows * entries * width,
            bytes_accessed=2 * (rows + entries) * width,
            transcendentals=rows * entries,
        ),
        name="rows_calc",
    )(place, stacked, *code)
    return out[0], out[1:]


def norm_kernel(scale, code_ref, out_ref):
    out_ref[...] = jnp.broadcast_to(norm_column(code_ref[...], scale), out_ref.shape)


def norm_calc(code, scale):
    k_dev, width = code.shape
    lanes = math.gcd(width, 128)
    vmem = pl.BlockSpec(memory_space=pltpu.VMEM)
    return pl.pallas_call(
        functools.partial(norm_kernel, scale),
        out_shape=jax.ShapeDtypeStruct((k_dev, lanes), jnp.float32),
        in_specs=[vmem],
        out_specs=vmem,
        compiler_params=pltpu.CompilerParams(vmem_limit_bytes=VMEM_LIMIT),
        cost_estimate=pl.CostEstimate(
            flops=2 * k_dev * width, bytes_accessed=2 * k_dev * width, transcendentals=0
        ),
        name="norm_calc",
    )(code)


def read_lse(lam_ref, outer, inner, spoke):
    each = [lam_ref[z * inner + spoke] for z in range(outer)]
    top = functools.reduce(jnp.maximum, each)
    return top + jnp.log(sum(jnp.exp(x - top) for x in each))


def add_groups(
    groups, tile, scale, levels, code_ref, norm_ref, emb, weighted, folded, before=None
):
    lanes = folded.shape[1]
    code = code_ref[...]
    norm = jnp.concatenate([norm_ref[...]] * (tile // lanes), axis=1)
    for g, emb_ref in zip(groups, emb):
        level = LOG2E * levels(g)
        for start in range(0, emb_ref.shape[0], tile):
            rows_here = emb_ref[start : start + tile, :]
            s = scale * nt_dot(code, rows_here) - norm
            shares = jnp.exp2(s - level[:, start : start + tile]).astype(jnp.bfloat16)
            wide = shares.astype(jnp.float32)
            part = fold_lanes(jnp.add, wide, lanes)
            product = jnp.dot(shares, rows_here, preferred_element_type=jnp.float32)
            if before is not None:
                product, part = product + before[0][...], part + before[1][...]
            weighted[...], folded[...] = product, part
            before = weighted, folded


def early_kernel(outer, inner, groups, tile, scale, order, place_ref, lam_ref, code_ref, norm_ref, *refs):
    emb = refs[: len(groups)]
    weighted, folded = refs[len(groups) :]
    spoke = place_ref[0] % inner
    levels = lambda g: read_lse(lam_ref, outer, inner, spoke ^ g)
    add_groups(groups, tile, scale, levels, code_ref, norm_ref, emb, weighted, folded)


def late_kernel(outer, inner, groups, tile, scale, order, place_ref, lam_ref, code_ref, norm_ref, *refs):
    emb, refs = refs[: len(groups)], refs[len(groups) :]
    weighted_in, folded_in, shift_ref, occ_ref, weight_ref, own_ref, weighted, folded = refs
    k_dev = code_ref.shape[0]
    rows = lam_ref.shape[2]
    rows_dev = rows // outer
    place, spoke = place_ref[0] // inner, place_ref[0] % inner
    levels = lambda g: read_lse(lam_ref, outer, inner, spoke ^ g)
    before = weighted_in, folded_in
    add_groups(groups, tile, scale, levels, code_ref, norm_ref, emb, weighted, folded, before)
    masses = jnp.sum(folded[...], axis=1, keepdims=True)
    share = 1.0 / (masses + rows_dev / k_dev)
    shift_ref[...] = (
        (weighted[...] - masses * code_ref[...].astype(jnp.float32)) * share
    ).astype(jnp.bfloat16)
    spread = jnp.broadcast_to(masses * (k_dev / rows_dev), folded.shape).T
    occ_ref[...] = spread[:1, :]

    mine = levels(0)
    lines = [jnp.exp(lam_ref[(place ^ j) * inner + spoke] - mine) for j in order] + [mine]
    lines += [mine] * (-len(lines) % 8)
    near = pltpu.roll(jnp.concatenate(lines, axis=0), (outer - place) % outer * rows_dev, 1)
    near = near[:, : min(rows, -(-rows_dev // 128) * 128)]
    weight_ref[...] = near.T[:rows_dev, :]
    own_ref[...] = near[outer : outer + 1, :rows_dev]


def soft_kernel(weight_ref, *refs):
    parts, soft_ref = refs[:-1], refs[-1]
    total = jnp.zeros(soft_ref.shape, jnp.float32)
    for i, part in enumerate(parts):
        total = total + weight_ref[:, i : i + 1] * part[...].astype(jnp.float32)
    soft_ref[...] = total.astype(jnp.bfloat16)


def soft_calc(weights, parts):
    vmem = pl.BlockSpec(memory_space=pltpu.VMEM)
    shape = parts[0].shape
    return pl.pallas_call(
        soft_kernel,
        out_shape=jax.ShapeDtypeStruct(shape, jnp.bfloat16),
        in_specs=[vmem] * (1 + len(parts)),
        out_specs=vmem,
        compiler_params=pltpu.CompilerParams(vmem_limit_bytes=VMEM_LIMIT),
        cost_estimate=pl.CostEstimate(
            flops=2 * len(parts) * shape[0] * shape[1],
            bytes_accessed=2 * (1 + len(parts)) * shape[0] * shape[1],
            transcendentals=0,
        ),
        name="soft_calc",
    )(weights, *parts)


def columns_calc(place, lam, code, norm, groups, emb, inner, sums=(), order=()):
    k_dev, width = code.shape
    rows = emb[0].shape[0]
    outer = lam.shape[0] // inner
    tile = math.gcd(rows, 768)
    lanes = norm.shape[1]
    totals = [((k_dev, width), jnp.float32), ((k_dev, lanes), jnp.float32)]
    if sums:
        body = late_kernel
        rows_dev = rows // outer
        out = [
            ((k_dev, width), jnp.bfloat16),
            ((1, k_dev), jnp.float32),
            ((rows_dev, -(-(outer + 1) // 8) * 8), jnp.float32),
            ((1, rows_dev), jnp.float32),
        ]
        scratch = [pltpu.VMEM(*x) for x in totals]
    else:
        body, out, scratch = early_kernel, totals, []
    vmem = pl.BlockSpec(memory_space=pltpu.VMEM)
    return pl.pallas_call(
        functools.partial(
            body, outer, inner, groups, tile, LOG2E * 3.0 / math.sqrt(width), order
        ),
        out_shape=[jax.ShapeDtypeStruct(*x) for x in out],
        in_specs=[pl.BlockSpec(memory_space=pltpu.SMEM)]
        + [vmem] * (3 + len(emb) + len(sums)),
        out_specs=[vmem] * len(out),
        scratch_shapes=scratch,
        compiler_params=pltpu.CompilerParams(vmem_limit_bytes=VMEM_LIMIT),
        cost_estimate=pl.CostEstimate(
            flops=(4 if sums else EARLY) * len(emb) * rows * k_dev * width,
            bytes_accessed=2 * (len(emb) * rows + 2 * k_dev) * width,
            transcendentals=len(emb) * rows * k_dev,
        ),
        name="columns_calc",
    )(place, lam, code, norm, *emb, *sums)


def after(x, y):
    return lax.optimization_barrier((x, y))[0]


def on_device(size, embeddings, codebook):
    inner = 4
    outer = size // inner
    place = lax.axis_index(AXIS).astype(jnp.int32).reshape(1)

    def swap(x, step):
        return lax.ppermute(x, AXIS, [(i, i ^ step) for i in range(size)])

    code_y = swap(codebook, 2)
    code_c = swap(codebook, 1)
    shape = (outer * embeddings.shape[0], embeddings.shape[1])
    order = (outer // 2, *(j for j in range(1, outer) if j != outer // 2), 0)
    own_rows, own_code = keep(embeddings, codebook)
    first = (*range(2, outer), 1, 0)
    blocks = [swap(embeddings, inner * j) for j in first[:-1]] + [own_rows]
    stacked = stack(place, blocks, first, inner, shape)
    stacked_y = swap(stacked, 2)
    stacked_c = swap(stacked, 1)
    code = [own_code, code_c, code_y, swap(code_y, 1)]
    lam, parts = rows_calc(place, stacked, code, outer)

    sent = [swap(parts[j], inner * j) for j in order[:-1]]
    lam = lax.all_to_all(lam, AXIS, 0, 0)
    lam = after(lam, sent[0])
    norm = norm_calc(own_code, LOG2E * 3.0 / math.sqrt(codebook.shape[1]))
    stacked_yc = swap(stacked_y, 1)
    sums = columns_calc(
        place, lam, own_code, norm, (0, 1, 2), [stacked, stacked_c, stacked_y], inner
    )
    shift, occupancy, weights, own_lse = columns_calc(
        place, lam, own_code, norm, (3,), [stacked_yc], inner, sums, order
    )
    soft = soft_calc(weights, [*sent, parts[0]])
    return shift, occupancy.reshape(-1), soft, own_lse.reshape(-1)


def solution(mesh):
    specs = P(("groups", AXIS), None)
    flat = P(("groups", AXIS))
    return jax.shard_map(
        functools.partial(on_device, mesh.shape[AXIS]),
        mesh=mesh,
        in_specs=(specs, specs),
        out_specs=(specs, flat, specs, flat),
        check_vma=False,
    )
```
